32 devices in a mesh: replica: 8 (over y, x, core), shard: 4 (over z).
Axes of the slice: x: 2, y: 2, z: 4, core: 2. Of those that a mesh axis runs over, the one named last changes fastest.
Arguments:
- tokens: float32 [8192, 768], P(('replica', 'shard')), may hold values from -6 to 6
- memory_rows: float32 [8, 20, 768], P('replica'), may hold values from -6 to 6
- doc_lengths: int32 [8, 16], P('replica'), may hold values from 1 to 512, 1024 in all within a row
- w_query: bfloat16 [768, 768], P('shard'), may hold values from -0.3125 to 0.3125
- w_key: bfloat16 [768, 768], P('shard'), may hold values from -0.3125 to 0.3125
- w_value: bfloat16 [768, 768], P('shard'), may hold values from -0.21875 to 0.21875
- w_attn_out: bfloat16 [768, 768], P('shard'), may hold values from -0.625 to 0.625
- w_hidden: bfloat16 [768, 3072], P('shard'), may hold values from -0.21875 to 0.21875
- w_output: bfloat16 [3072, 768], P('shard'), may hold values from -0.109375 to 0.109375
- b_query: bfloat16 [768], P('shard'), may hold values from -1.75 to 1.75
- b_value: bfloat16 [768], P('shard'), may hold values from -1.75 to 1.75
- b_attn_out: bfloat16 [768], P('shard'), may hold values from -1.75 to 1.75
- b_hidden: bfloat16 [3072], P('shard'), may hold values from -1.75 to 1.75
- b_output: bfloat16 [768], P('shard'), may hold values from -1.75 to 1.75
- gain_attn: bfloat16 [768], P('shard'), may hold values from 0.5 to 1.5
- shift_attn: bfloat16 [768], P('shard'), may hold values from -1.75 to 1.75
- gain_ffn: bfloat16 [768], P('shard'), may hold values from 0.5 to 1.5
- shift_ffn: bfloat16 [768], P('shard'), may hold values from -1.75 to 1.75
- out_grad: float32 [8192, 768], P(('replica', 'shard')), may hold values from -6 to 6
- memory_grad: float32 [8, 20, 768], P('replica'), may hold values from -6 to 6
Outputs:
- result_tokens: float32 [8192, 768], P(('replica', 'shard'))
- result_memory: float32 [8, 20, 768], P('replica')
- grad_tokens: float32 [8192, 768], P(('replica', 'shard'))
- grad_memory: float32 [8, 20, 768], P('replica')
- grad_w_query: float32 [768, 768], P('shard')
- grad_w_key: float32 [768, 768], P('shard')
- grad_w_value: float32 [768, 768], P('shard')
- grad_w_attn_out: float32 [768, 768], P('shard')
- grad_w_hidden: float32 [768, 3072], P('shard')
- grad_w_output: float32 [3072, 768], P('shard')
- grad_b_query: float32 [768], P('shard')
- grad_b_value: float32 [768], P('shard')
- grad_b_attn_out: float32 [768], P('shard')
- grad_b_hidden: float32 [3072], P('shard')
- grad_b_output: float32 [768], P('shard')
- grad_gain_attn: float32 [768], P('shard')
- grad_shift_attn: float32 [768], P('shard')
- grad_gain_ffn: float32 [768], P('shard')
- grad_shift_ffn: float32 [768], P('shard')
- rms_residual: float32 [], replicated
- rms_attn_branch: float32 [], replicated
- rms_ffn_branch: float32 [], replicated
The draws below stay inside these ranges and needn't reach their ends.
Inputs may be any that keep to these rules, and one draw needn't show every extreme that they name: Each row of doc_lengths sums to 1024, and its largest entry equals 512.
All inputs are finite; a program needn't handle non-finite values.
Results may differ from the reference program's by a relative error of at most 0.02.
Values may be sent and summed in bfloat16 or wider, within the bound.
A program may use at most 128 MiB of HBM per device.

```python
import math
import jax
import jax.numpy as jnp
import numpy as np
from jax import lax

D = 768
H = 12
HD = 64
FF = 3072
MEM = 10
NDOC = 16
SEQS = 8
SEQ_LEN = 1024
TOKENS = 8192
MAXDOC = 512


def steps_of(key, extent, pieces, low, high):
    loudness, own = 1.0, jax.random.fold_in(key, 6)
    for position, blocks in pieces:
        draws = jnp.exp(jax.random.uniform(jax.random.fold_in(own, position), (blocks,), jnp.float32, low / len(pieces), high / len(pieces)))
        loudness = loudness * jnp.repeat(draws, extent[position] // blocks).reshape([-1 if axis == position else 1 for axis in range(len(extent))])
    return loudness


def length_profile(number_of, total, limit, skew):
    loads = [(1 << 20) // math.isqrt(rank ** skew) + 1 for rank in range(2, number_of + 1)]
    rest, counts = total - limit - (number_of - 1), [1] * (number_of - 1)
    while rest > 0:
        candidates = [i for i in range(number_of - 1) if counts[i] < limit]
        mass, budget = sum([loads[i] for i in candidates]), rest
        for i in candidates:
            extra = min(limit - counts[i], max(1, budget * loads[i] // mass), rest)
            counts[i] = counts[i] + extra
            rest = rest - extra
    return np.array([limit] + counts)


def uneven_parts(key, number_of, total, bound, lean):
    if number_of == 2:
        one = jax.random.randint(key, (), max(1, total - bound), min(bound, total - 1) + 1)
        return jnp.stack([one, total - one])
    tallies = jnp.asarray(length_profile(number_of, total, bound, lean), jnp.int32)
    pairs = (number_of - 1) // 2
    donor, sink = tallies[1:1 + 2 * pairs:2], tallies[2:2 + 2 * pairs:2]
    slack = jnp.minimum(donor - 1, bound - sink)
    moved = jax.random.randint(jax.random.fold_in(key, 1), (pairs,), 0, 1 << 20) % (slack + 1)
    tallies = tallies.at[1:1 + 2 * pairs:2].set(donor - moved).at[2:2 + 2 * pairs:2].set(sink + moved)
    return tallies[jax.random.permutation(jax.random.fold_in(key, 2), number_of)]


def bell_draw(key, extent, width, reach, split=(), kind=jnp.bfloat16):
    values = width * jax.random.normal(key, extent, jnp.float32)
    if split:
        values = values * steps_of(key, extent, split, -0.22, 0.18)
    return jnp.clip(values, -reach, reach).astype(kind)


def setup_inputs(seed: int = 0) -> dict:
    key_list = jax.random.split(jax.random.key(seed), 21)
    tokens = bell_draw(key_list[0], (TOKENS, D), 1.0, 6.0, ((0, 32),), jnp.float32)
    memory_rows = bell_draw(key_list[1], (SEQS, 2 * MEM, D), 1.0, 6.0, ((0, 8),), jnp.float32)
    doc_lengths = jax.vmap(lambda own: uneven_parts(own, NDOC, SEQ_LEN, MAXDOC, 2))(jax.random.split(key_list[2], SEQS)).reshape((SEQS, NDOC)).astype(jnp.int32)
    w_query = bell_draw(key_list[3], (D, D), (D // 2) ** -0.5, 0.3125, ((0, 4),))
    w_key = bell_draw(key_list[4], (D, D), (D // 2) ** -0.5, 0.3125, ((0, 4),))
    w_value = bell_draw(key_list[5], (D, D), D ** -0.5, 0.21875, ((0, 4),))
    w_attn_out = bell_draw(key_list[6], (D, D), (D // 8) ** -0.5, 0.625, ((0, 4),))
    w_hidden = bell_draw(key_list[7], (D, FF), D ** -0.5, 0.21875, ((0, 4),))
    w_output = bell_draw(key_list[8], (FF, D), FF ** -0.5, 0.109375, ((0, 4),))
    b_query = bell_draw(key_list[9], (D,), 0.3, 1.75, ((0, 4),))
    b_value = bell_draw(key_list[10], (D,), 0.3, 1.75, ((0, 4),))
    b_attn_out = bell_draw(key_list[11], (D,), 0.3, 1.75, ((0, 4),))
    b_hidden = bell_draw(key_list[12], (FF,), 0.3, 1.75, ((0, 4),))
    b_output = bell_draw(key_list[13], (D,), 0.3, 1.75, ((0, 4),))
    gain_attn = jnp.clip(1.0 + 0.1 * jax.random.normal(key_list[14], (D,), jnp.float32), 0.5, 1.5).astype(jnp.bfloat16)
    shift_attn = bell_draw(key_list[15], (D,), 0.3, 1.75, ((0, 4),))
    gain_ffn = jnp.clip(1.0 + 0.1 * jax.random.normal(key_list[16], (D,), jnp.float32), 0.5, 1.5).astype(jnp.bfloat16)
    shift_ffn = bell_draw(key_list[17], (D,), 0.3, 1.75, ((0, 4),))
    out_grad = bell_draw(key_list[18], (TOKENS, D), 1.0, 6.0, ((0, 32),), jnp.float32)
    memory_grad = bell_draw(key_list[19], (SEQS, 2 * MEM, D), 1.0, 6.0, ((0, 8),), jnp.float32)
    return dict(tokens=tokens, memory_rows=memory_rows, doc_lengths=doc_lengths, w_query=w_query, w_key=w_key, w_value=w_value, w_attn_out=w_attn_out, w_hidden=w_hidden, w_output=w_output, b_query=b_query, b_value=b_value, b_attn_out=b_attn_out, b_hidden=b_hidden, b_output=b_output, gain_attn=gain_attn, shift_attn=shift_attn, gain_ffn=gain_ffn, shift_ffn=shift_ffn, out_grad=out_grad, memory_grad=memory_grad)


@jax.custom_vjp
def low(v):
    return lax.optimization_barrier(v.astype(jnp.bfloat16)).astype(jnp.float32)

@jax.custom_vjp
def low_back(v):
    return v

def low_keep(v):
    return (low(v), None)

def low_pass(kept, grad):
    return (grad,)

def back_keep(v):
    return (v, None)

def back_low(kept, grad):
    return (low(grad),)
low.defvjp(low_keep, low_pass)
low_back.defvjp(back_keep, back_low)
EPSILON = 1e-12
GELU_ROOT = 0.7071067811865476

def matmul(left, right):
    return jnp.dot(left, right, precision=lax.Precision.HIGHEST)

def layer_norm(totals, gain, shift):
    center = totals - lax.optimization_barrier(jnp.mean(totals, axis=-1, keepdims=True))
    spread = lax.optimization_barrier(jnp.mean(center * center, axis=-1, keepdims=True))
    return center * lax.rsqrt(spread + EPSILON) * gain + shift

def gelu_exact(inputs):
    return 0.5 * inputs * (1.0 + lax.erf(inputs * GELU_ROOT))

def attend_block(query, query_seg, keys, values, key_seg):
    raw_scores = jnp.einsum('rhd,khd->hrk', query, keys, precision=lax.Precision.HIGHEST) * (1.0 / math.sqrt(HD))
    allowed = (query_seg[:, None] == key_seg[None, :]) | (key_seg[None, :] == -1) | (query_seg[:, None] == -2)
    scores = jnp.where(allowed[None], low_back(raw_scores), -1e+30)
    top_score = lax.optimization_barrier(jnp.max(scores, axis=-1, keepdims=True))
    powers = jnp.exp(scores - top_score)
    attn_prob = powers / lax.optimization_barrier(jnp.sum(powers, axis=-1, keepdims=True))
    return jnp.einsum('hrk,khd->rhd', low(attn_prob), values, precision=lax.Precision.HIGHEST)

def sequence_attention(packed):
    query, keys, values, segment = packed
    mem_seg = jnp.where(jnp.arange(2 * MEM) < MEM, -1, -3).astype(jnp.int32)
    key_seg = jnp.concatenate([segment, mem_seg])
    block_len = min(512, SEQ_LEN)
    tok_query = query[:SEQ_LEN].reshape(SEQ_LEN // block_len, block_len, H, HD)
    tok_seg = segment.reshape(SEQ_LEN // block_len, block_len)

    def one_block(piece_pair):
        return attend_block(piece_pair[0], piece_pair[1], keys, values, key_seg)
    token_ctx = lax.map(jax.checkpoint(one_block), (tok_query, tok_seg))
    mem_query_seg = jnp.full((2 * MEM,), -2, jnp.int32)
    mem_ctx = attend_block(query[SEQ_LEN:], mem_query_seg, keys, values, key_seg)
    return jnp.concatenate([token_ctx.reshape(SEQ_LEN, H, HD), mem_ctx], axis=0)

def token_rms(flat):
    token_part = flat.reshape(SEQS, SEQ_LEN + 2 * MEM, D)[:, :SEQ_LEN]
    return jnp.sqrt(jnp.sum(token_part * token_part) / (TOKENS * D))

def forward(tokens, memory_rows, params, segments):
    w_query, w_key, w_value, w_attn_out, w_hidden, w_output, b_query, b_value, b_attn_out, b_hidden, b_output, gain_attn, shift_attn, gain_ffn, shift_ffn = params
    rows = jnp.concatenate([tokens.reshape(SEQS, SEQ_LEN, D), memory_rows], axis=1)
    flat_rows = rows.reshape(SEQS * (SEQ_LEN + 2 * MEM), D)
    low_rows = low(flat_rows)
    query = low(low_back(matmul(low_rows, w_query) + b_query))
    keys = low(low_back(matmul(low_rows, w_key)))
    values = low(low_back(matmul(low_rows, w_value) + b_value))
    shape_heads = (SEQS, SEQ_LEN + 2 * MEM, H, HD)
    context = lax.map(sequence_attention, (query.reshape(shape_heads), keys.reshape(shape_heads), values.reshape(shape_heads), segments))
    context = low(low_back(context.reshape(SEQS * (SEQ_LEN + 2 * MEM), D)))
    branch = low_back(matmul(context, w_attn_out) + b_attn_out)
    after_attn = layer_norm(flat_rows + branch, gain_attn, shift_attn)
    pre_act = low_back(matmul(low(after_attn), w_hidden) + b_hidden)
    act_low = low(gelu_exact(pre_act))
    second = low_back(matmul(act_low, w_output) + b_output)
    flat_result = layer_norm(after_attn + second, gain_ffn, shift_ffn)
    result = flat_result.reshape(SEQS, SEQ_LEN + 2 * MEM, D)
    extras = (token_rms(flat_result), token_rms(branch), token_rms(second))
    return ((result[:, :SEQ_LEN].reshape(TOKENS, D), result[:, SEQ_LEN:]), extras)

def reference(tokens, memory_rows, doc_lengths, w_query, w_key, w_value, w_attn_out, w_hidden, w_output, b_query, b_value, b_attn_out, b_hidden, b_output, gain_attn, shift_attn, gain_ffn, shift_ffn, out_grad, memory_grad):
    doc_ends = jnp.cumsum(doc_lengths, axis=1).astype(jnp.int32)
    positions = jnp.arange(SEQ_LEN, dtype=jnp.int32)
    segments = lax.optimization_barrier(jnp.sum((positions[None, :, None] >= doc_ends[:, None, :]).astype(jnp.int32), axis=2)).astype(jnp.int32)
    params = tuple((weight.astype(jnp.float32) for weight in (w_query, w_key, w_value, w_attn_out, w_hidden, w_output, b_query, b_value, b_attn_out, b_hidden, b_output, gain_attn, shift_attn, gain_ffn, shift_ffn)))

    def run_layer(inputs, memory, weights):
        return forward(inputs, memory, weights, segments)
    (result_tokens, result_memory), pullback, extras = jax.vjp(run_layer, tokens, memory_rows, params, has_aux=True)
    all_grads = pullback((out_grad, memory_grad))
    param_grads = all_grads[2]
    return (result_tokens, result_memory, all_grads[0], all_grads[1], param_grads[0], param_grads[1], param_grads[2], param_grads[3], param_grads[4], param_grads[5], param_grads[6], param_grads[7], param_grads[8], param_grads[9], param_grads[10], param_grads[11], param_grads[12], param_grads[13], param_grads[14], extras[0], extras[1], extras[2])
```

```python
import functools
import math

import jax
import jax.numpy as jnp
from jax import lax
from jax.experimental import pallas as pl
from jax.experimental.pallas import tpu as pltpu
from jax.sharding import PartitionSpec as P

H = 12
HD = 64
EPSILON = 1e-12
GELU_ROOT = 0.7071067811865476
GELU_DENSITY = 0.3989422804014327
MESH = pl.DeviceIdType.MESH
BF = jnp.bfloat16
F32 = jnp.float32
MEM_PAD = 32
MEM_KEYS = 128
VMEM_LIMIT = 60 << 20
NEG = -1e30


def region(ref, group, sh, q0, nq, h0, nh):
    hs = h0 if nh == 1 else pl.ds(h0, nh)
    qs = q0 if nq == 1 else pl.ds(q0, nq)
    if group == 2:
        return ref.at[sh, qs, hs]
    return ref.at[qs, sh, hs]


def neighbours():
    r = lax.axis_index("replica")
    s = lax.axis_index("shard")
    core, xbit, ybit = r % 2, (r // 2) % 2, (r // 4) % 2
    return r, s, core, xbit, ybit, r + 1 - 2 * core, r + 2 - 4 * xbit, r + 4 - 8 * ybit


def entry_barrier(peers, r, s, shards):
    sem = pltpu.get_barrier_semaphore()
    for p in peers:
        pl.semaphore_signal(sem, 1, device_id=(p, s), device_id_type=MESH)
    for t in range(1, shards):
        pl.semaphore_signal(sem, 1, device_id=(r, lax.rem(s + t, shards)), device_id_type=MESH)
    pl.semaphore_wait(sem, len(peers) + shards - 1)


def remote(src, dst, ssem, rsem, dev):
    return pltpu.make_async_remote_copy(
        src_ref=src, dst_ref=dst, send_sem=ssem, recv_sem=rsem, device_id=dev, device_id_type=MESH
    )


def gather_kernel(shards, half, width, qkvo, hid, outw, xtok, vec, o_qkvo, o_hid, o_out, o_x, o_vec,
                  zs, zr, as_, ar, bs, br, cs, cr, xs, xr, vs, vr, ls):
    r, s, core, xbit, ybit, fc, fx, fy = neighbours()
    q_own, q_lo = 2 * core + ybit, 2 * core
    outs = (o_qkvo, o_hid, o_out)
    entry_barrier((fc, fx, fy), r, s, shards)

    def piece(g, q, h):
        if g == 1:
            return hid.at[h, :, pl.ds(pl.multiple_of(q * width, width), width)]
        return (qkvo, None, outw)[g].at[q, h]

    def reg(g, sh, q0, nq, h0, nh):
        return region(outs[g], g, sh, q0, nq, h0, nh)

    def rows_copy(sh, k):
        block = o_x.at[sh]
        return remote(block, block, xs.at[k, sh], xr.at[sh], (r, s + 1 if k == 0 else s - 1))

    def on_line(k, fn):
        pl.when(s + 1 < shards if k == 0 else s > 0)(fn)

    sends = []
    for g in range(3):
        for t in range(1, shards):
            dst = lax.rem(s + t, shards)
            sends.append(
                remote(piece(g, q_own, xbit), reg(g, s, q_own, 1, xbit, 1), zs.at[g, t], zr.at[g, s], (r, dst))
            )
            sends[-1].start()
        if g == 0:
            for t in range(1, shards):
                sends.append(remote(vec, o_vec.at[s], vs.at[t], vr.at[s], (r, lax.rem(s + t, shards))))
                sends[-1].start()
            for k in range(2):
                on_line(
                    k,
                    lambda k=k: remote(
                        xtok, o_x.at[s], xs.at[k, s], xr.at[s], (r, s + 1 if k == 0 else s - 1)
                    ).start(),
                )

    local = [(xtok, o_x.at[s]), (vec, o_vec.at[s]), (qkvo, o_qkvo.at[:, s]), (outw, o_out.at[s])]
    for q in range(4):
        local.append((hid.at[:, :, pl.ds(q * width, width)], o_hid.at[q, s]))
    local = [pltpu.make_async_copy(a, b, ls.at[i]) for i, (a, b) in enumerate(local)]
    for c in local:
        c.start()

    order = [(g, t, left) for g in range(3) for t in range(1, shards) for left in (True, False)]

    def hops(g, sh, first_x):
        if first_x:
            return ((reg(g, sh, q_own, 1, xbit, 1), fx), (reg(g, sh, q_own, 1, 0, 2), fy), (reg(g, sh, q_lo, 2, 0, 2), fc))
        return ((reg(g, sh, q_own, 1, xbit, 1), fy), (reg(g, sh, q_lo, 2, xbit, 1), fx), (reg(g, sh, q_lo, 2, 0, 2), fc))

    sems = ((as_, ar), (bs, br), (cs, cr))

    def hop(g, sh, first_x, k):
        a, dev = hops(g, sh, first_x)[k]
        return remote(a, a, sems[k][0].at[g, sh], sems[k][1].at[g, sh], (dev, s))

    def at_slot(i, fn):
        g, t, left = order[i]
        sh = s - t if left else s + t
        first_x = (g + t + (1 if left else 0)) % 2 == 0
        pl.when(s >= t if left else s + t < shards)(lambda: fn(g, left, sh, first_x))

    def stage0(g, left, sh, first_x):
        if g == 0:
            rows_copy(sh, 0).wait_recv()
            k = 0 if left else 1
            on_line(k, lambda: rows_copy(sh, k).start())
        a = reg(g, sh, q_own, 1, xbit, 1)
        remote(a, a, zs.at[g, 0], zr.at[g, sh], (r, s)).wait_recv()
        hop(g, sh, first_x, 0).start()

    def stage1(g, left, sh, first_x):
        hop(g, sh, first_x, 0).wait_recv()
        hop(g, sh, first_x, 1).start()

    def stage2(g, left, sh, first_x):
        hop(g, sh, first_x, 1).wait_recv()
        hop(g, sh, first_x, 2).start()

    def finish(g, left, sh, first_x):
        for k in range(3):
            hop(g, sh, first_x, k).wait_send()
        hop(g, sh, first_x, 2).wait_recv()
        if g == 0:
            k = 0 if left else 1
            on_line(k, lambda: rows_copy(sh, k).wait_send())

    n, lag = len(order), 2
    for i in range(n + 2 * lag):
        if i < n:
            at_slot(i, stage0)
        if 0 <= i - lag < n:
            at_slot(i - lag, stage1)
        if 0 <= i - 2 * lag < n:
            at_slot(i - 2 * lag, stage2)
    for i in range(n):
        at_slot(i, finish)
    for t in range(1, shards):
        other = lax.rem(s + t, shards)
        remote(vec, o_vec.at[other], vs.at[t], vr.at[other], (r, other)).wait_recv()
    for c in sends:
        c.wait_send()
    for k in range(2):
        on_line(k, lambda k=k: rows_copy(s, k).wait_send())
    for c in local:
        c.wait()


def gather_all(qkvo, hid, outw, xtok, vec):
    shards = lax.axis_size("shard")
    half, width = qkvo.shape[1] // 2, qkvo.shape[2]
    tok = xtok.shape[0]
    any_space = pl.BlockSpec(memory_space=pl.ANY)
    dma = pltpu.SemaphoreType.DMA
    shapes = (
        jax.ShapeDtypeStruct((4, shards, 2, half, width), BF),
        jax.ShapeDtypeStruct((4, shards, 2, half, width), BF),
        jax.ShapeDtypeStruct((shards, 4, 2, half, width), BF),
        jax.ShapeDtypeStruct((shards, tok, width), BF),
        jax.ShapeDtypeStruct((shards,) + vec.shape, BF),
    )
    qkvo, hid, outw, x_all, vec_all = pl.pallas_call(
        functools.partial(gather_kernel, shards, half, width),
        out_shape=shapes,
        in_specs=[any_space] * 5,
        out_specs=[any_space] * 5,
        scratch_shapes=[dma((3, shards))] * 8 + [dma((2, shards))] + [dma((shards,))] * 3 + [dma((8,))],
        compiler_params=pltpu.CompilerParams(collective_id=1, has_side_effects=True, vmem_limit_bytes=16 << 20),
        name="gather_weights",
    )(
        qkvo.reshape(4, 2, half, width),
        hid.reshape(2, half, 4 * width),
        outw.reshape(4, 2, half, width),
        xtok,
        vec,
    )
    rows = 2 * half * shards
    return (
        qkvo.reshape(4, rows, width),
        hid.reshape(4, rows, width),
        outw.reshape(4 * rows, width),
        x_all.reshape(shards * tok, width),
        vec_all,
    )


def reduce_kernel(shards, half, width, g_qkvo, g_hid, g_out, dx, mem, vec, o_qkvo, o_hid, o_out, o_x, o_mem, o_vec,
                  own, ra, rb, rc, rd, rx, rm, rv, vz, vacc,
                  las, asem, arem, bsem, brem, csem, crem, zsem, zrem, dsem, drem, xsem, xrem, msem, mrem, vsem, vrem,
                  vzs, vzr, ls):
    r, s, core, xbit, ybit, fc, fx, fy = neighbours()
    q_own, q_lo, q_hi = 2 * core + ybit, 2 * core, 2 * (1 - core)
    grads = (g_qkvo, g_hid, g_out)
    outs = (o_qkvo, o_hid, o_out)
    entry_barrier((fc, fx, fy), r, s, shards)
    units = [(g, sh) for g in (2, 1, 0) for sh in range(shards)]
    n = len(units)

    def copy_a(u):
        g, sh = units[u]
        return remote(region(grads[g], g, sh, q_hi, 2, 0, 2), ra.at[u], asem.at[u], arem.at[u], (fc, s))

    def copy_own(u):
        g, sh = units[u]
        return pltpu.make_async_copy(region(grads[g], g, sh, q_lo, 2, 0, 2), own.at[u], las.at[u])

    def copy_b(u):
        if u % 2 == 0:
            return remote(own.at[u, :, 1 - xbit], rb.at[u], bsem.at[u], brem.at[u], (fx, s))
        return remote(own.at[u, 1 - ybit], rb.at[u], bsem.at[u], brem.at[u], (fy, s))

    def copy_c(u):
        if u % 2 == 0:
            return remote(own.at[u, 1 - ybit, xbit], rc.at[u], csem.at[u], crem.at[u], (fy, s))
        return remote(own.at[u, ybit, 1 - xbit], rc.at[u], csem.at[u], crem.at[u], (fx, s))

    def copy_z(u):
        g, sh = units[u]
        return remote(own.at[u, ybit, xbit], rd.at[g, s], zsem.at[u], zrem.at[g, s], (r, sh))

    def start_a(u):
        copy_a(u).start()
        copy_own(u).start()

    def start_b(u):
        copy_a(u).wait_recv()
        copy_own(u).wait()
        own[u] = own[u] + ra[u]
        copy_b(u).start()

    def start_c(u):
        copy_b(u).wait_recv()
        if u % 2 == 0:
            own[u, :, xbit] = own[u, :, xbit] + rb[u]
        else:
            own[u, ybit] = own[u, ybit] + rb[u]
        copy_c(u).start()

    def start_z(u):
        copy_c(u).wait_recv()
        own[u, ybit, xbit] = own[u, ybit, xbit] + rc[u]
        pl.when(s != units[u][1])(lambda: copy_z(u).start())

    def hop(g, k):
        o = outs[g]
        if g % 2 == 0:
            a, dev = ((o.at[q_own, xbit], fx), (o.at[q_own], fy), (o.at[pl.ds(q_lo, 2)], fc))[k]
        else:
            a, dev = ((o.at[q_own, xbit], fy), (o.at[pl.ds(q_lo, 2), xbit], fx), (o.at[pl.ds(q_lo, 2)], fc))[k]
        return remote(a, a, dsem.at[g, k], drem.at[g, k], (dev, s))

    def finish_group(g):
        total = own[units.index((g, 0)) + s, ybit, xbit].astype(F32)
        for t in range(1, shards):
            other = lax.rem(s + t, shards)
            slot = rd.at[g, other]
            remote(slot, slot, zsem.at[0], zrem.at[g, other], (r, s)).wait_recv()
            total = total + rd[g, other].astype(F32)
        outs[g][q_own, xbit] = total.astype(BF)
        hop(g, 0).start()

    def vec_hop(k):
        return remote(vacc.at[k], rv.at[k], vsem.at[k], vrem.at[k], ((fc, fx, fy)[k], s))

    def to_shard(src, dst, ssem, rsem, t):
        return remote(src, dst.at[s], ssem.at[t], rsem.at[s], (r, lax.rem(s + t, shards)))

    start_a(0)
    start_a(1)
    vacc[0] = vec[...]
    vec_hop(0).start()
    small = []
    for t in range(1, shards):
        small.append(to_shard(dx.at[lax.rem(s + t, shards)], rx, xsem, xrem, t))
        small.append(to_shard(mem, rm, msem, mrem, t))
    for c in small:
        c.start()
    keep = [pltpu.make_async_copy(mem, rm.at[s], ls.at[0]), pltpu.make_async_copy(dx.at[s], rx.at[s], ls.at[1])]
    for c in keep:
        c.start()

    events = {}
    last = n + 2
    for k, g in enumerate((2, 1, 0)):
        at = shards * (k + 1) + 2
        for j, fn in enumerate((
            functools.partial(finish_group, g),
            lambda g=g: (hop(g, 0).wait_recv(), hop(g, 1).start()),
            lambda g=g: (hop(g, 1).wait_recv(), hop(g, 2).start()),
        )):
            events.setdefault(at + j, []).append(fn)
            last = max(last, at + j)
    for i in range(last + 1):
        if i + 2 < n:
            start_a(i + 2)
        if i < n:
            start_b(i)
        if 0 <= i - 1 < n:
            start_c(i - 1)
        if 0 <= i - 2 < n:
            start_z(i - 2)
        if i in (1, 2):
            vec_hop(i - 1).wait_recv()
            vacc[i] = vacc[i - 1] + rv[i - 1]
            vec_hop(i).start()
        if i == 3:
            vec_hop(2).wait_recv()
            vz[s] = vacc[2] + rv[2]
            for t in range(1, shards):
                small.append(to_shard(vz.at[s], vz, vzs, vzr, t))
                small[-1].start()
        for fn in events.get(i, ()):
            fn()
    for c in keep:
        c.wait()
    for t in range(1, shards):
        other = lax.rem(s + t, shards)
        for buf, rsem in ((rx, xrem), (rm, mrem), (vz, vzr)):
            remote(buf.at[other], buf.at[other], xsem.at[0], rsem.at[other], (r, s)).wait_recv()
    for buf, out in ((rx, o_x), (rm, o_mem), (vz, o_vec)):
        total = buf[0].astype(F32)
        for t in range(1, shards):
            total = total + buf[t].astype(F32)
        out[...] = total
    for g in range(3):
        hop(g, 2).wait_recv()
    for u in range(n):
        copy_a(u).wait_send()
        copy_b(u).wait_send()
        copy_c(u).wait_send()
        pl.when(s != units[u][1])(lambda u=u: copy_z(u).wait_send())
    for g in range(3):
        for k in range(3):
            hop(g, k).wait_send()
    for c in small:
        c.wait_send()
    for k in range(3):
        vec_hop(k).wait_send()


def reduce_all(g_qkvo, g_hid, g_out, dx, mem, vec):
    shards = lax.axis_size("shard")
    width = g_qkvo.shape[2]
    half = g_qkvo.shape[1] // shards // 2
    tok = dx.shape[0] // shards
    any_space = pl.BlockSpec(memory_space=pl.ANY)
    vm = pl.BlockSpec(memory_space=pltpu.VMEM)
    dma = pltpu.SemaphoreType.DMA
    n = 3 * shards
    shapes = tuple(jax.ShapeDtypeStruct((4, 2, half, width), BF) for g in range(3)) + (
        jax.ShapeDtypeStruct((tok, width), F32),
        jax.ShapeDtypeStruct(mem.shape, F32),
        jax.ShapeDtypeStruct(vec.shape, F32),
    )
    o_qkvo, o_hid, o_out, o_x, o_mem, o_vec = pl.pallas_call(
        functools.partial(reduce_kernel, shards, half, width),
        out_shape=shapes,
        in_specs=[any_space] * 4 + [vm] * 2,
        out_specs=[vm] * 6,
        scratch_shapes=[
            pltpu.VMEM((n, 2, 2, half, width), BF),
            pltpu.VMEM((n, 2, 2, half, width), BF),
            pltpu.VMEM((n, 2, half, width), BF),
            pltpu.VMEM((n, half, width), BF),
            pltpu.VMEM((3, shards, half, width), BF),
            pltpu.VMEM((shards, tok, width), BF),
            pltpu.VMEM((shards,) + mem.shape, F32),
            pltpu.VMEM((3,) + vec.shape, F32),
            pltpu.VMEM((shards,) + vec.shape, F32),
            pltpu.VMEM((3,) + vec.shape, F32),
        ]
        + [dma((n,))] * 8
        + [dma((3, shards)), dma((3, 3)), dma((3, 3))]
        + [dma((shards,))] * 4
        + [dma((3,)), dma((3,)), dma((shards,)), dma((shards,)), dma((2,))],
        compiler_params=pltpu.CompilerParams(collective_id=2, has_side_effects=True, vmem_limit_bytes=VMEM_LIMIT),
        name="reduce_grads",
    )(
        g_qkvo.reshape(4, shards, 2, half, width),
        g_hid.reshape(4, shards, 2, half, width),
        g_out.reshape(shards, 4, 2, half, width),
        dx.reshape(shards, tok, width),
        mem,
        vec,
    )
    srows = 2 * half
    return (
        o_qkvo.reshape(4, srows, width),
        o_hid.reshape(4, srows, width),
        o_out.reshape(4 * srows, width),
        o_x,
        o_mem,
        o_vec,
    )


def gather_plain(qkvo, hid, outw, xtok, vec):
    width = qkvo.shape[2]
    full = functools.partial(lax.all_gather, axis_name="shard", tiled=True)
    hid = full(hid, axis=0)
    return (
        full(qkvo, axis=1),
        jnp.stack([hid[:, q * width : (q + 1) * width] for q in range(4)]),
        full(outw, axis=0),
        full(xtok, axis=0),
        lax.all_gather(vec, "shard", axis=0),
    )


def reduce_plain(g_qkvo, g_hid, g_out, dx, mem, vec):
    scatter = functools.partial(lax.psum_scatter, axis_name="shard", tiled=True)
    return (
        lax.psum(scatter(g_qkvo, scatter_dimension=1), "replica"),
        lax.psum(scatter(g_hid, scatter_dimension=1), "replica"),
        lax.psum(scatter(g_out, scatter_dimension=0), "replica"),
        scatter(dx, scatter_dimension=0).astype(F32),
        lax.psum(mem, "shard"),
        lax.psum(vec, ("replica", "shard")),
    )


NT = (((1,), (1,)), ((), ()))
NN = (((1,), (0,)), ((), ()))
TN = (((0,), (0,)), ((), ()))


def dot(a, b, dims=NN):
    return lax.dot_general(a, b, dims, preferred_element_type=F32)


def head_lanes(shape, head):
    lane = lax.broadcasted_iota(jnp.int32, shape, 1)
    return (lane < HD) if head == 0 else (lane >= HD)


def mask_bias(qseg, kseg):
    allowed = (qseg == kseg) | (kseg == -1) | ((qseg == -2) & (kseg != -4))
    return jnp.where(allowed, 0.0, NEG)


def attend_kernel(scaling, q_ref, k_ref, v_ref, qseg_ref, kseg_ref, ctx_ref, lse_ref, bias_ref):
    @pl.when(pl.program_id(0) == 0)
    def _():
        bias_ref[...] = mask_bias(qseg_ref[...], kseg_ref[...])

    q, k, v = q_ref[...], k_ref[...], v_ref[...]
    zero_q = jnp.zeros_like(q)
    contexts, totals = [], []
    for head in range(2):
        qh = jnp.where(head_lanes(q.shape, head), q, zero_q)
        scores = dot(qh, k, NT) * scaling + bias_ref[...]
        top = jnp.max(scores, axis=1, keepdims=True)
        powers = jnp.exp(scores - top)
        lse = top + jnp.log(jnp.sum(powers, axis=1, keepdims=True))
        probs = powers * jnp.exp(top - lse)
        contexts.append(dot(probs.astype(BF), v))
        totals.append(lse)
    first = head_lanes(q.shape, 0)
    ctx_ref[...] = jnp.where(first, contexts[0], contexts[1])
    lse_ref[...] = jnp.where(first, totals[0], totals[1])


def attend_back_kernel(scaling, q_ref, k_ref, v_ref, qseg_ref, kseg_ref, weight_ref, ctx_ref, lse_ref, do_ref,
                       dq_ref, dk_ref, dv_ref, bias_ref):
    @pl.when(pl.program_id(0) == 0)
    def _():
        bias_ref[...] = mask_bias(qseg_ref[...], kseg_ref[...])

    q, k, v, do = q_ref[...], k_ref[...], v_ref[...], do_ref[...]
    weight = weight_ref[...] > 0
    dq, dk, dv = None, None, None
    for head in range(2):
        lanes = head_lanes(q.shape, head)
        qh = jnp.where(lanes, q, jnp.zeros_like(q))
        doh = jnp.where(lanes, do, jnp.zeros_like(do))
        lse = lse_ref[:, head * HD : head * HD + 1]
        scores = dot(qh, k, NT) * scaling + bias_ref[...]
        probs = jnp.exp(scores - lse)
        delta = jnp.sum(doh.astype(F32) * ctx_ref[...], axis=1, keepdims=True)
        d_scores = (probs * (dot(doh, v, NT) - delta)).astype(BF)
        kh = jnp.where(head_lanes(k.shape, head), k, jnp.zeros_like(k))
        part_q = dot(d_scores, kh)
        part_k = dot(jnp.where(weight, qh, jnp.zeros_like(qh)), d_scores, TN)
        part_v = dot(jnp.where(weight, doh, jnp.zeros_like(doh)), probs.astype(BF), TN)
        dq = part_q if dq is None else dq + part_q
        dk = part_k if dk is None else dk + part_k
        dv = part_v if dv is None else dv + part_v
    dq_ref[...] = (dq * scaling).astype(BF)
    dk_ref[...] = (dk * scaling).astype(BF)
    dv_ref[...] = dv.astype(BF)


def attention(query, keys, values, qseg, kseg, scaling):
    m, width = query.shape
    n = keys.shape[0]
    rows = pl.BlockSpec((m, 2 * HD), lambda i: (0, i))
    cols = pl.BlockSpec((n, 2 * HD), lambda i: (0, i))
    return pl.pallas_call(
        functools.partial(attend_kernel, scaling),
        grid=(width // (2 * HD),),
        out_shape=(jax.ShapeDtypeStruct((m, width), F32), jax.ShapeDtypeStruct((m, width), F32)),
        in_specs=[rows, cols, cols, pl.BlockSpec((m, 1), lambda i: (0, 0)), pl.BlockSpec((1, n), lambda i: (0, 0))],
        out_specs=[rows, rows],
        scratch_shapes=[pltpu.VMEM((m, n), F32)],
        compiler_params=pltpu.CompilerParams(vmem_limit_bytes=VMEM_LIMIT),
        name="attend",
    )(query, keys, values, qseg, kseg)


def attention_back(query, keys, values, qseg, kseg, weight, context, lse, d_context, scaling):
    m, width = query.shape
    n = keys.shape[0]
    rows = pl.BlockSpec((m, 2 * HD), lambda i: (0, i))
    cols = pl.BlockSpec((n, 2 * HD), lambda i: (0, i))
    turned = pl.BlockSpec((2 * HD, n), lambda i: (i, 0))
    column = pl.BlockSpec((m, 1), lambda i: (0, 0))
    return pl.pallas_call(
        functools.partial(attend_back_kernel, scaling),
        grid=(width // (2 * HD),),
        out_shape=(
            jax.ShapeDtypeStruct((m, width), BF),
            jax.ShapeDtypeStruct((width, n), BF),
            jax.ShapeDtypeStruct((width, n), BF),
        ),
        in_specs=[rows, cols, cols, column, pl.BlockSpec((1, n), lambda i: (0, 0)), column, rows, rows, rows],
        out_specs=[rows, turned, turned],
        scratch_shapes=[pltpu.VMEM((m, n), F32)],
        compiler_params=pltpu.CompilerParams(vmem_limit_bytes=VMEM_LIMIT),
        name="attend_back",
    )(query, keys, values, qseg, kseg, weight, context, lse, d_context)


def layer_stats(totals):
    center = totals - jnp.mean(totals, axis=-1, keepdims=True)
    spread = jnp.mean(center * center, axis=-1, keepdims=True)
    inverse = lax.rsqrt(spread + EPSILON)
    return (center * inverse, inverse)


def norm_back(grad_normed, normed, inverse):
    return inverse * (
        grad_normed
        - jnp.mean(grad_normed, axis=-1, keepdims=True)
        - normed * jnp.mean(grad_normed * normed, axis=-1, keepdims=True)
    )


def body(direct, tokens, memory_rows, doc_lengths, w_query, w_key, w_value, w_attn_out, w_hidden, w_output,
         b_query, b_value, b_attn_out, b_hidden, b_output, gain_attn, shift_attn, gain_ffn, shift_ffn,
         out_grad, memory_grad):
    tok, width = tokens.shape
    mem = memory_rows.shape[1]
    shards = lax.axis_size("shard")
    s = lax.axis_index("shard")
    seq = tok * shards
    srows = w_query.shape[0]
    m = tok + MEM_PAD
    n = seq + MEM_KEYS
    scaling = 1.0 / math.sqrt(HD)

    vec = jnp.concatenate(
        [v.reshape(-1, srows) for v in (
            b_query, b_value, b_attn_out, b_output, gain_attn, shift_attn, gain_ffn, shift_ffn, b_hidden
        )]
        + [jnp.zeros((4, srows), BF)]
    )
    vec = lax.dynamic_update_slice(jnp.zeros((16, width), BF), vec, (0, s * srows))
    rows = jnp.concatenate([tokens, memory_rows[0], jnp.zeros((MEM_PAD - mem, width), F32)])
    low_rows = rows.astype(BF)
    qkvo = jnp.stack([w_query, w_key, w_value, w_attn_out])
    gather, reduce = (gather_all, reduce_all) if direct else (gather_plain, reduce_plain)
    qkvo, w_hid, w_out, x_tok, vec_all = gather(qkvo, w_hidden, w_output, low_rows[:tok], vec)
    vec = jnp.sum(vec_all.astype(F32), axis=0)
    bq, bv, bo, bout, ga, sa, gf, sf = (vec[i] for i in range(8))
    bh = jnp.transpose(vec[8:12].reshape(4, shards, srows), (1, 0, 2)).reshape(4 * width)

    doc_ends = jnp.cumsum(doc_lengths[0])
    seg = jnp.sum((jnp.arange(seq, dtype=jnp.int32)[:, None] >= doc_ends[None, :]).astype(jnp.int32), axis=1)
    place = jnp.arange(MEM_KEYS, dtype=jnp.int32)
    mem_seg = jnp.where(place < mem // 2, -1, jnp.where(place < mem, -3, -4)).astype(jnp.int32)
    kseg = jnp.concatenate([seg, mem_seg])[None, :]
    qseg = jnp.concatenate(
        [lax.dynamic_slice_in_dim(seg, s * tok, tok), jnp.full((MEM_PAD,), -2, jnp.int32)]
    )[:, None]
    index = jnp.arange(m, dtype=jnp.int32)[:, None]
    once = jnp.where(index < tok, 1.0, jnp.where((index < tok + mem) & (s == 0), 1.0, 0.0)).astype(F32)
    once_low = once.astype(BF)

    x_all = jnp.concatenate([x_tok, low_rows[tok:], jnp.zeros((MEM_KEYS - MEM_PAD, width), BF)])
    query = (jnp.dot(low_rows, qkvo[0], preferred_element_type=F32) + bq).astype(BF)
    keys = jnp.dot(x_all, qkvo[1], preferred_element_type=F32).astype(BF)
    values = (jnp.dot(x_all, qkvo[2], preferred_element_type=F32) + bv).astype(BF)
    context, lse = attention(query, keys, values, qseg, kseg, scaling)
    context_low = context.astype(BF)
    branch = jnp.dot(context_low, qkvo[3], preferred_element_type=F32) + bo
    normed_attn, inverse_attn = layer_stats(rows + branch)
    after_attn = normed_attn * ga + sa
    after_low = after_attn.astype(BF)
    pre_act = jnp.concatenate([jnp.dot(after_low, w_hid[q], preferred_element_type=F32) for q in range(4)], axis=1) + bh
    half_erf = 0.5 * (1.0 + lax.erf(pre_act * GELU_ROOT))
    act_low = (pre_act * half_erf).astype(BF)
    second = jnp.dot(act_low, w_out, preferred_element_type=F32) + bout
    normed_ffn, inverse_ffn = layer_stats(after_attn + second)
    result = normed_ffn * gf + sf

    grads = jnp.concatenate([out_grad, memory_grad[0], jnp.zeros((MEM_PAD - mem, width), F32)])
    back_ffn = norm_back(grads * gf, normed_ffn, inverse_ffn)
    d_output = back_ffn.astype(BF)
    g_out = jnp.einsum("rf,rd->fd", act_low * once_low, d_output, preferred_element_type=F32).astype(BF)
    d_act = jnp.einsum("rd,fd->rf", d_output, w_out, preferred_element_type=F32)
    d_pre = (d_act * (half_erf + pre_act * jnp.exp(-0.5 * pre_act * pre_act) * GELU_DENSITY)).astype(BF)
    after_once = after_low * once_low
    g_hid = jnp.stack(
        [jnp.einsum("rd,rf->df", after_once, d_pre[:, q * width : (q + 1) * width], preferred_element_type=F32).astype(BF)
         for q in range(4)]
    )
    back_first = back_ffn + sum(
        jnp.einsum("rf,df->rd", d_pre[:, q * width : (q + 1) * width], w_hid[q], preferred_element_type=F32)
        for q in range(4)
    )
    back_attn = norm_back(back_first * ga, normed_attn, inverse_attn)
    d_branch = back_attn.astype(BF)
    d_context = jnp.einsum("re,de->rd", d_branch, qkvo[3], preferred_element_type=F32).astype(BF)
    dq, dkt, dvt = attention_back(query, keys, values, qseg, kseg, once, context, lse, d_context, scaling)
    g_qkvo = jnp.stack([
        jnp.einsum("rd,re->de", low_rows * once_low, dq, preferred_element_type=F32).astype(BF),
        jnp.einsum("rd,er->de", x_all, dkt, preferred_element_type=F32).astype(BF),
        jnp.einsum("rd,er->de", x_all, dvt, preferred_element_type=F32).astype(BF),
        jnp.einsum("rd,re->de", context_low * once_low, d_branch, preferred_element_type=F32).astype(BF),
    ])
    dx = jnp.einsum("er,de->rd", dkt, qkvo[1], preferred_element_type=F32) + jnp.einsum(
        "er,de->rd", dvt, qkvo[2], preferred_element_type=F32
    )
    base = back_attn + jnp.einsum("re,de->rd", dq, qkvo[0], preferred_element_type=F32)

    def over_rows(terms):
        return jnp.sum(once * terms, axis=0)

    gb_hidden = over_rows(d_pre.astype(F32)).reshape(shards, 4, srows).transpose(1, 0, 2).reshape(4, width)
    squares = jnp.stack([jnp.sum(v[:tok] * v[:tok]) for v in (result, branch, second)])
    vec_grads = jnp.concatenate([
        jnp.stack([
            over_rows(dq.astype(F32)),
            jnp.sum(dvt.astype(F32), axis=1),
            over_rows(d_branch.astype(F32)),
            over_rows(d_output.astype(F32)),
            over_rows(back_first * normed_attn),
            over_rows(back_first),
            over_rows(grads * normed_ffn),
            over_rows(grads),
        ]),
        gb_hidden,
        jnp.pad(squares[None], ((0, 3), (0, width - 3))),
    ])
    g_qkvo, g_hid, g_out, dx_own, dx_mem, vec_sum = reduce(
        g_qkvo, g_hid, g_out, dx[:seq].astype(BF), dx[seq : seq + MEM_PAD], vec_grads
    )
    own = lax.dynamic_slice(vec_sum, (0, s * srows), (12, srows))
    rms = jnp.sqrt(vec_sum[12, :3] / float(seq * width * lax.axis_size("replica")))
    g_qkvo = g_qkvo.astype(F32)
    grad_hidden = jnp.concatenate([g_hid[q] for q in range(4)], axis=1).astype(F32)
    return (
        result[:tok],
        result[tok : tok + mem][None],
        base[:tok] + dx_own,
        (base[tok : tok + mem] + dx_mem[:mem])[None],
        g_qkvo[0],
        g_qkvo[1],
        g_qkvo[2],
        g_qkvo[3],
        grad_hidden,
        g_out.astype(F32),
        own[0],
        own[1],
        own[2],
        own[8:12].reshape(-1),
        own[3],
        own[4],
        own[5],
        own[6],
        own[7],
        rms[0],
        rms[1],
        rms[2],
    )


def solution(mesh):
    direct = mesh.shape["replica"] == 8 and mesh.shape["shard"] == 4
    shard1, shard2 = P("shard"), P("shard", None)
    both, rep3 = P(("replica", "shard"), None), P("replica", None, None)
    return jax.shard_map(
        functools.partial(body, direct),
        mesh=mesh,
        in_specs=(both, rep3, P("replica", None)) + (shard2,) * 6 + (shard1,) * 9 + (both, rep3),
        out_specs=(both, rep3, both, rep3) + (shard2,) * 6 + (shard1,) * 9 + (P(), P(), P()),
        check_vma=False,
    )
```

```python
import functools
import math

import jax
import jax.numpy as jnp
from jax import lax
from jax.experimental import pallas as pl
from jax.experimental.pallas import tpu as pltpu
from jax.sharding import PartitionSpec as P

H = 12
HD = 64
EPSILON = 1e-12
GELU_ROOT = 0.7071067811865476
GELU_DENSITY = 0.3989422804014327
MESH = pl.DeviceIdType.MESH
BF = jnp.bfloat16
F32 = jnp.float32
MEM_PAD = 32
MEM_KEYS = 128
VMEM_LIMIT = 60 << 20
NEG = -1e30


def region(ref, group, sh, q0, nq, h0, nh):
    hs = h0 if nh == 1 else pl.ds(h0, nh)
    qs = q0 if nq == 1 else pl.ds(q0, nq)
    if group == 2:
        return ref.at[sh, qs, hs]
    return ref.at[qs, sh, hs]


def neighbours():
    r = lax.axis_index("replica")
    s = lax.axis_index("shard")
    core, xbit, ybit = r % 2, (r // 2) % 2, (r // 4) % 2
    return r, s, core, xbit, ybit, r + 1 - 2 * core, r + 2 - 4 * xbit, r + 4 - 8 * ybit


def entry_barrier(peers, r, s, shards):
    sem = pltpu.get_barrier_semaphore()
    for p in peers:
        pl.semaphore_signal(sem, 1, device_id=(p, s), device_id_type=MESH)
    for t in range(1, shards):
        pl.semaphore_signal(sem, 1, device_id=(r, lax.rem(s + t, shards)), device_id_type=MESH)
    pl.semaphore_wait(sem, len(peers) + shards - 1)


def remote(src, dst, ssem, rsem, dev):
    return pltpu.make_async_remote_copy(
        src_ref=src, dst_ref=dst, send_sem=ssem, recv_sem=rsem, device_id=dev, device_id_type=MESH
    )


def gather_plain(qkvo, hid, outw, xtok, vec):
    width = qkvo.shape[2]
    full = functools.partial(lax.all_gather, axis_name="shard", tiled=True)
    hid = full(hid, axis=0)
    return (
        full(qkvo, axis=1),
        jnp.stack([hid[:, q * width : (q + 1) * width] for q in range(4)]),
        full(outw, axis=0),
        full(xtok, axis=0),
        lax.all_gather(vec, "shard", axis=0),
    )


def reduce_plain(g_qkvo, g_hid, g_out, dx, mem, vec):
    scatter = functools.partial(lax.psum_scatter, axis_name="shard", tiled=True)
    return (
        lax.psum(scatter(g_qkvo, scatter_dimension=1), "replica"),
        lax.psum(scatter(g_hid, scatter_dimension=1), "replica"),
        lax.psum(scatter(g_out, scatter_dimension=0), "replica"),
        scatter(dx, scatter_dimension=0).astype(F32),
        lax.psum(mem, "shard"),
        lax.psum(vec, ("replica", "shard")),
    )


NT = (((1,), (1,)), ((), ()))
NN = (((1,), (0,)), ((), ()))
TN = (((0,), (0,)), ((), ()))


def dot(a, b, dims=NN):
    return lax.dot_general(a, b, dims, preferred_element_type=F32)


def head_lanes(shape, head):
    lane = lax.broadcasted_iota(jnp.int32, shape, 1)
    return (lane < HD) if head == 0 else (lane >= HD)


def mask_bias(qseg, kseg):
    allowed = (qseg == kseg) | (kseg == -1) | ((qseg == -2) & (kseg != -4))
    return jnp.where(allowed, 0.0, NEG)


def attend_kernel(scaling, q_ref, k_ref, v_ref, qseg_ref, kseg_ref, ctx_ref, lse_ref, bias_ref):
    @pl.when(pl.program_id(0) == 0)
    def _():
        bias_ref[...] = mask_bias(qseg_ref[...], kseg_ref[...])

    q, k, v = q_ref[...], k_ref[...], v_ref[...]
    zero_q = jnp.zeros_like(q)
    contexts, totals = [], []
    for head in range(2):
        qh = jnp.where(head_lanes(q.shape, head), q, zero_q)
        scores = dot(qh, k, NT) * scaling + bias_ref[...]
        top = jnp.max(scores, axis=1, keepdims=True)
        powers = jnp.exp(scores - top)
        lse = top + jnp.log(jnp.sum(powers, axis=1, keepdims=True))
        probs = powers * jnp.exp(top - lse)
        contexts.append(dot(probs.astype(BF), v))
        totals.append(lse)
    first = head_lanes(q.shape, 0)
    ctx_ref[...] = jnp.where(first, contexts[0], contexts[1])
    lse_ref[...] = jnp.where(first, totals[0], totals[1])


def attend_back_kernel(scaling, q_ref, k_ref, v_ref, qseg_ref, kseg_ref, weight_ref, ctx_ref, lse_ref, do_ref,
                       dq_ref, dk_ref, dv_ref, bias_ref):
    @pl.when(pl.program_id(0) == 0)
    def _():
        bias_ref[...] = mask_bias(qseg_ref[...], kseg_ref[...])

    q, k, v, do = q_ref[...], k_ref[...], v_ref[...], do_ref[...]
    weight = weight_ref[...] > 0
    dq, dk, dv = None, None, None
    for head in range(2):
        lanes = head_lanes(q.shape, head)
        qh = jnp.where(lanes, q, jnp.zeros_like(q))
        doh = jnp.where(lanes, do, jnp.zeros_like(do))
        lse = lse_ref[:, head * HD : head * HD + 1]
        scores = dot(qh, k, NT) * scaling + bias_ref[...]
        probs = jnp.exp(scores - lse)
        delta = jnp.sum(doh.astype(F32) * ctx_ref[...], axis=1, keepdims=True)
        d_scores = (probs * (dot(doh, v, NT) - delta)).astype(BF)
        kh = jnp.where(head_lanes(k.shape, head), k, jnp.zeros_like(k))
        part_q = dot(d_scores, kh)
        part_k = dot(jnp.where(weight, qh, jnp.zeros_like(qh)), d_scores, TN)
        part_v = dot(jnp.where(weight, doh, jnp.zeros_like(doh)), probs.astype(BF), TN)
        dq = part_q if dq is None else dq + part_q
        dk = part_k if dk is None else dk + part_k
        dv = part_v if dv is None else dv + part_v
    dq_ref[...] = (dq * scaling).astype(BF)
    dk_ref[...] = (dk * scaling).astype(BF)
    dv_ref[...] = dv.astype(BF)


def attention(query, keys, values, qseg, kseg, scaling):
    m, width = query.shape
    n = keys.shape[0]
    rows = pl.BlockSpec((m, 2 * HD), lambda i: (0, i))
    cols = pl.BlockSpec((n, 2 * HD), lambda i: (0, i))
    return pl.pallas_call(
        functools.partial(attend_kernel, scaling),
        grid=(width // (2 * HD),),
        out_shape=(jax.ShapeDtypeStruct((m, width), F32), jax.ShapeDtypeStruct((m, width), F32)),
        in_specs=[rows, cols, cols, pl.BlockSpec((m, 1), lambda i: (0, 0)), pl.BlockSpec((1, n), lambda i: (0, 0))],
        out_specs=[rows, rows],
        scratch_shapes=[pltpu.VMEM((m, n), F32)],
        compiler_params=pltpu.CompilerParams(vmem_limit_bytes=VMEM_LIMIT),
        name="attend",
    )(query, keys, values, qseg, kseg)


def attention_back(query, keys, values, qseg, kseg, weight, context, lse, d_context, scaling):
    m, width = query.shape
    n = keys.shape[0]
    rows = pl.BlockSpec((m, 2 * HD), lambda i: (0, i))
    cols = pl.BlockSpec((n, 2 * HD), lambda i: (0, i))
    turned = pl.BlockSpec((2 * HD, n), lambda i: (i, 0))
    column = pl.BlockSpec((m, 1), lambda i: (0, 0))
    return pl.pallas_call(
        functools.partial(attend_back_kernel, scaling),
        grid=(width // (2 * HD),),
        out_shape=(
            jax.ShapeDtypeStruct((m, width), BF),
            jax.ShapeDtypeStruct((width, n), BF),
            jax.ShapeDtypeStruct((width, n), BF),
        ),
        in_specs=[rows, cols, cols, column, pl.BlockSpec((1, n), lambda i: (0, 0)), column, rows, rows, rows],
        out_specs=[rows, turned, turned],
        scratch_shapes=[pltpu.VMEM((m, n), F32)],
        compiler_params=pltpu.CompilerParams(vmem_limit_bytes=VMEM_LIMIT),
        name="attend_back",
    )(query, keys, values, qseg, kseg, weight, context, lse, d_context)


def layer_stats(totals):
    center = totals - jnp.mean(totals, axis=-1, keepdims=True)
    spread = jnp.mean(center * center, axis=-1, keepdims=True)
    inverse = lax.rsqrt(spread + EPSILON)
    return (center * inverse, inverse)


def norm_back(grad_normed, normed, inverse):
    return inverse * (
        grad_normed
        - jnp.mean(grad_normed, axis=-1, keepdims=True)
        - normed * jnp.mean(grad_normed * normed, axis=-1, keepdims=True)
    )


LOG_ROWS = 32


def row_blocks(m, step=LOG_ROWS):
    return [pl.ds(i, step) for i in range(0, m, step)]


def matrix(ref, *lead, cols=None):
    value = ref[lead + (slice(None),) * 3 + ((slice(None),) if cols is None else (cols,))]
    return value.reshape(-1, value.shape[-1])


def full_vectors(vec_all, shards, srows, width):
    total = None
    for i in range(shards):
        row = lax.broadcasted_iota(jnp.int32, (srows, width), 0)
        col = lax.broadcasted_iota(jnp.int32, (srows, width), 1)
        place = jnp.where(col == row + i * srows, 1.0, 0.0).astype(BF)
        part = dot(vec_all[i], place)
        total = part if total is None else total + part
    return total


def segments(docs, ndoc, pos):
    end = docs[0, 0]
    seg = jnp.where(pos >= end, 1, 0)
    for i in range(1, ndoc):
        end = end + docs[0, i]
        seg = seg + jnp.where(pos >= end, 1, 0)
    return seg


def write_bias(bias, docs, ndoc, s, tok, seq, mem):
    m, n = bias.shape
    kpos = lax.broadcasted_iota(jnp.int32, (1, n), 1)
    place = kpos - seq
    mem_seg = jnp.where(place < mem // 2, -1, jnp.where(place < mem, -3, -4))
    kseg = jnp.where(kpos < seq, segments(docs, ndoc, kpos), mem_seg)
    for rows in row_blocks(m):
        index = lax.broadcasted_iota(jnp.int32, (LOG_ROWS, 1), 0) + rows.start
        qseg = jnp.where(index < tok, segments(docs, ndoc, index + s * tok), -2)
        bias[rows, :] = mask_bias(qseg, kseg)


def forward_kernel(shards, half, width, mem, ndoc,
                   wq, wk, wv, wo, hid, outw, tokens, memr, vec, bhid, docs,
                   o_qkvo, o_hid, o_out, o_x, o_q, o_k, o_v, o_ctx, o_lse, o_na, o_ia, o_al, o_act, o_slope, o_nf, o_if,
                   o_res, o_vec, o_sq,
                   w_qkvo, w_hid, w_out, x_all, vec_all, bh_all, rows, q_s, k_s, v_s, s_s, p_s, bias, inv_s, ctx, ctx_low, lse,
                   branch, na, ia, after, al, act, slope, second, nf, if_, res, vfull, sq,
                   zs, zr, as_, ar, bs, br, cs, cr, xs, xr, vs, vr, hs, hr, ls, os_):
    r, s, core, xbit, ybit, fc, fx, fy = neighbours()
    q_own, q_lo = 2 * core + ybit, 2 * core
    bufs = (w_qkvo, w_hid, w_out)
    tok = tokens.shape[0]
    m, n = rows.shape[0], x_all.shape[0]
    seq = tok * shards

    local = [pltpu.make_async_copy(w, w_qkvo.at[i, s], ls.at[i]) for i, w in enumerate((wq, wk, wv, wo))]
    local.append(pltpu.make_async_copy(tokens, rows.at[pl.ds(0, tok), :], ls.at[4]))
    late = [pltpu.make_async_copy(hid.at[:, :, pl.ds(q * width, width)], w_hid.at[q, s], ls.at[5 + q]) for q in range(4)]
    late.append(pltpu.make_async_copy(outw, w_out.at[s], ls.at[9]))
    for c in local + late:
        c.start()
    entry_barrier((fc, fx, fy), r, s, shards)

    def reg(g, sh, q0, nq, h0, nh):
        return region(bufs[g], g, sh, q0, nq, h0, nh)

    def block(i):
        return x_all.at[pl.ds(pl.multiple_of(i * tok, tok), tok), :]

    def rows_copy(sh, k):
        return remote(block(sh), block(sh), xs.at[k, sh], xr.at[sh], (r, s + 1 if k == 0 else s - 1))

    def on_line(k, fn):
        pl.when(s + 1 < shards if k == 0 else s > 0)(fn)

    sends = []

    def push(g):
        a = reg(g, s, q_own, 1, xbit, 1)
        for t in range(1, shards):
            sends.append(remote(a, a, zs.at[g, t], zr.at[g, s], (r, lax.rem(s + t, shards))))
            sends[-1].start()

    def hops(g, sh, first_x):
        if first_x:
            return ((reg(g, sh, q_own, 1, xbit, 1), fx), (reg(g, sh, q_own, 1, 0, 2), fy), (reg(g, sh, q_lo, 2, 0, 2), fc))
        return ((reg(g, sh, q_own, 1, xbit, 1), fy), (reg(g, sh, q_lo, 2, xbit, 1), fx), (reg(g, sh, q_lo, 2, 0, 2), fc))

    sems = ((as_, ar), (bs, br), (cs, cr))

    def hop(g, sh, first_x, k):
        a, dev = hops(g, sh, first_x)[k]
        return remote(a, a, sems[k][0].at[g, sh], sems[k][1].at[g, sh], (dev, s))

    def each_foreign(fn, g, t):
        for left in (True, False):
            sh = s - t if left else s + t
            first_x = (g + t + (1 if left else 0)) % 2 == 0
            pl.when(s >= t if left else s + t < shards)(functools.partial(fn, g, left, sh, first_x))

    def relay_rows(g, left, sh, first_x):
        rows_copy(sh, 0).wait_recv()
        k = 0 if left else 1
        on_line(k, lambda: rows_copy(sh, k).start())

    def stage0(g, left, sh, first_x):
        a = reg(g, sh, q_own, 1, xbit, 1)
        remote(a, a, zs.at[g, 0], zr.at[g, sh], (r, s)).wait_recv()
        hop(g, sh, first_x, 0).start()

    def stage1(g, left, sh, first_x):
        hop(g, sh, first_x, 0).wait_recv()
        hop(g, sh, first_x, 1).start()

    def stage2(g, left, sh, first_x):
        hop(g, sh, first_x, 1).wait_recv()
        hop(g, sh, first_x, 2).start()

    def stage3(g, left, sh, first_x):
        hop(g, sh, first_x, 2).wait_recv()

    def finish(g, left, sh, first_x):
        for k in range(3):
            hop(g, sh, first_x, k).wait_send()
        if g == 0:
            k = 0 if left else 1
            on_line(k, lambda: rows_copy(sh, k).wait_send())

    def run(stage, g):
        for t in range(1, shards):
            each_foreign(stage, g, t)

    saves = []

    def save(src, dst):
        saves.append(pltpu.make_async_copy(src, dst, os_.at[len(saves)]))
        saves[-1].start()

    for c in local[:4]:
        c.wait()
    push(0)
    local[4].wait()
    rows[pl.ds(tok, mem), :] = memr[...]
    rows[pl.ds(tok + mem, MEM_PAD - mem), :] = jnp.zeros((MEM_PAD - mem, width), F32)
    block(s)[...] = rows[pl.ds(0, tok), :].astype(BF)
    x_all[pl.ds(seq, MEM_PAD), :] = rows[pl.ds(tok, MEM_PAD), :].astype(BF)
    x_all[pl.ds(seq + MEM_PAD, MEM_KEYS - MEM_PAD), :] = jnp.zeros((MEM_KEYS - MEM_PAD, width), BF)
    for k in range(2):
        on_line(k, lambda k=k: rows_copy(s, k).start())
    vec_all[s] = vec[...]
    bh_all[s] = bhid[...]
    for t in range(1, shards):
        dev = (r, lax.rem(s + t, shards))
        sends.append(remote(vec_all.at[s], vec_all.at[s], vs.at[t], vr.at[s], dev))
        sends[-1].start()
        sends.append(remote(bh_all.at[s], bh_all.at[s], hs.at[t], hr.at[s], dev))
        sends[-1].start()
    write_bias(bias, docs, ndoc, s, tok, seq, mem)
    for c in late:
        c.wait()
    run(stage0, 0)
    for t in range(1, shards):
        other = lax.rem(s + t, shards)
        remote(vec_all.at[other], vec_all.at[other], vs.at[t], vr.at[other], (r, other)).wait_recv()
        remote(bh_all.at[other], bh_all.at[other], hs.at[t], hr.at[other], (r, other)).wait_recv()
    vfull[...] = full_vectors(vec_all, shards, 2 * half, width)
    each_foreign(relay_rows, 0, 1)
    push(1)
    run(stage1, 0)
    each_foreign(relay_rows, 0, 2)
    run(stage2, 0)
    for t in range(3, shards):
        each_foreign(relay_rows, 0, t)
    run(stage0, 1)
    push(2)
    run(stage3, 0)
    save(w_qkvo, o_qkvo)
    save(x_all, o_x)
    save(vfull, o_vec)
    run(stage1, 1)

    def vrow(i):
        return vfull[pl.ds(i, 1), :]

    def bias_cols(i, c):
        return vfull[pl.ds(i, 1), c]

    @pl.loop(0, width // 256)
    def _(ct):
        c = pl.ds(pl.multiple_of(ct * 256, 256), 256)
        a = block(s)[...]
        wt = matrix(w_qkvo, 0, cols=c)
        b = bias_cols(0, c)
        for part, at, size in ((a, 0, tok), (x_all[pl.ds(seq, MEM_PAD), :], tok, MEM_PAD)):
            y = (dot(part, wt) + b).astype(BF) * jnp.asarray(0.125, BF)
            q_s[2 * ct, pl.ds(at, size)] = y[:, :128]
            q_s[2 * ct + 1, pl.ds(at, size)] = y[:, 128:]
        step = 384 if n % 384 == 0 else 128

        @pl.loop(0, n // step)
        def _(i):
            at = pl.ds(pl.multiple_of(i * step, step), step)
            xb = x_all[at, :]
            y = dot(xb, matrix(w_qkvo, 1, cols=c)).astype(BF)
            k_s[2 * ct, at] = y[:, :128]
            k_s[2 * ct + 1, at] = y[:, 128:]
            y = (dot(xb, matrix(w_qkvo, 2, cols=c)) + bias_cols(1, c)).astype(BF)
            v_s[2 * ct, at] = y[:, :128]
            v_s[2 * ct + 1, at] = y[:, 128:]

    save(q_s, o_q)
    save(k_s, o_k)
    save(v_s, o_v)
    run(stage2, 1)
    lane = lax.broadcasted_iota(jnp.int32, (m, 128), 1)

    def pair(p):
        outs = []
        for head in range(2):
            qh = jnp.where((lane < HD) == (head == 0), q_s[p], jnp.zeros((m, 128), BF))
            s_s[...] = dot(qh, k_s[p], NT)
            for rb in row_blocks(m):
                sc = s_s[rb, :] + bias[rb, :]
                top = jnp.max(sc, axis=1, keepdims=True)
                e = jnp.exp(sc - top)
                tot = jnp.sum(e, axis=1, keepdims=True)
                p_s[rb, :] = e.astype(BF)
                wide = jnp.broadcast_to(top + jnp.log(tot), (LOG_ROWS, 128))
                inv = jnp.broadcast_to(1.0 / tot, (LOG_ROWS, 128))
                if head == 0:
                    lse[p, rb] = wide
                    inv_s[rb, :] = inv
                else:
                    right = lane[:LOG_ROWS] >= HD
                    lse[p, rb] = jnp.where(right, wide, lse[p, rb])
                    inv_s[rb, :] = jnp.where(right, inv, inv_s[rb, :])
            outs.append(dot(p_s[...], v_s[p]))
        value = jnp.where(lane < HD, outs[0], outs[1]) * inv_s[...]
        c = pl.ds(pl.multiple_of(p * 128, 128), 128)
        ctx[:, c] = value
        ctx_low[:, c] = value.astype(BF)

    pl.loop(0, 2)(pair)
    run(stage0, 2)
    pl.loop(2, 4)(pair)
    run(stage1, 2)
    pl.loop(4, width // 128)(pair)
    run(stage2, 2)
    save(ctx, o_ctx)
    save(lse, o_lse)

    def stats(totals):
        center = totals - jnp.mean(totals, axis=1, keepdims=True)
        spread = jnp.mean(center * center, axis=1, keepdims=True)
        inverse = lax.rsqrt(spread + EPSILON)
        return center * inverse, inverse

    @pl.loop(0, width // 256)
    def _(ct):
        c = pl.ds(pl.multiple_of(ct * 256, 256), 256)
        branch[:, c] = dot(ctx_low[...], matrix(w_qkvo, 3, cols=c)) + bias_cols(2, c)

    sq[...] = jnp.zeros_like(sq)

    def add_square(i, rb, value):
        if rb.start < tok:
            total = jnp.sum(value * value, axis=0, keepdims=True)
            sq[pl.ds(i, 1), :] = sq[pl.ds(i, 1), :] + total

    for rb in row_blocks(m):
        b = branch[rb, :]
        add_square(1, rb, b)
        normed, inverse = stats(rows[rb, :] + b)
        na[rb, :] = normed
        ia[rb, :] = jnp.broadcast_to(inverse, (LOG_ROWS, 128))
        y = normed * vrow(4) + vrow(5)
        after[rb, :] = y
        al[rb, :] = y.astype(BF)
    save(na, o_na)
    save(ia, o_ia)
    save(al, o_al)
    run(stage3, 1)
    save(w_hid, o_hid)

    @pl.loop(0, 4)
    def _(q):
        @pl.loop(0, width // 256)
        def _(ct):
            c = pl.ds(pl.multiple_of(ct * 256, 256), 256)
            s_s[:, :256] = dot(al[...], matrix(w_hid, q, cols=c))
            b = bh_all[q, pl.ds(0, 1), c]
            for rb in row_blocks(m):
                z = s_s[rb, :256] + b
                he = 0.5 * (1.0 + lax.erf(z * GELU_ROOT))
                act[q, rb, c] = (z * he).astype(BF)
                slope[q, rb, c] = he + z * jnp.exp(-0.5 * z * z) * GELU_DENSITY

    save(act, o_act)
    save(slope, o_slope)
    run(stage3, 2)
    save(w_out, o_out)

    @pl.loop(0, width // 256)
    def _(ct):
        c = pl.ds(pl.multiple_of(ct * 256, 256), 256)
        total = dot(act[0], matrix(w_out, 0, cols=c))
        for q in range(1, 4):
            total = total + dot(act[q], matrix(w_out, q, cols=c))
        second[:, c] = total + bias_cols(3, c)

    for rb in row_blocks(m):
        b = second[rb, :]
        add_square(2, rb, b)
        normed, inverse = stats(after[rb, :] + b)
        nf[rb, :] = normed
        if_[rb, :] = jnp.broadcast_to(inverse, (LOG_ROWS, 128))
        y = normed * vrow(6) + vrow(7)
        add_square(0, rb, y)
        res[rb, :] = y
    save(nf, o_nf)
    save(if_, o_if)
    save(res, o_res)
    save(sq, o_sq)
    for g in range(3):
        run(finish, g)
    for c in sends:
        c.wait_send()
    for k in range(2):
        on_line(k, lambda k=k: rows_copy(s, k).wait_send())
    for c in saves:
        c.wait()


def forward_all(wq, wk, wv, wo, hid, outw, tokens, memr, vec, bhid, docs):
    shards = lax.axis_size("shard")
    half, width = wq.shape[0] // 2, wq.shape[1]
    tok, mem = tokens.shape[0], memr.shape[0]
    m, n = tok + MEM_PAD, tok * shards + MEM_KEYS
    pairs = width // 128
    stack = (4, shards, 2, half, width)
    any_space = pl.BlockSpec(memory_space=pl.ANY)
    vm = pl.BlockSpec(memory_space=pltpu.VMEM)
    dma = pltpu.SemaphoreType.DMA

    def sd(shape, dtype):
        return jax.ShapeDtypeStruct(shape, dtype)

    outs = (
        sd(stack, BF), sd(stack, BF), sd((shards, 4, 2, half, width), BF), sd((n, width), BF),
        sd((pairs, m, 128), BF), sd((pairs, n, 128), BF), sd((pairs, n, 128), BF),
        sd((m, width), F32), sd((pairs, m, 128), F32), sd((m, width), F32), sd((m, 128), F32), sd((m, width), BF),
        sd((4, m, width), BF), sd((4, m, width), F32), sd((m, width), F32), sd((m, 128), F32), sd((m, width), F32),
        sd((16, width), F32), sd((8, width), F32),
    )
    V = pltpu.VMEM
    scratch = [
        V(stack, BF), V(stack, BF), V((shards, 4, 2, half, width), BF), V((n, width), BF), V((shards,) + vec.shape, BF), V((shards, 8, width), F32),
        V((m, width), F32), V((pairs, m, 128), BF), V((pairs, n, 128), BF), V((pairs, n, 128), BF), V((m, n), F32),
        V((m, n), BF), V((m, n), F32), V((m, 128), F32), V((m, width), F32), V((m, width), BF), V((pairs, m, 128), F32),
        V((m, width), F32), V((m, width), F32), V((m, 128), F32), V((m, width), F32), V((m, width), BF),
        V((4, m, width), BF), V((4, m, width), F32), V((m, width), F32), V((m, width), F32), V((m, 128), F32),
        V((m, width), F32), V((16, width), F32), V((8, width), F32),
    ]
    return pl.pallas_call(
        functools.partial(forward_kernel, shards, half, width, mem, docs.shape[1]),
        out_shape=outs,
        in_specs=[any_space] * 7 + [vm, vm, vm, pl.BlockSpec(memory_space=pltpu.SMEM)],
        out_specs=[any_space] * len(outs),
        scratch_shapes=scratch
        + [dma((3, shards))] * 8 + [dma((2, shards))] + [dma((shards,))] * 5 + [dma((10,)), dma((len(outs),))],
        compiler_params=pltpu.CompilerParams(collective_id=3, has_side_effects=True, vmem_limit_bytes=VMEM_LIMIT),
        name="forward_layer",
    )(
        wq.reshape(2, half, width), wk.reshape(2, half, width), wv.reshape(2, half, width), wo.reshape(2, half, width),
        hid.reshape(2, half, 4 * width), outw.reshape(4, 2, half, width), tokens, memr, vec, bhid, docs,
    )


def backward_kernel(shards, half, width, mem,
                    h_qkvo, h_hid, h_out, h_x, h_q, h_k, h_v, h_ctx, h_lse, h_na, h_ia, h_al, h_act, h_slope, h_nf, h_if,
                    vfull, sq, out_grad, mem_grad, docs,
                    o_qkvo, o_hid, o_out, o_x, o_vec,
                    grad, ra, rb, rc, rd, rx, rm, rv, vz, vacc,
                    wbuf, x_all, pq, pk, pv, pctx, plse, bias, s_s, dp_s, p_s, ds_s, al, abuf, sbuf, d_pre, nf, if_,
                    gr, d_out, back, d_branch, dctx, dq, dkt, dvt, mem_s,
                    asem, arem, bsem, brem, csem, crem, zsem, zrem, dsem, drem, xsem, xrem, msem, mrem, vsem, vrem,
                    vzs, vzr, fsem, wsem, psem, asem_, lsem, osem):
    r, s, core, xbit, ybit, fc, fx, fy = neighbours()
    q_own, q_lo = 2 * core + ybit, 2 * core
    tok = out_grad.shape[0]
    m, n = gr.shape[0], x_all.shape[0]
    seq = tok * shards
    pairs = width // 128
    outs = (o_qkvo, o_hid, o_out)
    groups = (2, 1, 0)
    units = 3 * shards

    def load(src, dst, i):
        c = pltpu.make_async_copy(src, dst, lsem.at[i])
        c.start()
        return c

    def w_copy(j):
        if j < 8:
            src = (h_out if j % 2 == 0 else h_hid).at[j // 2]
        else:
            src = h_qkvo.at[(3, 1, 2, 0)[j - 8]]
        return pltpu.make_async_copy(src, wbuf.at[j % 4], wsem.at[j])

    def a_copy(q):
        return (
            pltpu.make_async_copy(h_act.at[q], abuf.at[q % 2], asem_.at[0, q]),
            pltpu.make_async_copy(h_slope.at[q], sbuf.at[q % 2], asem_.at[1, q]),
        )

    def p_copy(p, slot):
        return [
            pltpu.make_async_copy(a.at[p], b.at[slot], psem.at[i, slot])
            for i, (a, b) in enumerate(((h_q, pq), (h_k, pk), (h_v, pv), (h_lse, plse)))
        ]

    first = [load(h_nf, nf, 0), load(out_grad, gr.at[pl.ds(0, tok), :], 1), load(h_if, if_, 2)]
    for j in range(3):
        w_copy(j).start()
    for c in a_copy(0):
        c.start()
    second = [load(h_al, al, 3), load(h_x, x_all, 6), load(h_ctx, pctx, 7)]
    entry_barrier((fc, fx, fy), r, s, shards)

    def unit_shard(u):
        return lax.rem(u, shards)

    def copy_a(u):
        return remote(grad.at[u, 1 - core], ra.at[u], asem.at[u], arem.at[u], (fc, s))

    def by_order(u, x_first, y_first):
        pl.when(lax.rem(u, 2) == 0)(x_first)
        pl.when(lax.rem(u, 2) == 1)(y_first)

    def copy_b(u, x_first):
        if x_first:
            return remote(grad.at[u, core, :, 1 - xbit], rb.at[u], bsem.at[u], brem.at[u], (fx, s))
        return remote(grad.at[u, core, 1 - ybit], rb.at[u], bsem.at[u], brem.at[u], (fy, s))

    def copy_c(u, x_first):
        if x_first:
            return remote(grad.at[u, core, 1 - ybit, xbit], rc.at[u], csem.at[u], crem.at[u], (fy, s))
        return remote(grad.at[u, core, ybit, 1 - xbit], rc.at[u], csem.at[u], crem.at[u], (fx, s))

    def copy_z(u):
        return remote(
            grad.at[u, core, ybit, xbit], rd.at[u // shards, s], zsem.at[u], zrem.at[u // shards, s], (r, unit_shard(u))
        )

    def start_b(u):
        copy_a(u).wait_recv()
        grad[u, core] = grad[u, core] + ra[u]
        by_order(u, lambda: copy_b(u, True).start(), lambda: copy_b(u, False).start())

    def start_c(u):
        copy_b(u, True).wait_recv()

        def x_first():
            grad[u, core, :, xbit] = grad[u, core, :, xbit] + rb[u]
            copy_c(u, True).start()

        def y_first():
            grad[u, core, ybit] = grad[u, core, ybit] + rb[u]
            copy_c(u, False).start()

        by_order(u, x_first, y_first)

    def start_z(u):
        copy_c(u, True).wait_recv()
        grad[u, core, ybit, xbit] = grad[u, core, ybit, xbit] + rc[u]
        pl.when(s != unit_shard(u))(lambda: copy_z(u).start())

    def hop(k, j):
        o = outs[groups[k]]
        if k % 2 == 0:
            a, dev = ((o.at[q_own, xbit], fx), (o.at[q_own], fy), (o.at[pl.ds(q_lo, 2)], fc))[j]
        else:
            a, dev = ((o.at[q_own, xbit], fy), (o.at[pl.ds(q_lo, 2), xbit], fx), (o.at[pl.ds(q_lo, 2)], fc))[j]
        return remote(a, a, dsem.at[k, j], drem.at[k, j], (dev, s))

    def finish_group(k):
        total = grad[k * shards + s, core, ybit, xbit].astype(F32)
        for t in range(1, shards):
            other = lax.rem(s + t, shards)
            slot = rd.at[k, other]
            remote(slot, slot, zsem.at[0], zrem.at[k, other], (r, s)).wait_recv()
            total = total + rd[k, other].astype(F32)
        fin = rc.at[k * shards]
        fin[...] = total.astype(BF)
        c = pltpu.make_async_copy(fin, outs[groups[k]].at[q_own, xbit], fsem.at[k])
        c.start()
        c.wait()
        hop(k, 0).start()

    def hop_step(k, j):
        hop(k, j - 1).wait_recv()
        hop(k, j).start()

    lag = 2
    ticks = units + 2 * lag + 1 + 2 * lag

    def tick(i):
        def guarded(lo, fn):
            pl.when((i >= lo) & (i < lo + units))(lambda: fn(i - lo))

        guarded(0, start_b)
        guarded(lag, start_c)
        guarded(2 * lag, start_z)
        for k in range(3):
            when = shards * (k + 1) + 2 * lag
            pl.when(i == when)(functools.partial(finish_group, k))
            for j in (1, 2):
                pl.when(i == when + j * lag)(functools.partial(hop_step, k, j))

    def vrow(i):
        return vfull[pl.ds(i, 1), :]

    index = lax.broadcasted_iota(jnp.int32, (m, 1), 0)
    once = jnp.where((index < tok) | ((index < tok + mem) & (s == 0)), 1.0, 0.0)

    def add_sum(i, rw, value):
        total = jnp.sum(value * once[rw.start : rw.start + LOG_ROWS], axis=0, keepdims=True)
        vacc[0, pl.ds(i, 1), :] = vacc[0, pl.ds(i, 1), :] + total

    def mean(v):
        return jnp.mean(v, axis=1, keepdims=True)

    def norm_back_rows(e, normed, inverse):
        return inverse * (e - mean(e) - normed * mean(e * normed))

    vacc[0] = jnp.zeros(vacc.shape[1:], F32)
    for c in first:
        c.wait()
    gr[pl.ds(tok, mem), :] = mem_grad[...]
    gr[pl.ds(tok + mem, MEM_PAD - mem), :] = jnp.zeros((MEM_PAD - mem, width), F32)
    for rw in row_blocks(m):
        g, normed = gr[rw, :], nf[rw, :]
        add_sum(6, rw, g * normed)
        add_sum(7, rw, g)
        v = norm_back_rows(g * vrow(6), normed, if_[rw, :1])
        back[rw, :] = v
        low = v.astype(BF)
        add_sum(3, rw, low.astype(F32))
        d_out[rw, :] = low
    na, ia = nf, if_
    second += [load(h_na, na, 4), load(h_ia, ia, 5)]
    second[0].wait()
    once_low = once.astype(BF)

    def turned(a, b):
        return dot(a, b, TN)

    def put(k, q, j, value):
        grad[pl.ds(k * shards + 2 * j, 2), q // 2, q % 2] = value.astype(BF).reshape(2, 2, half, width)

    wide = 2 * 2 * half
    for q in range(4):
        for c in a_copy(q):
            c.wait()
        if q + 1 < 4:
            for c in a_copy(q + 1):
                c.start()
        w_copy(2 * q).wait()
        w_copy(2 * q + 3).start()
        a = abuf.at[q % 2]
        do = d_out[...] * once_low
        for j in range(2):
            value = turned(a[:, j * wide : (j + 1) * wide], do)
            grad[q, j] = value.astype(BF).reshape(2, 2, half, width)
        copy_a(q).start()
        for j in range(2):
            wt = wbuf[(2 * q) % 4, 2 * j : 2 * j + 2].reshape(wide, width)
            s_s[:, j * wide : (j + 1) * wide] = dot(d_out[...], wt, NT)
        for rw in row_blocks(m):
            v = s_s[rw, :width] * sbuf[q % 2, rw, :]
            low = v.astype(BF)
            d_pre[rw, :] = low
            add_sum(8 + q, rw, low.astype(F32))
        if q >= 1:
            tick(jnp.int32(q - 1))
        w_copy(2 * q + 1).wait()
        w_copy(2 * q + 4).start()
        dp = d_pre[...] * once_low
        for j in range(2):
            put(1, q, j, turned(al[:, j * wide : (j + 1) * wide], dp))
        for j in range(2):
            wt = wbuf[(2 * q + 1) % 4, 2 * j : 2 * j + 2].reshape(wide, width)
            c = pl.ds(j * wide, wide)
            s_s[:, c] = dot(d_pre[...], wt, NT)
        for rw in row_blocks(m):
            back[rw, :] = back[rw, :] + s_s[rw, :width]
    for j in range(shards):
        copy_a(shards + j).start()
    tick(jnp.int32(3))
    for c in p_copy(0, 0):
        c.start()

    for c in second[1:]:
        c.wait()

    for rw in row_blocks(m):
        f, normed = back[rw, :], na[rw, :]
        add_sum(4, rw, f * normed)
        add_sum(5, rw, f)
        v = norm_back_rows(f * vrow(4), normed, ia[rw, :1])
        back[rw, :] = v
        low = v.astype(BF)
        d_branch[rw, :] = low
        add_sum(2, rw, low.astype(F32))
        d_out[rw, :] = pctx[rw, :].astype(BF)
    write_bias(bias, docs, docs.shape[1], s, tok, seq, mem)
    w_copy(8).wait()
    w_copy(11).start()
    db = d_branch[...] * once_low
    for j in range(2):
        put(2, 3, j, turned(d_out[:, j * wide : (j + 1) * wide], db))
    for j in range(2):
        wt = wbuf[0, 2 * j : 2 * j + 2].reshape(wide, width)
        value = dot(d_branch[...], wt, NT).astype(BF)
        for i in range(wide // 128):
            dctx[j * (wide // 128) + i] = value[:, i * 128 : (i + 1) * 128]
    lane = lax.broadcasted_iota(jnp.int32, (m, 128), 1)
    lane_k = lax.broadcasted_iota(jnp.int32, (n, 128), 1)
    tick(jnp.int32(4))

    def pair(p):
        slot = lax.rem(p, 2)
        for c in p_copy(p, slot):
            c.wait()

        @pl.when(p + 1 < pairs)
        def _():
            for c in p_copy(p + 1, 1 - slot):
                c.start()

        c = pl.ds(pl.multiple_of(p * 128, 128), 128)
        part_q, part_k, part_v = None, None, None
        zero = jnp.zeros((m, 128), BF)
        for head in range(2):
            mine = (lane < HD) == (head == 0)
            qh = jnp.where(mine, pq[slot], zero)
            doh = jnp.where(mine, dctx[p], zero)
            s_s[...] = dot(qh, pk[slot], NT)
            dp_s[...] = dot(doh, pv[slot], NT)
            for rw in row_blocks(m):
                sub = slice(rw.start, rw.start + LOG_ROWS)
                delta = jnp.sum(doh[sub].astype(F32) * pctx[rw, c], axis=1, keepdims=True)
                top = plse[slot, rw, head * HD : head * HD + 1]
                probs = jnp.exp(s_s[rw, :] + bias[rw, :] - top)
                p_s[rw, :] = probs.astype(BF)
                ds_s[rw, :] = (probs * (dp_s[rw, :] - delta)).astype(BF)
            kh = jnp.where((lane_k < HD) == (head == 0), pk[slot], jnp.zeros((n, 128), BF))
            a = dot(ds_s[...], kh)
            b = turned(qh * once_low, ds_s[...])
            d = turned(doh * once_low, p_s[...])
            part_q = a if head == 0 else part_q + a
            part_k = b if head == 0 else part_k + b
            part_v = d if head == 0 else part_v + d
        dq[:, c] = (part_q * 0.125).astype(BF)
        dkt[c, :] = part_k.astype(BF)
        dvt[c, :] = part_v.astype(BF)
        pl.when(lax.rem(p, 2) == 1)(lambda: tick(5 + p // 2))

    pl.loop(0, pairs)(pair)

    ones = jnp.ones((8, n), BF)
    vacc[0, pl.ds(1, 1), :] = dot(ones, dvt[...], NT)[:1]
    for rw in row_blocks(m):
        add_sum(0, rw, dq[rw, :].astype(F32))
    vacc[0, pl.ds(12, 3), :] = sq[pl.ds(0, 3), :]
    rv_first = remote(vacc.at[0], rv.at[0], vsem.at[0], vrem.at[0], (fc, s))
    rv_first.start()
    dqm = dq[...] * once_low
    for j in range(2):
        xs_ = x_all[:, j * wide : (j + 1) * wide]
        x_own = jnp.concatenate([
            x_all[pl.ds(pl.multiple_of(s * tok, tok), tok), j * wide : (j + 1) * wide],
            x_all[pl.ds(seq, MEM_PAD), j * wide : (j + 1) * wide],
        ])
        put(2, 0, j, turned(x_own, dqm))
        xt = jnp.transpose(xs_)
        put(2, 1, j, dot(xt, dkt[...], NT))
        put(2, 2, j, dot(xt, dvt[...], NT))
    for j in range(shards):
        copy_a(2 * shards + j).start()
    tick(jnp.int32(8))

    def vec_hop(k):
        return remote(vacc.at[k], rv.at[k], vsem.at[k], vrem.at[k], ((fc, fx, fy)[k], s))

    def vec_step(k):
        vec_hop(k - 1).wait_recv()
        vacc[k] = vacc[k - 1] + rv[k - 1]
        vec_hop(k).start()

    vec_step(1)
    w_copy(9).wait()
    w_copy(10).wait()
    wkm = wbuf[1].reshape(width, width)
    wvm = wbuf[2].reshape(width, width)
    spare = (abuf.at[0, pl.ds(0, tok)], abuf.at[1, pl.ds(0, tok)], d_pre.at[pl.ds(0, tok)])
    small = []

    def to_shard(src, dst, ssem, rsem, t):
        return remote(src, dst.at[s], ssem.at[t], rsem.at[s], (r, lax.rem(s + t, shards)))

    for i in range(shards):
        t = i + 1
        blk = lax.rem(s + t, shards)
        c = pl.ds(pl.multiple_of(blk * tok, tok), tok)
        value = dot(wkm, dkt[:, c]) + dot(wvm, dvt[:, c])
        value = jnp.transpose(value).astype(BF)
        if t < shards:
            spare[i][...] = value
            small.append(to_shard(spare[i], rx, xsem, xrem, t))
            small[-1].start()
        else:
            rx[s] = value
        if i == 1:
            tick(jnp.int32(9))
    value = dot(wkm, dkt[:, pl.ds(seq, MEM_KEYS)]) + dot(wvm, dvt[:, pl.ds(seq, MEM_KEYS)])
    mem_s[...] = jnp.transpose(value)[:MEM_PAD]
    rm[s] = mem_s[...]
    for t in range(1, shards):
        small.append(to_shard(mem_s, rm, msem, mrem, t))
        small[-1].start()
    vec_step(2)
    tick(jnp.int32(10))
    w_copy(11).wait()
    for j in range(2):
        wt = wbuf[3, 2 * j : 2 * j + 2].reshape(wide, width)
        c = pl.ds(j * wide, wide)
        back[:, c] = back[:, c] + dot(dq[...], wt, NT)
    vec_hop(2).wait_recv()
    vz[s] = vacc[2] + rv[2]
    for t in range(1, shards):
        small.append(to_shard(vz.at[s], vz, vzs, vzr, t))
        small[-1].start()
    pl.loop(11, ticks)(tick)

    for t in range(1, shards):
        other = lax.rem(s + t, shards)
        for buf, rsem in ((rx, xrem), (rm, mrem), (vz, vzr)):
            remote(buf.at[other], buf.at[other], xsem.at[0], rsem.at[other], (r, s)).wait_recv()
    sx, sm, sv = back[pl.ds(0, tok), :], back[pl.ds(tok, MEM_PAD), :], vz[0]
    for t in range(shards):
        sx = sx + rx[t].astype(F32)
        sm = sm + rm[t]
        if t:
            sv = sv + vz[t]
    gr[pl.ds(0, tok), :] = sx
    gr[pl.ds(tok, MEM_PAD), :] = sm
    final = [
        pltpu.make_async_copy(gr, o_x, osem.at[0]),
    ]
    for c in final:
        c.start()
    o_vec[...] = sv
    for k in range(3):
        hop(k, 2).wait_recv()
    for c in final:
        c.wait()

    @pl.loop(0, units)
    def _(u):
        copy_a(u).wait_send()
        copy_b(u, True).wait_send()
        copy_c(u, True).wait_send()
        pl.when(s != unit_shard(u))(lambda: copy_z(u).wait_send())

    for k in range(3):
        for j in range(3):
            hop(k, j).wait_send()
    for c in small:
        c.wait_send()
    for k in range(3):
        vec_hop(k).wait_send()


def backward_all(saved, out_grad, mem_grad, docs):
    shards = lax.axis_size("shard")
    tok, width = out_grad.shape
    mem = mem_grad.shape[0]
    half = saved[0].shape[3]
    m, n = tok + MEM_PAD, tok * shards + MEM_KEYS
    pairs = width // 128
    any_space = pl.BlockSpec(memory_space=pl.ANY)
    vm = pl.BlockSpec(memory_space=pltpu.VMEM)
    dma = pltpu.SemaphoreType.DMA
    V = pltpu.VMEM
    units = 3 * shards
    piece4 = (4, 2, half, width)
    outs = tuple(jax.ShapeDtypeStruct(piece4, BF) for _ in range(3)) + (
        jax.ShapeDtypeStruct((m, width), F32),
        jax.ShapeDtypeStruct((16, width), F32),
    )
    big = (4, 2, half, width)
    scratch = [
        V((units, 2, 2, 2, half, width), BF), V((units, 2, 2, half, width), BF), V((units, 2, half, width), BF),
        V((units, half, width), BF), V((3, shards, half, width), BF), V((shards, tok, width), BF),
        V((shards, MEM_PAD, width), F32), V((3, 16, width), F32), V((shards, 16, width), F32), V((3, 16, width), F32),
        V((4,) + big, BF), V((n, width), BF), V((2, m, 128), BF), V((2, n, 128), BF), V((2, n, 128), BF),
        V((m, width), F32), V((2, m, 128), F32), V((m, n), F32), V((m, n), F32), V((m, n), F32), V((m, n), BF),
        V((m, n), BF), V((m, width), BF), V((2, m, width), BF),
        V((2, m, width), F32), V((m, width), BF), V((m, width), F32), V((m, 128), F32), V((m, width), F32),
        V((m, width), BF), V((m, width), F32), V((m, width), BF), V((pairs, m, 128), BF), V((m, width), BF),
        V((width, n), BF), V((width, n), BF), V((MEM_PAD, width), F32),
    ]
    sems = (
        [dma((units,))] * 8
        + [dma((3, 3)), dma((3, 3)), dma((shards,)), dma((shards,)), dma((shards,)), dma((shards,))]
        + [dma((3,)), dma((3,)), dma((shards,)), dma((shards,)), dma((3,)), dma((12,)), dma((4, 2)), dma((2, 4))]
        + [dma((8,)), dma((1,))]
    )
    sems[7] = dma((3, shards))
    return pl.pallas_call(
        functools.partial(backward_kernel, shards, half, width, mem),
        out_shape=outs,
        in_specs=[any_space] * 16 + [vm, vm, any_space, vm, pl.BlockSpec(memory_space=pltpu.SMEM)],
        out_specs=[any_space] * 4 + [vm],
        scratch_shapes=scratch + sems,
        compiler_params=pltpu.CompilerParams(collective_id=4, has_side_effects=True, vmem_limit_bytes=VMEM_LIMIT),
        name="backward_layer",
    )(*saved, out_grad, mem_grad, docs)


def plain_body(tokens, memory_rows, doc_lengths, w_query, w_key, w_value, w_attn_out, w_hidden, w_output,
         b_query, b_value, b_attn_out, b_hidden, b_output, gain_attn, shift_attn, gain_ffn, shift_ffn,
         out_grad, memory_grad):
    tok, width = tokens.shape
    mem = memory_rows.shape[1]
    shards = lax.axis_size("shard")
    s = lax.axis_index("shard")
    seq = tok * shards
    srows = w_query.shape[0]
    m = tok + MEM_PAD
    n = seq + MEM_KEYS
    scaling = 1.0 / math.sqrt(HD)

    vec = jnp.concatenate(
        [v.reshape(-1, srows) for v in (
            b_query, b_value, b_attn_out, b_output, gain_attn, shift_attn, gain_ffn, shift_ffn, b_hidden
        )]
        + [jnp.zeros((4, srows), BF)]
    )
    vec = lax.dynamic_update_slice(jnp.zeros((16, width), BF), vec, (0, s * srows))
    rows = jnp.concatenate([tokens, memory_rows[0], jnp.zeros((MEM_PAD - mem, width), F32)])
    low_rows = rows.astype(BF)
    qkvo = jnp.stack([w_query, w_key, w_value, w_attn_out])
    qkvo, w_hid, w_out, x_tok, vec_all = gather_plain(qkvo, w_hidden, w_output, low_rows[:tok], vec)
    vec = jnp.sum(vec_all.astype(F32), axis=0)
    bq, bv, bo, bout, ga, sa, gf, sf = (vec[i] for i in range(8))
    bh = jnp.transpose(vec[8:12].reshape(4, shards, srows), (1, 0, 2)).reshape(4 * width)

    doc_ends = jnp.cumsum(doc_lengths[0])
    seg = jnp.sum((jnp.arange(seq, dtype=jnp.int32)[:, None] >= doc_ends[None, :]).astype(jnp.int32), axis=1)
    place = jnp.arange(MEM_KEYS, dtype=jnp.int32)
    mem_seg = jnp.where(place < mem // 2, -1, jnp.where(place < mem, -3, -4)).astype(jnp.int32)
    kseg = jnp.concatenate([seg, mem_seg])[None, :]
    qseg = jnp.concatenate(
        [lax.dynamic_slice_in_dim(seg, s * tok, tok), jnp.full((MEM_PAD,), -2, jnp.int32)]
    )[:, None]
    index = jnp.arange(m, dtype=jnp.int32)[:, None]
    once = jnp.where(index < tok, 1.0, jnp.where((index < tok + mem) & (s == 0), 1.0, 0.0)).astype(F32)
    once_low = once.astype(BF)

    x_all = jnp.concatenate([x_tok, low_rows[tok:], jnp.zeros((MEM_KEYS - MEM_PAD, width), BF)])
    query = (jnp.dot(low_rows, qkvo[0], preferred_element_type=F32) + bq).astype(BF)
    keys = jnp.dot(x_all, qkvo[1], preferred_element_type=F32).astype(BF)
    values = (jnp.dot(x_all, qkvo[2], preferred_element_type=F32) + bv).astype(BF)
    context, lse = attention(query, keys, values, qseg, kseg, scaling)
    context_low = context.astype(BF)
    branch = jnp.dot(context_low, qkvo[3], preferred_element_type=F32) + bo
    normed_attn, inverse_attn = layer_stats(rows + branch)
    after_attn = normed_attn * ga + sa
    after_low = after_attn.astype(BF)
    pre_act = jnp.concatenate([jnp.dot(after_low, w_hid[q], preferred_element_type=F32) for q in range(4)], axis=1) + bh
    half_erf = 0.5 * (1.0 + lax.erf(pre_act * GELU_ROOT))
    act_low = (pre_act * half_erf).astype(BF)
    second = jnp.dot(act_low, w_out, preferred_element_type=F32) + bout
    normed_ffn, inverse_ffn = layer_stats(after_attn + second)
    result = normed_ffn * gf + sf

    grads = jnp.concatenate([out_grad, memory_grad[0], jnp.zeros((MEM_PAD - mem, width), F32)])
    back_ffn = norm_back(grads * gf, normed_ffn, inverse_ffn)
    d_output = back_ffn.astype(BF)
    g_out = jnp.einsum("rf,rd->fd", act_low * once_low, d_output, preferred_element_type=F32).astype(BF)
    d_act = jnp.einsum("rd,fd->rf", d_output, w_out, preferred_element_type=F32)
    d_pre = (d_act * (half_erf + pre_act * jnp.exp(-0.5 * pre_act * pre_act) * GELU_DENSITY)).astype(BF)
    after_once = after_low * once_low
    g_hid = jnp.stack(
        [jnp.einsum("rd,rf->df", after_once, d_pre[:, q * width : (q + 1) * width], preferred_element_type=F32).astype(BF)
         for q in range(4)]
    )
    back_first = back_ffn + sum(
        jnp.einsum("rf,df->rd", d_pre[:, q * width : (q + 1) * width], w_hid[q], preferred_element_type=F32)
        for q in range(4)
    )
    back_attn = norm_back(back_first * ga, normed_attn, inverse_attn)
    d_branch = back_attn.astype(BF)
    d_context = jnp.einsum("re,de->rd", d_branch, qkvo[3], preferred_element_type=F32).astype(BF)
    dq, dkt, dvt = attention_back(query, keys, values, qseg, kseg, once, context, lse, d_context, scaling)
    g_qkvo = jnp.stack([
        jnp.einsum("rd,re->de", low_rows * once_low, dq, preferred_element_type=F32).astype(BF),
        jnp.einsum("rd,er->de", x_all, dkt, preferred_element_type=F32).astype(BF),
        jnp.einsum("rd,er->de", x_all, dvt, preferred_element_type=F32).astype(BF),
        jnp.einsum("rd,re->de", context_low * once_low, d_branch, preferred_element_type=F32).astype(BF),
    ])
    dx = jnp.einsum("er,de->rd", dkt, qkvo[1], preferred_element_type=F32) + jnp.einsum(
        "er,de->rd", dvt, qkvo[2], preferred_element_type=F32
    )
    base = back_attn + jnp.einsum("re,de->rd", dq, qkvo[0], preferred_element_type=F32)

    def over_rows(terms):
        return jnp.sum(once * terms, axis=0)

    gb_hidden = over_rows(d_pre.astype(F32)).reshape(shards, 4, srows).transpose(1, 0, 2).reshape(4, width)
    squares = jnp.stack([jnp.sum(v[:tok] * v[:tok]) for v in (result, branch, second)])
    vec_grads = jnp.concatenate([
        jnp.stack([
            over_rows(dq.astype(F32)),
            jnp.sum(dvt.astype(F32), axis=1),
            over_rows(d_branch.astype(F32)),
            over_rows(d_output.astype(F32)),
            over_rows(back_first * normed_attn),
            over_rows(back_first),
            over_rows(grads * normed_ffn),
            over_rows(grads),
        ]),
        gb_hidden,
        jnp.pad(squares[None], ((0, 3), (0, width - 3))),
    ])
    g_qkvo, g_hid, g_out, dx_own, dx_mem, vec_sum = reduce_plain(
        g_qkvo, g_hid, g_out, dx[:seq].astype(BF), dx[seq : seq + MEM_PAD], vec_grads
    )
    own = lax.dynamic_slice(vec_sum, (0, s * srows), (12, srows))
    rms = jnp.sqrt(vec_sum[12, :3] / float(seq * width * lax.axis_size("replica")))
    g_qkvo = g_qkvo.astype(F32)
    grad_hidden = jnp.concatenate([g_hid[q] for q in range(4)], axis=1).astype(F32)
    return (
        result[:tok],
        result[tok : tok + mem][None],
        base[:tok] + dx_own,
        (base[tok : tok + mem] + dx_mem[:mem])[None],
        g_qkvo[0],
        g_qkvo[1],
        g_qkvo[2],
        g_qkvo[3],
        grad_hidden,
        g_out.astype(F32),
        own[0],
        own[1],
        own[2],
        own[8:12].reshape(-1),
        own[3],
        own[4],
        own[5],
        own[6],
        own[7],
        rms[0],
        rms[1],
        rms[2],
    )


def direct_body(tokens, memory_rows, doc_lengths, w_query, w_key, w_value, w_attn_out, w_hidden, w_output,
                b_query, b_value, b_attn_out, b_hidden, b_output, gain_attn, shift_attn, gain_ffn, shift_ffn,
                out_grad, memory_grad):
    tok, width = tokens.shape
    mem = memory_rows.shape[1]
    shards = lax.axis_size("shard")
    s = lax.axis_index("shard")
    srows = w_query.shape[0]
    vec = jnp.concatenate(
        [b_query, b_value, b_attn_out, b_output, gain_attn, shift_attn, gain_ffn, shift_ffn]
        + [jnp.zeros((8 * srows,), BF)]
    ).reshape(16, srows)
    b_hid = jnp.broadcast_to(b_hidden.astype(F32)[None], (8, width))
    *saved, result, vec_full, squares = forward_all(
        w_query, w_key, w_value, w_attn_out, w_hidden, w_output, tokens, memory_rows[0], vec, b_hid, doc_lengths
    )
    g_qkvo, g_hid, g_out, grad_rows, vec_sum = backward_all(
        tuple(saved) + (vec_full, squares), out_grad, memory_grad[0], doc_lengths
    )
    own = lax.dynamic_slice(vec_sum, (0, s * srows), (8, srows))
    own_hid = lax.dynamic_slice(vec_sum, (8 + s, 0), (1, width))[0]
    count = float(tok * shards * width * lax.axis_size("replica"))
    rms = jnp.sqrt(jnp.sum(vec_sum[12:15], axis=1) / count)
    g_qkvo = g_qkvo.reshape(4, srows, width).astype(F32)
    g_hid = g_hid.reshape(4, srows, width)
    return (
        result[:tok],
        result[tok : tok + mem][None],
        grad_rows[:tok],
        grad_rows[tok : tok + mem][None],
        g_qkvo[0],
        g_qkvo[1],
        g_qkvo[2],
        g_qkvo[3],
        jnp.concatenate([g_hid[q] for q in range(4)], axis=1).astype(F32),
        g_out.reshape(4 * srows, width).astype(F32),
        own[0],
        own[1],
        own[2],
        own_hid,
        own[3],
        own[4],
        own[5],
        own[6],
        own[7],
        rms[0],
        rms[1],
        rms[2],
    )


def solution(mesh):
    direct = mesh.shape["replica"] == 8 and mesh.shape["shard"] == 4
    shard1, shard2 = P("shard"), P("shard", None)
    both, rep3 = P(("replica", "shard"), None), P("replica", None, None)
    return jax.shard_map(
        direct_body if direct else plain_body,
        mesh=mesh,
        in_specs=(both, rep3, P("replica", None)) + (shard2,) * 6 + (shard1,) * 9 + (both, rep3),
        out_specs=(both, rep3, both, rep3) + (shard2,) * 6 + (shard1,) * 9 + (P(), P(), P()),
        check_vma=False,
    )
```

```python
import functools
import math

import jax
import jax.numpy as jnp
from jax import lax
from jax.experimental import pallas as pl
from jax.experimental.pallas import tpu as pltpu
from jax.sharding import PartitionSpec as P

H = 12
HD = 64
EPSILON = 1e-12
GELU_ROOT = 0.7071067811865476
GELU_DENSITY = 0.3989422804014327
MESH = pl.DeviceIdType.MESH
BF = jnp.bfloat16
F32 = jnp.float32
MEM_PAD = 32
MEM_KEYS = 128
VMEM_LIMIT = 60 << 20
NEG = -1e30


def region(ref, group, sh, q0, nq, h0, nh, cols=None):
    hs = h0 if nh == 1 else pl.ds(h0, nh)
    qs = q0 if nq == 1 else pl.ds(q0, nq)
    tail = () if cols is None else (slice(None), cols)
    return ref.at[((sh, qs, hs) if group == 2 else (qs, sh, hs)) + tail]


def neighbours():
    r = lax.axis_index("replica")
    s = lax.axis_index("shard")
    core, xbit, ybit = r % 2, (r // 2) % 2, (r // 4) % 2
    return r, s, core, xbit, ybit, r + 1 - 2 * core, r + 2 - 4 * xbit, r + 4 - 8 * ybit


def entry_barrier(peers, r, s, shards):
    sem = pltpu.get_barrier_semaphore()
    for p in peers:
        pl.semaphore_signal(sem, 1, device_id=(p, s), device_id_type=MESH)
    for t in range(1, shards):
        pl.semaphore_signal(sem, 1, device_id=(r, lax.rem(s + t, shards)), device_id_type=MESH)
    pl.semaphore_wait(sem, len(peers) + shards - 1)


def remote(src, dst, ssem, rsem, dev):
    return pltpu.make_async_remote_copy(
        src_ref=src, dst_ref=dst, send_sem=ssem, recv_sem=rsem, device_id=dev, device_id_type=MESH
    )


def gather_plain(qkvo, hid, outw, xtok, vec):
    width = qkvo.shape[2]
    full = functools.partial(lax.all_gather, axis_name="shard", tiled=True)
    hid = full(hid, axis=0)
    return (
        full(qkvo, axis=1),
        jnp.stack([hid[:, q * width : (q + 1) * width] for q in range(4)]),
        full(outw, axis=0),
        full(xtok, axis=0),
        lax.all_gather(vec, "shard", axis=0),
    )


def reduce_plain(g_qkvo, g_hid, g_out, dx, mem, vec):
    scatter = functools.partial(lax.psum_scatter, axis_name="shard", tiled=True)
    return (
        lax.psum(scatter(g_qkvo, scatter_dimension=1), "replica"),
        lax.psum(scatter(g_hid, scatter_dimension=1), "replica"),
        lax.psum(scatter(g_out, scatter_dimension=0), "replica"),
        scatter(dx, scatter_dimension=0).astype(F32),
        lax.psum(mem, "shard"),
        lax.psum(vec, ("replica", "shard")),
    )


NT = (((1,), (1,)), ((), ()))
NN = (((1,), (0,)), ((), ()))
TN = (((0,), (0,)), ((), ()))


def dot(a, b, dims=NN):
    return lax.dot_general(a, b, dims, preferred_element_type=F32)


def head_lanes(shape, head):
    lane = lax.broadcasted_iota(jnp.int32, shape, 1)
    return (lane < HD) if head == 0 else (lane >= HD)


def mask_bias(qseg, kseg):
    allowed = (qseg == kseg) | (kseg == -1) | ((qseg == -2) & (kseg != -4))
    return jnp.where(allowed, 0.0, NEG)


def attend_kernel(scaling, q_ref, k_ref, v_ref, qseg_ref, kseg_ref, ctx_ref, lse_ref, bias_ref):
    @pl.when(pl.program_id(0) == 0)
    def _():
        bias_ref[...] = mask_bias(qseg_ref[...], kseg_ref[...])

    q, k, v = q_ref[...], k_ref[...], v_ref[...]
    zero_q = jnp.zeros_like(q)
    contexts, totals = [], []
    for head in range(2):
        qh = jnp.where(head_lanes(q.shape, head), q, zero_q)
        scores = dot(qh, k, NT) * scaling + bias_ref[...]
        top = jnp.max(scores, axis=1, keepdims=True)
        powers = jnp.exp(scores - top)
        lse = top + jnp.log(jnp.sum(powers, axis=1, keepdims=True))
        probs = powers * jnp.exp(top - lse)
        contexts.append(dot(probs.astype(BF), v))
        totals.append(lse)
    first = head_lanes(q.shape, 0)
    ctx_ref[...] = jnp.where(first, contexts[0], contexts[1])
    lse_ref[...] = jnp.where(first, totals[0], totals[1])


def attend_back_kernel(scaling, q_ref, k_ref, v_ref, qseg_ref, kseg_ref, weight_ref, ctx_ref, lse_ref, do_ref,
                       dq_ref, dk_ref, dv_ref, bias_ref):
    @pl.when(pl.program_id(0) == 0)
    def _():
        bias_ref[...] = mask_bias(qseg_ref[...], kseg_ref[...])

    q, k, v, do = q_ref[...], k_ref[...], v_ref[...], do_ref[...]
    weight = weight_ref[...] > 0
    dq, dk, dv = None, None, None
    for head in range(2):
        lanes = head_lanes(q.shape, head)
        qh = jnp.where(lanes, q, jnp.zeros_like(q))
        doh = jnp.where(lanes, do, jnp.zeros_like(do))
        lse = lse_ref[:, head * HD : head * HD + 1]
        scores = dot(qh, k, NT) * scaling + bias_ref[...]
        probs = jnp.exp(scores - lse)
        delta = jnp.sum(doh.astype(F32) * ctx_ref[...], axis=1, keepdims=True)
        d_scores = (probs * (dot(doh, v, NT) - delta)).astype(BF)
        kh = jnp.where(head_lanes(k.shape, head), k, jnp.zeros_like(k))
        part_q = dot(d_scores, kh)
        part_k = dot(jnp.where(weight, qh, jnp.zeros_like(qh)), d_scores, TN)
        part_v = dot(jnp.where(weight, doh, jnp.zeros_like(doh)), probs.astype(BF), TN)
        dq = part_q if dq is None else dq + part_q
        dk = part_k if dk is None else dk + part_k
        dv = part_v if dv is None else dv + part_v
    dq_ref[...] = (dq * scaling).astype(BF)
    dk_ref[...] = (dk * scaling).astype(BF)
    dv_ref[...] = dv.astype(BF)


def attention(query, keys, values, qseg, kseg, scaling):
    m, width = query.shape
    n = keys.shape[0]
    rows = pl.BlockSpec((m, 2 * HD), lambda i: (0, i))
    cols = pl.BlockSpec((n, 2 * HD), lambda i: (0, i))
    return pl.pallas_call(
        functools.partial(attend_kernel, scaling),
        grid=(width // (2 * HD),),
        out_shape=(jax.ShapeDtypeStruct((m, width), F32), jax.ShapeDtypeStruct((m, width), F32)),
        in_specs=[rows, cols, cols, pl.BlockSpec((m, 1), lambda i: (0, 0)), pl.BlockSpec((1, n), lambda i: (0, 0))],
        out_specs=[rows, rows],
        scratch_shapes=[pltpu.VMEM((m, n), F32)],
        compiler_params=pltpu.CompilerParams(vmem_limit_bytes=VMEM_LIMIT),
        name="attend",
    )(query, keys, values, qseg, kseg)


def attention_back(query, keys, values, qseg, kseg, weight, context, lse, d_context, scaling):
    m, width = query.shape
    n = keys.shape[0]
    rows = pl.BlockSpec((m, 2 * HD), lambda i: (0, i))
    cols = pl.BlockSpec((n, 2 * HD), lambda i: (0, i))
    turned = pl.BlockSpec((2 * HD, n), lambda i: (i, 0))
    column = pl.BlockSpec((m, 1), lambda i: (0, 0))
    return pl.pallas_call(
        functools.partial(attend_back_kernel, scaling),
        grid=(width // (2 * HD),),
        out_shape=(
            jax.ShapeDtypeStruct((m, width), BF),
            jax.ShapeDtypeStruct((width, n), BF),
            jax.ShapeDtypeStruct((width, n), BF),
        ),
        in_specs=[rows, cols, cols, column, pl.BlockSpec((1, n), lambda i: (0, 0)), column, rows, rows, rows],
        out_specs=[rows, turned, turned],
        scratch_shapes=[pltpu.VMEM((m, n), F32)],
        compiler_params=pltpu.CompilerParams(vmem_limit_bytes=VMEM_LIMIT),
        name="attend_back",
    )(query, keys, values, qseg, kseg, weight, context, lse, d_context)


def layer_stats(totals):
    center = totals - jnp.mean(totals, axis=-1, keepdims=True)
    spread = jnp.mean(center * center, axis=-1, keepdims=True)
    inverse = lax.rsqrt(spread + EPSILON)
    return (center * inverse, inverse)


def norm_back(grad_normed, normed, inverse):
    return inverse * (
        grad_normed
        - jnp.mean(grad_normed, axis=-1, keepdims=True)
        - normed * jnp.mean(grad_normed * normed, axis=-1, keepdims=True)
    )


LOG_ROWS = 32


def row_blocks(m, step=LOG_ROWS):
    return [pl.ds(i, step) for i in range(0, m, step)]


def matrix(ref, *lead, cols=None):
    value = ref[lead + (slice(None),) * 3 + ((slice(None),) if cols is None else (cols,))]
    return value.reshape(-1, value.shape[-1])


def full_vectors(vec_all, shards, srows, width):
    total = None
    for i in range(shards):
        row = lax.broadcasted_iota(jnp.int32, (srows, width), 0)
        col = lax.broadcasted_iota(jnp.int32, (srows, width), 1)
        place = jnp.where(col == row + i * srows, 1.0, 0.0).astype(BF)
        part = dot(vec_all[i], place)
        total = part if total is None else total + part
    return total


def segments(docs, ndoc, pos):
    end = docs[0, 0]
    seg = jnp.where(pos >= end, 1, 0)
    for i in range(1, ndoc):
        end = end + docs[0, i]
        seg = seg + jnp.where(pos >= end, 1, 0)
    return seg


def write_bias(bias, docs, ndoc, s, tok, seq, mem):
    m, n = bias.shape
    kpos = lax.broadcasted_iota(jnp.int32, (1, n), 1)
    place = kpos - seq
    kseg = jnp.where(kpos < seq, segments(docs, ndoc, kpos), jnp.where((place >= 0) & (place < mem // 2), -1, -3))
    for rows in row_blocks(tok):
        index = lax.broadcasted_iota(jnp.int32, (LOG_ROWS, 1), 0) + rows.start
        allowed = (segments(docs, ndoc, index + s * tok) == kseg) | (kseg == -1)
        bias[rows, :] = jnp.where(allowed, 0.0, NEG)
    if m > tok:
        own = (kpos >= s * tok) & (kpos < (s + 1) * tok)
        allowed = own | ((s == 0) & (place >= 0) & (place < mem))
        bias[pl.ds(tok, m - tok), :] = jnp.broadcast_to(jnp.where(allowed, 0.0, NEG), (m - tok, n))


def forward_kernel(shards, half, width, mem, ndoc,
                   wq, wk, wv, wo, hid, outw, tokens, memr, vec, bhid, docs,
                   o_qkvo, o_hid, o_out, o_x, o_q, o_k, o_v, o_ctx, o_lse, o_na, o_ia, o_al, o_act, o_slope, o_nf, o_if,
                   o_res, o_vec, o_sq,
                   w_qkvo, w_hid, w_out, x_all, vec_all, bh_all, rows, q_s, k_s, v_s, s_s, p_s, bias, inv_s, ctx, ctx_low, lse,
                   branch, na, ia, after, al, act, slope, second, nf, if_, res, vfull, sq, mctx, mlse,
                   zs, zr, hsem, hrem, xs, xr, vs, vr, hs, hr, ms, mr, es, er, ls, os_):
    r, s, core, xbit, ybit, fc, fx, fy = neighbours()
    q_own, q_lo = 2 * core + ybit, 2 * core
    bufs = (w_qkvo, w_hid, w_out)
    tok = tokens.shape[0]
    m, n = rows.shape[0], x_all.shape[0]
    seq = tok * shards
    reach = shards // 2

    local = [pltpu.make_async_copy(w, w_qkvo.at[i, s], ls.at[i]) for i, w in enumerate((wq, wk, wv, wo))]
    local.append(pltpu.make_async_copy(tokens, rows.at[pl.ds(0, tok), :], ls.at[4]))
    late = [pltpu.make_async_copy(hid.at[:, :, pl.ds(q * width, width)], w_hid.at[q, s], ls.at[5 + q]) for q in range(4)]
    late.append(pltpu.make_async_copy(outw, w_out.at[s], ls.at[9]))
    for c in local + late:
        c.start()
    entry_barrier((fc, fx, fy), r, s, shards)

    def reg(g, sh, q0, nq, h0, nh):
        return region(bufs[g], g, sh, q0, nq, h0, nh)

    def block(i):
        return x_all.at[pl.ds(pl.multiple_of(i * tok, tok), tok), :]

    def rows_copy(sh, k):
        return remote(block(sh), block(sh), xs.at[k, sh], xr.at[sh], (r, s + 1 if k == 0 else s - 1))

    def on_line(k, fn):
        pl.when(s + 1 < shards if k == 0 else s > 0)(fn)

    sends = []
    side = width // 2
    left_cols, right_cols = pl.ds(0, side), pl.ds(side, side)

    def piece_copy(g, sh, k):
        a = reg(g, sh, q_own, 1, xbit, 1)
        return remote(a, a, zs.at[g, k, sh], zr.at[g, sh], (r, s + 1 if k == 0 else s - 1))

    def push(g):
        for k in range(2):
            on_line(k, lambda k=k: piece_copy(g, s, k).start())

    def hop(g, sh, k):
        if k == 0:
            moves = ((q_own, 1, xbit, 1, left_cols, fx), (q_own, 1, xbit, 1, right_cols, fy))
        elif k == 1:
            moves = ((q_own, 1, 0, 2, left_cols, fy), (q_lo, 2, xbit, 1, right_cols, fx))
        else:
            moves = ((q_lo, 2, 0, 2, None, fc),)
        out = []
        for i, (q0, nq, h0, nh, cols, dev) in enumerate(moves):
            a = region(bufs[g], g, sh, q0, nq, h0, nh, cols)
            out.append(remote(a, a, hsem.at[g, k, i, sh], hrem.at[g, k, i, sh], (dev, s)))
        return out

    def each_foreign(fn, g, t):
        for left in (True, False):
            sh = s - t if left else s + t
            pl.when(s >= t if left else s + t < shards)(functools.partial(fn, g, left, sh))

    def relay_rows(last, g, left, sh):
        rows_copy(sh, 0).wait_recv()
        if not last:
            k = 0 if left else 1
            on_line(k, lambda: rows_copy(sh, k).start())

    def far_block(g, left, sh):
        at = pl.ds(pl.multiple_of(sh * tok, tok), tok)
        x_all[at, :] = jnp.zeros((tok, width), BF)
        k_s[:, at, :] = jnp.zeros((width // 128, tok, 128), BF)
        v_s[:, at, :] = jnp.zeros((width // 128, tok, 128), BF)

    def rows_in(t):
        if t <= reach:
            each_foreign(functools.partial(relay_rows, t == reach), 0, t)

    def stage0(g, left, sh):
        piece_copy(g, sh, 0).wait_recv()
        k = 0 if left else 1
        on_line(k, lambda: piece_copy(g, sh, k).start())
        for c in hop(g, sh, 0):
            c.start()

    def advance(k, g, left, sh):
        for c in hop(g, sh, k - 1):
            c.wait_recv()
        for c in hop(g, sh, k):
            c.start()

    stage1, stage2 = functools.partial(advance, 1), functools.partial(advance, 2)

    def stage3(g, left, sh):
        hop(g, sh, 2)[0].wait_recv()

    def finish(g, left, sh):
        for k in range(3):
            for c in hop(g, sh, k):
                c.wait_send()
        k = 0 if left else 1

        on_line(k, lambda: piece_copy(g, sh, k).wait_send())

    def finish_rows(g, left, sh):
        k = 0 if left else 1
        on_line(k, lambda: rows_copy(sh, k).wait_send())

    def run(stage, g):
        for t in range(1, shards):
            each_foreign(stage, g, t)

    saves = []

    def save(src, dst):
        saves.append(pltpu.make_async_copy(src, dst, os_.at[len(saves)]))
        saves[-1].start()

    for c in local[:4]:
        c.wait()
    push(0)
    local[4].wait()
    rows[pl.ds(tok, mem), :] = memr[...]
    rows[pl.ds(tok + mem, MEM_PAD - mem), :] = jnp.zeros((MEM_PAD - mem, width), F32)
    block(s)[...] = rows[pl.ds(0, tok), :].astype(BF)
    x_all[pl.ds(seq, MEM_PAD), :] = rows[pl.ds(tok, MEM_PAD), :].astype(BF)
    x_all[pl.ds(seq + MEM_PAD, MEM_KEYS - MEM_PAD), :] = jnp.zeros((MEM_KEYS - MEM_PAD, width), BF)
    for t in range(reach + 1, shards):
        each_foreign(far_block, 0, t)
    for k in range(2):
        on_line(k, lambda k=k: rows_copy(s, k).start())
    vec_all[s] = vec[...]
    bh_all[s] = bhid[...]
    for t in range(1, shards):
        dev = (r, lax.rem(s + t, shards))
        sends.append(remote(vec_all.at[s], vec_all.at[s], vs.at[t], vr.at[s], dev))
        sends[-1].start()
        sends.append(remote(bh_all.at[s], bh_all.at[s], hs.at[t], hr.at[s], dev))
        sends[-1].start()
    write_bias(bias, docs, ndoc, s, tok, seq, mem)
    for c in late:
        c.wait()
    each_foreign(stage0, 0, 1)
    rows_in(1)
    each_foreign(stage0, 0, 2)
    push(1)
    each_foreign(stage1, 0, 1)
    for t in range(3, shards):
        each_foreign(stage0, 0, t)
    each_foreign(stage1, 0, 2)
    each_foreign(stage2, 0, 1)
    rows_in(2)
    for t in range(3, shards):
        each_foreign(stage1, 0, t)
    for t in range(2, shards):
        each_foreign(stage2, 0, t)
    each_foreign(stage0, 1, 1)
    push(2)
    for t in range(1, shards):
        other = lax.rem(s + t, shards)
        remote(vec_all.at[other], vec_all.at[other], vs.at[t], vr.at[other], (r, other)).wait_recv()
        remote(bh_all.at[other], bh_all.at[other], hs.at[t], hr.at[other], (r, other)).wait_recv()
    vfull[...] = full_vectors(vec_all, shards, 2 * half, width)
    each_foreign(stage0, 1, 2)
    run(stage3, 0)
    save(w_qkvo, o_qkvo)
    save(vfull, o_vec)

    def vrow(i):
        return vfull[pl.ds(i, 1), :]

    def bias_cols(i, c):
        return vfull[pl.ds(i, 1), c]

    def keys_values(start, size):
        at = pl.ds(start, size)

        @pl.loop(0, width // 256)
        def _(ct):
            c = pl.ds(pl.multiple_of(ct * 256, 256), 256)
            xb = x_all[at, :]
            y = dot(xb, matrix(w_qkvo, 1, cols=c)).astype(BF)
            k_s[2 * ct, at] = y[:, :128]
            k_s[2 * ct + 1, at] = y[:, 128:]
            y = (dot(xb, matrix(w_qkvo, 2, cols=c)) + bias_cols(1, c)).astype(BF)
            v_s[2 * ct, at] = y[:, :128]
            v_s[2 * ct + 1, at] = y[:, 128:]

    @pl.loop(0, width // 256)
    def _(ct):
        c = pl.ds(pl.multiple_of(ct * 256, 256), 256)
        wt = matrix(w_qkvo, 0, cols=c)
        b = bias_cols(0, c)
        for part, at, size in ((block(s)[...], 0, tok), (x_all[pl.ds(seq, MEM_PAD), :], tok, MEM_PAD)):
            y = (dot(part, wt) + b).astype(BF) * jnp.asarray(0.125, BF)
            q_s[2 * ct, pl.ds(at, size)] = y[:, :128]
            q_s[2 * ct + 1, pl.ds(at, size)] = y[:, 128:]

    own_at = pl.multiple_of(s * tok, tok)
    keys_values(own_at, tok)
    keys_values(seq, MEM_KEYS)
    save(q_s, o_q)
    lane = lax.broadcasted_iota(jnp.int32, (tok, 128), 1)
    lane_m = lane[:MEM_PAD]
    mrows = pl.ds(tok, MEM_PAD)

    def memory_pair(p):
        seen = jnp.concatenate([bias[mrows, pl.ds(own_at, tok)], bias[mrows, pl.ds(seq, MEM_KEYS)]], axis=1)
        kk = jnp.concatenate([k_s[p, pl.ds(own_at, tok)], k_s[p, pl.ds(seq, MEM_KEYS)]])
        vv = jnp.concatenate([v_s[p, pl.ds(own_at, tok)], v_s[p, pl.ds(seq, MEM_KEYS)]])
        q = q_s[p, mrows]
        outs = []
        for head in range(2):
            sc = dot(jnp.where((lane_m < HD) == (head == 0), q, jnp.zeros_like(q)), kk, NT) + seen
            top = jnp.max(sc, axis=1, keepdims=True)
            e = jnp.exp(sc - top)
            tot = jnp.sum(e, axis=1, keepdims=True)
            outs.append(dot(e.astype(BF), vv) / tot)
            mlse[s] = jnp.where(lane_m == 2 * p + head, top + jnp.log(tot), mlse[s])
        mctx[s, :, pl.ds(pl.multiple_of(p * 128, 128), 128)] = jnp.where(lane_m < HD, outs[0], outs[1]).astype(BF)

    mlse[s] = jnp.zeros((MEM_PAD, 128), F32)
    pl.loop(0, width // 128)(memory_pair)
    for t in range(1, shards):
        dev = (r, lax.rem(s + t, shards))
        for buf, ssem, rsem in ((mctx, ms, mr), (mlse, es, er)):
            sends.append(remote(buf.at[s], buf.at[s], ssem.at[t], rsem.at[s], dev))
            sends[-1].start()
    for t in range(3, shards):
        each_foreign(stage0, 1, t)
    each_foreign(stage1, 1, 1)
    each_foreign(stage0, 2, 1)
    for t in range(1, reach + 1):
        each_foreign(lambda g, left, sh: keys_values(pl.multiple_of(sh * tok, tok), tok), 0, t)
    each_foreign(stage1, 1, 2)
    each_foreign(stage2, 1, 1)
    each_foreign(stage0, 2, 2)
    save(x_all, o_x)
    save(k_s, o_k)
    save(v_s, o_v)

    def pair(p):
        outs = []
        for head in range(2):
            q = q_s[p, pl.ds(0, tok)]
            s_s[pl.ds(0, tok), :] = dot(jnp.where((lane < HD) == (head == 0), q, jnp.zeros_like(q)), k_s[p], NT)
            for rb in row_blocks(tok):
                sc = s_s[rb, :] + bias[rb, :]
                top = jnp.max(sc, axis=1, keepdims=True)
                e = jnp.exp(sc - top)
                tot = jnp.sum(e, axis=1, keepdims=True)
                p_s[rb, :] = e.astype(BF)
                wide = jnp.broadcast_to(top + jnp.log(tot), (LOG_ROWS, 128))
                inv = jnp.broadcast_to(1.0 / tot, (LOG_ROWS, 128))
                if head == 0:
                    lse[p, rb] = wide
                    inv_s[rb, :] = inv
                else:
                    right = lane[:LOG_ROWS] >= HD
                    lse[p, rb] = jnp.where(right, wide, lse[p, rb])
                    inv_s[rb, :] = jnp.where(right, inv, inv_s[rb, :])
            outs.append(dot(p_s[...], v_s[p]))
        value = jnp.where(lane < HD, outs[0], outs[1]) * inv_s[...]
        c = pl.ds(pl.multiple_of(p * 128, 128), 128)
        ctx[pl.ds(0, tok), c] = value
        ctx_low[pl.ds(0, tok), c] = value.astype(BF)

    pl.loop(0, 1)(pair)
    for t in range(3, shards):
        each_foreign(stage1, 1, t)
        each_foreign(stage0, 2, t)
    each_foreign(stage2, 1, 2)
    each_foreign(stage1, 2, 1)
    pl.loop(1, 3)(pair)
    for t in range(3, shards):
        each_foreign(stage2, 1, t)
    each_foreign(stage1, 2, 2)
    each_foreign(stage2, 2, 1)
    pl.loop(3, 5)(pair)
    for t in range(3, shards):
        each_foreign(stage1, 2, t)
    each_foreign(stage2, 2, 2)
    pl.loop(5, width // 128)(pair)

    for t in range(1, shards):
        other = lax.rem(s + t, shards)
        remote(mctx.at[other], mctx.at[other], ms.at[t], mr.at[other], (r, other)).wait_recv()
        remote(mlse.at[other], mlse.at[other], es.at[t], er.at[other], (r, other)).wait_recv()
    top = mlse[0]
    for i in range(1, shards):
        top = jnp.maximum(top, mlse[i])
    tot = sum(jnp.exp(mlse[i] - top) for i in range(shards))
    whole = top + jnp.log(tot)
    shares = [jnp.exp(mlse[i] - whole) for i in range(shards)]

    def spread(v, p):
        return jnp.where(lane_m < HD, v[:, 2 * p : 2 * p + 1], v[:, 2 * p + 1 : 2 * p + 2])

    for p in range(width // 128):
        c = pl.ds(p * 128, 128)
        value = sum(spread(shares[i], p) * mctx[i, :, c].astype(F32) for i in range(shards))
        ctx[mrows, c] = value
        ctx_low[mrows, c] = value.astype(BF)
        lse[p, mrows] = spread(whole, p)
    save(ctx, o_ctx)
    save(lse, o_lse)

    def stats(totals):
        center = totals - jnp.mean(totals, axis=1, keepdims=True)
        spread = jnp.mean(center * center, axis=1, keepdims=True)
        inverse = lax.rsqrt(spread + EPSILON)
        return center * inverse, inverse

    @pl.loop(0, width // 256)
    def _(ct):
        c = pl.ds(pl.multiple_of(ct * 256, 256), 256)
        branch[:, c] = dot(ctx_low[...], matrix(w_qkvo, 3, cols=c)) + bias_cols(2, c)

    sq[...] = jnp.zeros_like(sq)

    def add_square(i, rb, value):
        if rb.start < tok:
            total = jnp.sum(value * value, axis=0, keepdims=True)
            sq[pl.ds(i, 1), :] = sq[pl.ds(i, 1), :] + total

    for rb in row_blocks(m):
        b = branch[rb, :]
        add_square(1, rb, b)
        normed, inverse = stats(rows[rb, :] + b)
        na[rb, :] = normed
        ia[rb, :] = jnp.broadcast_to(inverse, (LOG_ROWS, 128))
        y = normed * vrow(4) + vrow(5)
        after[rb, :] = y
        al[rb, :] = y.astype(BF)
    save(na, o_na)
    save(ia, o_ia)
    save(al, o_al)
    for k in range(3, shards):
        each_foreign(stage2, 2, k)
    run(stage3, 1)
    save(w_hid, o_hid)

    @pl.loop(0, 4)
    def _(q):
        @pl.loop(0, width // 256)
        def _(ct):
            c = pl.ds(pl.multiple_of(ct * 256, 256), 256)
            s_s[:, :256] = dot(al[...], matrix(w_hid, q, cols=c))
            b = bh_all[q, pl.ds(0, 1), c]
            for rb in row_blocks(m):
                z = s_s[rb, :256] + b
                he = 0.5 * (1.0 + lax.erf(z * GELU_ROOT))
                act[q, rb, c] = (z * he).astype(BF)
                slope[q, rb, c] = he + z * jnp.exp(-0.5 * z * z) * GELU_DENSITY

    save(act, o_act)
    save(slope, o_slope)
    run(stage3, 2)
    save(w_out, o_out)

    @pl.loop(0, width // 256)
    def _(ct):
        c = pl.ds(pl.multiple_of(ct * 256, 256), 256)
        total = dot(act[0], matrix(w_out, 0, cols=c))
        for q in range(1, 4):
            total = total + dot(act[q], matrix(w_out, q, cols=c))
        second[:, c] = total + bias_cols(3, c)

    for rb in row_blocks(m):
        b = second[rb, :]
        add_square(2, rb, b)
        normed, inverse = stats(after[rb, :] + b)
        nf[rb, :] = normed
        if_[rb, :] = jnp.broadcast_to(inverse, (LOG_ROWS, 128))
        y = normed * vrow(6) + vrow(7)
        add_square(0, rb, y)
        res[rb, :] = y
    save(nf, o_nf)
    save(if_, o_if)
    save(res, o_res)
    save(sq, o_sq)
    for g in range(3):
        run(finish, g)
    for t in range(1, reach):
        each_foreign(finish_rows, 0, t)
    for c in sends:
        c.wait_send()
    for k in range(2):
        on_line(k, lambda k=k: rows_copy(s, k).wait_send())
        for g in range(3):
            on_line(k, lambda g=g, k=k: piece_copy(g, s, k).wait_send())
    for c in saves:
        c.wait()


def forward_all(wq, wk, wv, wo, hid, outw, tokens, memr, vec, bhid, docs):
    shards = lax.axis_size("shard")
    half, width = wq.shape[0] // 2, wq.shape[1]
    tok, mem = tokens.shape[0], memr.shape[0]
    m, n = tok + MEM_PAD, tok * shards + MEM_KEYS
    pairs = width // 128
    stack = (4, shards, 2, half, width)
    any_space = pl.BlockSpec(memory_space=pl.ANY)
    vm = pl.BlockSpec(memory_space=pltpu.VMEM)
    dma = pltpu.SemaphoreType.DMA

    def sd(shape, dtype):
        return jax.ShapeDtypeStruct(shape, dtype)

    outs = (
        sd(stack, BF), sd(stack, BF), sd((shards, 4, 2, half, width), BF), sd((n, width), BF),
        sd((pairs, m, 128), BF), sd((pairs, n, 128), BF), sd((pairs, n, 128), BF),
        sd((m, width), F32), sd((pairs, m, 128), F32), sd((m, width), F32), sd((m, 128), F32), sd((m, width), BF),
        sd((4, m, width), BF), sd((4, m, width), F32), sd((m, width), F32), sd((m, 128), F32), sd((m, width), F32),
        sd((16, width), F32), sd((8, width), F32),
    )
    V = pltpu.VMEM
    scratch = [
        V(stack, BF), V(stack, BF), V((shards, 4, 2, half, width), BF), V((n, width), BF), V((shards,) + vec.shape, BF), V((shards, 8, width), F32),
        V((m, width), F32), V((pairs, m, 128), BF), V((pairs, n, 128), BF), V((pairs, n, 128), BF), V((m, n), F32),
        V((tok, n), BF), V((m, n), F32), V((tok, 128), F32), V((m, width), F32), V((m, width), BF), V((pairs, m, 128), F32),
        V((m, width), F32), V((m, width), F32), V((m, 128), F32), V((m, width), F32), V((m, width), BF),
        V((4, m, width), BF), V((4, m, width), F32), V((m, width), F32), V((m, width), F32), V((m, 128), F32),
        V((m, width), F32), V((16, width), F32), V((8, width), F32),
        V((shards, MEM_PAD, width), BF), V((shards, MEM_PAD, 128), F32),
    ]
    return pl.pallas_call(
        functools.partial(forward_kernel, shards, half, width, mem, docs.shape[1]),
        out_shape=outs,
        in_specs=[any_space] * 7 + [vm, vm, vm, pl.BlockSpec(memory_space=pltpu.SMEM)],
        out_specs=[any_space] * len(outs),
        scratch_shapes=scratch
        + [dma((3, 2, shards)), dma((3, shards)), dma((3, 3, 2, shards)), dma((3, 3, 2, shards)), dma((2, shards))] + [dma((shards,))] * 9 + [dma((10,)), dma((len(outs),))],
        compiler_params=pltpu.CompilerParams(collective_id=3, has_side_effects=True, vmem_limit_bytes=VMEM_LIMIT),
        name="forward_layer",
    )(
        wq.reshape(2, half, width), wk.reshape(2, half, width), wv.reshape(2, half, width), wo.reshape(2, half, width),
        hid.reshape(2, half, 4 * width), outw.reshape(4, 2, half, width), tokens, memr, vec, bhid, docs,
    )


def backward_kernel(shards, half, width, mem,
                    h_qkvo, h_hid, h_out, h_x, h_q, h_k, h_v, h_ctx, h_lse, h_na, h_ia, h_al, h_act, h_slope, h_nf, h_if,
                    vfull, sq, out_grad, mem_grad, docs,
                    o_qkvo, o_hid, o_out, o_x, o_vec,
                    grad, ra, rb, rc, rd, rx, relay, rm, rv, vz, vacc,
                    wbuf, x_all, pq, pk, pv, pctx, plse, bias, s_s, dp_s, p_s, ds_s, al, abuf, sbuf, d_pre, nf, if_,
                    gr, d_out, back, d_branch, dctx, dq, dkt, dvt,
                    asem, arem, bsem, brem, csem, crem, zsem, zrem, dsem, drem, xsem, xrem, msem, mrem, vsem, vrem,
                    vzs, vzr, fsem, wsem, psem, asem_, lsem, osem):
    r, s, core, xbit, ybit, fc, fx, fy = neighbours()
    q_own, q_lo = 2 * core + ybit, 2 * core
    tok = out_grad.shape[0]
    m, n = gr.shape[0], x_all.shape[0]
    seq = tok * shards
    pairs = width // 128
    outs = (o_qkvo, o_hid, o_out)
    groups = (2, 1, 0)
    units = 3 * shards

    def load(src, dst, i):
        c = pltpu.make_async_copy(src, dst, lsem.at[i])
        c.start()
        return c

    def w_copy(j):
        if j < 8:
            src = (h_out if j % 2 == 0 else h_hid).at[j // 2]
        else:
            src = h_qkvo.at[(3, 1, 2, 0)[j - 8]]
        return pltpu.make_async_copy(src, wbuf.at[j % 4], wsem.at[j])

    def a_copy(q):
        return (
            pltpu.make_async_copy(h_act.at[q], abuf.at[q % 2], asem_.at[0, q]),
            pltpu.make_async_copy(h_slope.at[q], sbuf.at[q % 2], asem_.at[1, q]),
        )

    def p_copy(p, slot):
        return [
            pltpu.make_async_copy(a.at[p], b.at[slot], psem.at[i, slot])
            for i, (a, b) in enumerate(((h_q, pq), (h_k, pk), (h_v, pv), (h_lse, plse)))
        ]

    first = [load(h_nf, nf, 0), load(out_grad, gr.at[pl.ds(0, tok), :], 1), load(h_if, if_, 2)]
    for j in range(3):
        w_copy(j).start()
    for c in a_copy(0):
        c.start()
    second = [load(h_al, al, 3), load(h_x, x_all, 6), load(h_ctx, pctx, 7)]
    entry_barrier((fc, fx, fy), r, s, shards)

    def unit_shard(u):
        return lax.rem(u, shards)

    def copy_a(u):
        return remote(grad.at[u, 1 - core], ra.at[u], asem.at[u], arem.at[u], (fc, s))

    side = width // 2
    left_cols, right_cols = pl.ds(0, side), pl.ds(side, side)

    def copy_b(u):
        return (
            remote(grad.at[u, core, :, 1 - xbit, :, left_cols], rb.at[u, 0], bsem.at[u, 0], brem.at[u, 0], (fx, s)),
            remote(grad.at[u, core, 1 - ybit, :, :, right_cols], rb.at[u, 1], bsem.at[u, 1], brem.at[u, 1], (fy, s)),
        )

    def copy_c(u):
        return (
            remote(grad.at[u, core, 1 - ybit, xbit, :, left_cols], rc.at[u, 0], csem.at[u, 0], crem.at[u, 0], (fy, s)),
            remote(grad.at[u, core, ybit, 1 - xbit, :, right_cols], rc.at[u, 1], csem.at[u, 1], crem.at[u, 1], (fx, s)),
        )

    def copy_z(u):
        return remote(
            grad.at[u, core, ybit, xbit], rd.at[u // shards, s], zsem.at[u], zrem.at[u // shards, s], (r, unit_shard(u))
        )

    def start_b(u):
        copy_a(u).wait_recv()
        grad[u, core] = grad[u, core] + ra[u]
        for c in copy_b(u):
            c.start()

    def start_c(u):
        for c in copy_b(u):
            c.wait_recv()
        grad[u, core, :, xbit, :, left_cols] = grad[u, core, :, xbit, :, left_cols] + rb[u, 0]
        grad[u, core, ybit, :, :, right_cols] = grad[u, core, ybit, :, :, right_cols] + rb[u, 1]
        for c in copy_c(u):
            c.start()

    def start_z(u):
        for c in copy_c(u):
            c.wait_recv()
        grad[u, core, ybit, xbit, :, left_cols] = grad[u, core, ybit, xbit, :, left_cols] + rc[u, 0]
        grad[u, core, ybit, xbit, :, right_cols] = grad[u, core, ybit, xbit, :, right_cols] + rc[u, 1]
        pl.when(s != unit_shard(u))(lambda: copy_z(u).start())

    def hop(k, j):
        o = outs[groups[k]]
        if j == 0:
            moves = ((o.at[q_own, xbit, :, left_cols], fx), (o.at[q_own, xbit, :, right_cols], fy))
        elif j == 1:
            moves = ((o.at[q_own, :, :, left_cols], fy), (o.at[pl.ds(q_lo, 2), xbit, :, right_cols], fx))
        else:
            moves = ((o.at[pl.ds(q_lo, 2)], fc),)
        return [remote(a, a, dsem.at[k, j, i], drem.at[k, j, i], (dev, s)) for i, (a, dev) in enumerate(moves)]

    def hop_start(k, j):
        for c in hop(k, j):
            c.start()

    def hop_wait(k, j):
        for c in hop(k, j):
            c.wait_recv()

    def finish_group(k):
        total = grad[k * shards + s, core, ybit, xbit].astype(F32)
        for t in range(1, shards):
            other = lax.rem(s + t, shards)
            slot = rd.at[k, other]
            remote(slot, slot, zsem.at[0], zrem.at[k, other], (r, s)).wait_recv()
            total = total + rd[k, other].astype(F32)
        fin = ra.at[k * shards, 0, 0]
        fin[...] = total.astype(BF)
        c = pltpu.make_async_copy(fin, outs[groups[k]].at[q_own, xbit], fsem.at[k])
        c.start()
        c.wait()
        hop_start(k, 0)

    def hop_step(k, j):
        hop_wait(k, j - 1)
        hop_start(k, j)

    lag = 2
    ticks = units + 2 * lag + 1 + 2 * lag

    def tick(i):
        def guarded(lo, fn):
            pl.when((i >= lo) & (i < lo + units))(lambda: fn(i - lo))

        guarded(0, start_b)
        guarded(lag, start_c)
        guarded(2 * lag, start_z)
        for k in range(3):
            when = shards * (k + 1) + 2 * lag
            pl.when(i == when)(functools.partial(finish_group, k))
            for j in (1, 2):
                pl.when(i == when + j * lag)(functools.partial(hop_step, k, j))

    def vrow(i):
        return vfull[pl.ds(i, 1), :]

    index = lax.broadcasted_iota(jnp.int32, (m, 1), 0)
    once = jnp.where((index < tok) | ((index < tok + mem) & (s == 0)), 1.0, 0.0)

    def add_sum(i, rw, value):
        total = jnp.sum(value * once[rw.start : rw.start + LOG_ROWS], axis=0, keepdims=True)
        vacc[0, pl.ds(i, 1), :] = vacc[0, pl.ds(i, 1), :] + total

    def mean(v):
        return jnp.mean(v, axis=1, keepdims=True)

    def norm_back_rows(e, normed, inverse):
        return inverse * (e - mean(e) - normed * mean(e * normed))

    vacc[0] = jnp.zeros(vacc.shape[1:], F32)
    for c in first:
        c.wait()
    gr[pl.ds(tok, mem), :] = mem_grad[...]
    gr[pl.ds(tok + mem, MEM_PAD - mem), :] = jnp.zeros((MEM_PAD - mem, width), F32)
    for rw in row_blocks(m):
        g, normed = gr[rw, :], nf[rw, :]
        add_sum(6, rw, g * normed)
        add_sum(7, rw, g)
        v = norm_back_rows(g * vrow(6), normed, if_[rw, :1])
        back[rw, :] = v
        low = v.astype(BF)
        add_sum(3, rw, low.astype(F32))
        d_out[rw, :] = low
    na, ia = nf, if_
    second += [load(h_na, na, 4), load(h_ia, ia, 5)]
    second[0].wait()
    once_low = once.astype(BF)

    def turned(a, b):
        return dot(a, b, TN)

    def put(k, q, j, value):
        grad[pl.ds(k * shards + 2 * j, 2), q // 2, q % 2] = value.astype(BF).reshape(2, 2, half, width)

    wide = 2 * 2 * half
    for q in range(4):
        for c in a_copy(q):
            c.wait()
        if q + 1 < 4:
            for c in a_copy(q + 1):
                c.start()
        w_copy(2 * q).wait()
        w_copy(2 * q + 3).start()
        a = abuf.at[q % 2]
        do = d_out[...] * once_low
        for j in range(2):
            value = turned(a[:, j * wide : (j + 1) * wide], do)
            grad[q, j] = value.astype(BF).reshape(2, 2, half, width)
        copy_a(q).start()
        for j in range(2):
            wt = wbuf[(2 * q) % 4, 2 * j : 2 * j + 2].reshape(wide, width)
            s_s[:, j * wide : (j + 1) * wide] = dot(d_out[...], wt, NT)
        for rw in row_blocks(m):
            v = s_s[rw, :width] * sbuf[q % 2, rw, :]
            low = v.astype(BF)
            d_pre[rw, :] = low
            add_sum(8 + q, rw, low.astype(F32))
        if q == 1:
            tick(jnp.int32(0))
        w_copy(2 * q + 1).wait()
        w_copy(2 * q + 4).start()
        dp = d_pre[...] * once_low
        for j in range(2):
            put(1, q, j, turned(al[:, j * wide : (j + 1) * wide], dp))
        for j in range(2):
            wt = wbuf[(2 * q + 1) % 4, 2 * j : 2 * j + 2].reshape(wide, width)
            c = pl.ds(j * wide, wide)
            s_s[:, c] = dot(d_pre[...], wt, NT)
        for rw in row_blocks(m):
            back[rw, :] = back[rw, :] + s_s[rw, :width]
    for j in range(shards):
        copy_a(shards + j).start()
    tick(jnp.int32(1))
    for c in p_copy(0, 0):
        c.start()

    for c in second[1:]:
        c.wait()

    for rw in row_blocks(m):
        f, normed = back[rw, :], na[rw, :]
        add_sum(4, rw, f * normed)
        add_sum(5, rw, f)
        v = norm_back_rows(f * vrow(4), normed, ia[rw, :1])
        back[rw, :] = v
        low = v.astype(BF)
        d_branch[rw, :] = low
        add_sum(2, rw, low.astype(F32))
        d_out[rw, :] = pctx[rw, :].astype(BF)
    write_bias(bias, docs, docs.shape[1], s, tok, seq, mem)
    w_copy(8).wait()
    w_copy(11).start()
    db = d_branch[...] * once_low
    for j in range(2):
        put(2, 3, j, turned(d_out[:, j * wide : (j + 1) * wide], db))
    for j in range(2):
        wt = wbuf[0, 2 * j : 2 * j + 2].reshape(wide, width)
        value = dot(d_branch[...], wt, NT).astype(BF)
        for i in range(wide // 128):
            dctx[j * (wide // 128) + i] = value[:, i * 128 : (i + 1) * 128]
    lane = lax.broadcasted_iota(jnp.int32, (m, 128), 1)
    lane_k = lax.broadcasted_iota(jnp.int32, (n, 128), 1)
    tick(jnp.int32(2))

    def pair(p):
        slot = lax.rem(p, 2)
        for c in p_copy(p, slot):
            c.wait()

        @pl.when(p + 1 < pairs)
        def _():
            for c in p_copy(p + 1, 1 - slot):
                c.start()

        c = pl.ds(pl.multiple_of(p * 128, 128), 128)
        part_q, part_k, part_v = None, None, None
        zero = jnp.zeros((m, 128), BF)
        for head in range(2):
            mine = (lane < HD) == (head == 0)
            qh = jnp.where(mine, pq[slot], zero)
            doh = jnp.where(mine, dctx[p], zero)
            s_s[...] = dot(qh, pk[slot], NT)
            dp_s[...] = dot(doh, pv[slot], NT)
            for rw in row_blocks(m):
                sub = slice(rw.start, rw.start + LOG_ROWS)
                delta = jnp.sum(doh[sub].astype(F32) * pctx[rw, c], axis=1, keepdims=True)
                top = plse[slot, rw, head * HD : head * HD + 1]
                probs = jnp.exp(s_s[rw, :] + bias[rw, :] - top)
                p_s[rw, :] = probs.astype(BF)
                ds_s[rw, :] = (probs * (dp_s[rw, :] - delta)).astype(BF)
            kh = jnp.where((lane_k < HD) == (head == 0), pk[slot], jnp.zeros((n, 128), BF))
            a = dot(ds_s[...], kh)
            b = turned(qh, ds_s[...])
            d = turned(doh, p_s[...])
            part_q = a if head == 0 else part_q + a
            part_k = b if head == 0 else part_k + b
            part_v = d if head == 0 else part_v + d
        dq[:, c] = (part_q * 0.125).astype(BF)
        dkt[c, :] = part_k.astype(BF)
        dvt[c, :] = part_v.astype(BF)
        pl.when(lax.rem(p, 2) == 1)(lambda: tick(3 + p // 2))

    pl.loop(0, pairs)(pair)

    ones = jnp.ones((8, n), BF)
    vacc[0, pl.ds(1, 1), :] = dot(ones, dvt[...], NT)[:1]
    vacc[0, pl.ds(0, 1), :] = jnp.sum(dq[...].astype(F32), axis=0, keepdims=True)
    vacc[0, pl.ds(12, 3), :] = sq[pl.ds(0, 3), :]
    rv_first = remote(vacc.at[0], rv.at[0], vsem.at[0], vrem.at[0], (fc, s))
    rv_first.start()
    for j in range(2):
        xs_ = x_all[:, j * wide : (j + 1) * wide]
        x_own = jnp.concatenate([
            x_all[pl.ds(pl.multiple_of(s * tok, tok), tok), j * wide : (j + 1) * wide],
            x_all[pl.ds(seq, MEM_PAD), j * wide : (j + 1) * wide],
        ])
        put(2, 0, j, turned(x_own, dq[...]))
        xt = jnp.transpose(xs_)
        put(2, 1, j, dot(xt, dkt[...], NT))
        put(2, 2, j, dot(xt, dvt[...], NT))
        if j == 0:
            tick(jnp.int32(6))
    for j in range(shards):
        copy_a(2 * shards + j).start()
    tick(jnp.int32(7))

    def vec_hop(k):
        return remote(vacc.at[k], rv.at[k], vsem.at[k], vrem.at[k], ((fc, fx, fy)[k], s))

    def vec_step(k):
        vec_hop(k - 1).wait_recv()
        vacc[k] = vacc[k - 1] + rv[k - 1]
        vec_hop(k).start()

    vec_step(1)
    w_copy(9).wait()
    w_copy(10).wait()
    wkm = wbuf[1].reshape(width, width)
    wvm = wbuf[2].reshape(width, width)
    spare = (abuf.at[0, pl.ds(0, tok)], abuf.at[1, pl.ds(0, tok)], d_pre.at[pl.ds(0, tok)])
    small = []

    def to_shard(src, dst, ssem, rsem, t):
        return remote(src, dst.at[s], ssem.at[t], rsem.at[s], (r, lax.rem(s + t, shards)))

    def row_grads(blk):
        c = pl.ds(pl.multiple_of(blk * tok, tok), tok)
        return jnp.transpose(dot(wkm, dkt[:, c]) + dot(wvm, dvt[:, c]))

    def along(src, dst, i, up):
        return remote(src, dst, xsem.at[i], xrem.at[i], (r, s + 1 if up else s - 1))

    far = (along(spare[0], relay.at[0], 0, True), along(spare[0], relay.at[1], 1, False))
    near = (along(spare[1], rx.at[0], 2, True), along(spare[2], rx.at[1], 3, False))
    has_far = (s < 2, s >= 2)
    has_near = (s < shards - 1, s > 0)
    has_relay = (s > 0, s < shards - 1)
    spare[0][...] = row_grads(lax.rem(s + 2, shards)).astype(BF)
    for i in range(2):
        pl.when(has_far[i])(far[i].start)
    tick(jnp.int32(8))
    for i in range(2):
        @pl.when(has_near[i])
        def _():
            spare[1 + i][...] = row_grads(s + 1 - 2 * i).astype(BF)

            @pl.when(has_relay[i])
            def _():
                along(spare[0], relay.at[i], i, i == 0).wait_recv()
                spare[1 + i][...] = (spare[1 + i][...].astype(F32) + relay[i].astype(F32)).astype(BF)

            near[i].start()

        if i == 0:
            tick(jnp.int32(9))
    own_rows = pl.ds(0, tok)
    back[own_rows, :] = back[own_rows, :] + row_grads(s)
    value = dot(wkm, dkt[:, pl.ds(seq, MEM_KEYS)]) + dot(wvm, dvt[:, pl.ds(seq, MEM_KEYS)])
    w_copy(11).wait()
    mrows = pl.ds(tok, MEM_PAD)
    value = jnp.transpose(value)[:MEM_PAD] + dot(dq[mrows, :], wbuf[3].reshape(width, width), NT)
    rm[s] = value.astype(BF)
    for t in range(1, shards):
        small.append(remote(rm.at[s], rm.at[s], msem.at[t], mrem.at[s], (r, lax.rem(s + t, shards))))
        small[-1].start()
    vec_step(2)
    tick(jnp.int32(10))
    for j in range(2):
        wt = wbuf[3, 2 * j : 2 * j + 2].reshape(wide, width)
        c = pl.ds(j * wide, wide)
        back[own_rows, c] = back[own_rows, c] + dot(dq[own_rows, :], wt, NT)
    vec_hop(2).wait_recv()
    vz[s] = vacc[2] + rv[2]
    for t in range(1, shards):
        small.append(to_shard(vz.at[s], vz, vzs, vzr, t))
        small[-1].start()
    pl.loop(11, ticks)(tick)

    for t in range(1, shards):
        other = lax.rem(s + t, shards)
        for buf, rsem in ((rm, mrem), (vz, vzr)):
            remote(buf.at[other], buf.at[other], msem.at[0], rsem.at[other], (r, s)).wait_recv()
    for i in range(2):
        @pl.when(has_relay[i])
        def _():
            along(spare[0], rx.at[i], 2 + i, i == 0).wait_recv()
            back[own_rows, :] = back[own_rows, :] + rx[i].astype(F32)

    sx, sm, sv = back[own_rows, :], back[mrows, :], vz[0]
    for t in range(shards):
        sm = sm + rm[t].astype(F32)
        if t:
            sv = sv + vz[t]
    gr[pl.ds(0, tok), :] = sx
    gr[pl.ds(tok, MEM_PAD), :] = sm
    final = [
        pltpu.make_async_copy(gr, o_x, osem.at[0]),
    ]
    for c in final:
        c.start()
    o_vec[...] = sv
    for k in range(3):
        hop_wait(k, 2)
    for c in final:
        c.wait()

    @pl.loop(0, units)
    def _(u):
        copy_a(u).wait_send()
        for c in copy_b(u) + copy_c(u):
            c.wait_send()
        pl.when(s != unit_shard(u))(lambda: copy_z(u).wait_send())

    for k in range(3):
        for j in range(3):
            for c in hop(k, j):
                c.wait_send()
    for c in small:
        c.wait_send()
    for i in range(2):
        pl.when(has_far[i])(far[i].wait_send)
        pl.when(has_near[i])(near[i].wait_send)
    for k in range(3):
        vec_hop(k).wait_send()


def backward_all(saved, out_grad, mem_grad, docs):
    shards = lax.axis_size("shard")
    tok, width = out_grad.shape
    mem = mem_grad.shape[0]
    half = saved[0].shape[3]
    m, n = tok + MEM_PAD, tok * shards + MEM_KEYS
    pairs = width // 128
    any_space = pl.BlockSpec(memory_space=pl.ANY)
    vm = pl.BlockSpec(memory_space=pltpu.VMEM)
    dma = pltpu.SemaphoreType.DMA
    V = pltpu.VMEM
    units = 3 * shards
    piece4 = (4, 2, half, width)
    outs = tuple(jax.ShapeDtypeStruct(piece4, BF) for _ in range(3)) + (
        jax.ShapeDtypeStruct((m, width), F32),
        jax.ShapeDtypeStruct((16, width), F32),
    )
    big = (4, 2, half, width)
    scratch = [
        V((units, 2, 2, 2, half, width), BF), V((units, 2, 2, half, width), BF), V((units, 2, 2, half, width // 2), BF),
        V((units, 2, half, width // 2), BF), V((3, shards, half, width), BF), V((2, tok, width), BF), V((2, tok, width), BF),
        V((shards, MEM_PAD, width), BF), V((3, 16, width), F32), V((shards, 16, width), F32), V((3, 16, width), F32),
        V((4,) + big, BF), V((n, width), BF), V((2, m, 128), BF), V((2, n, 128), BF), V((2, n, 128), BF),
        V((m, width), F32), V((2, m, 128), F32), V((m, n), F32), V((m, n), F32), V((m, n), F32), V((m, n), BF),
        V((m, n), BF), V((m, width), BF), V((2, m, width), BF),
        V((2, m, width), F32), V((m, width), BF), V((m, width), F32), V((m, 128), F32), V((m, width), F32),
        V((m, width), BF), V((m, width), F32), V((m, width), BF), V((pairs, m, 128), BF), V((m, width), BF),
        V((width, n), BF), V((width, n), BF),
    ]
    sems = (
        [dma((units,))] * 2 + [dma((units, 2))] * 4 + [dma((units,)), dma((3, shards))]
        + [dma((3, 3, 2)), dma((3, 3, 2)), dma((shards,)), dma((shards,)), dma((shards,)), dma((shards,))]
        + [dma((3,)), dma((3,)), dma((shards,)), dma((shards,)), dma((3,)), dma((12,)), dma((4, 2)), dma((2, 4))]
        + [dma((8,)), dma((1,))]
    )
    return pl.pallas_call(
        functools.partial(backward_kernel, shards, half, width, mem),
        out_shape=outs,
        in_specs=[any_space] * 16 + [vm, vm, any_space, vm, pl.BlockSpec(memory_space=pltpu.SMEM)],
        out_specs=[any_space] * 4 + [vm],
        scratch_shapes=scratch + sems,
        compiler_params=pltpu.CompilerParams(collective_id=4, has_side_effects=True, vmem_limit_bytes=VMEM_LIMIT),
        name="backward_layer",
    )(*saved, out_grad, mem_grad, docs)


def plain_body(tokens, memory_rows, doc_lengths, w_query, w_key, w_value, w_attn_out, w_hidden, w_output,
         b_query, b_value, b_attn_out, b_hidden, b_output, gain_attn, shift_attn, gain_ffn, shift_ffn,
         out_grad, memory_grad):
    tok, width = tokens.shape
    mem = memory_rows.shape[1]
    shards = lax.axis_size("shard")
    s = lax.axis_index("shard")
    seq = tok * shards
    srows = w_query.shape[0]
    m = tok + MEM_PAD
    n = seq + MEM_KEYS
    scaling = 1.0 / math.sqrt(HD)

    vec = jnp.concatenate(
        [v.reshape(-1, srows) for v in (
            b_query, b_value, b_attn_out, b_output, gain_attn, shift_attn, gain_ffn, shift_ffn, b_hidden
        )]
        + [jnp.zeros((4, srows), BF)]
    )
    vec = lax.dynamic_update_slice(jnp.zeros((16, width), BF), vec, (0, s * srows))
    rows = jnp.concatenate([tokens, memory_rows[0], jnp.zeros((MEM_PAD - mem, width), F32)])
    low_rows = rows.astype(BF)
    qkvo = jnp.stack([w_query, w_key, w_value, w_attn_out])
    qkvo, w_hid, w_out, x_tok, vec_all = gather_plain(qkvo, w_hidden, w_output, low_rows[:tok], vec)
    vec = jnp.sum(vec_all.astype(F32), axis=0)
    bq, bv, bo, bout, ga, sa, gf, sf = (vec[i] for i in range(8))
    bh = jnp.transpose(vec[8:12].reshape(4, shards, srows), (1, 0, 2)).reshape(4 * width)

    doc_ends = jnp.cumsum(doc_lengths[0])
    seg = jnp.sum((jnp.arange(seq, dtype=jnp.int32)[:, None] >= doc_ends[None, :]).astype(jnp.int32), axis=1)
    place = jnp.arange(MEM_KEYS, dtype=jnp.int32)
    mem_seg = jnp.where(place < mem // 2, -1, jnp.where(place < mem, -3, -4)).astype(jnp.int32)
    kseg = jnp.concatenate([seg, mem_seg])[None, :]
    qseg = jnp.concatenate(
        [lax.dynamic_slice_in_dim(seg, s * tok, tok), jnp.full((MEM_PAD,), -2, jnp.int32)]
    )[:, None]
    index = jnp.arange(m, dtype=jnp.int32)[:, None]
    once = jnp.where(index < tok, 1.0, jnp.where((index < tok + mem) & (s == 0), 1.0, 0.0)).astype(F32)
    once_low = once.astype(BF)

    x_all = jnp.concatenate([x_tok, low_rows[tok:], jnp.zeros((MEM_KEYS - MEM_PAD, width), BF)])
    query = (jnp.dot(low_rows, qkvo[0], preferred_element_type=F32) + bq).astype(BF)
    keys = jnp.dot(x_all, qkvo[1], preferred_element_type=F32).astype(BF)
    values = (jnp.dot(x_all, qkvo[2], preferred_element_type=F32) + bv).astype(BF)
    context, lse = attention(query, keys, values, qseg, kseg, scaling)
    context_low = context.astype(BF)
    branch = jnp.dot(context_low, qkvo[3], preferred_element_type=F32) + bo
    normed_attn, inverse_attn = layer_stats(rows + branch)
    after_attn = normed_attn * ga + sa
    after_low = after_attn.astype(BF)
    pre_act = jnp.concatenate([jnp.dot(after_low, w_hid[q], preferred_element_type=F32) for q in range(4)], axis=1) + bh
    half_erf = 0.5 * (1.0 + lax.erf(pre_act * GELU_ROOT))
    act_low = (pre_act * half_erf).astype(BF)
    second = jnp.dot(act_low, w_out, preferred_element_type=F32) + bout
    normed_ffn, inverse_ffn = layer_stats(after_attn + second)
    result = normed_ffn * gf + sf

    grads = jnp.concatenate([out_grad, memory_grad[0], jnp.zeros((MEM_PAD - mem, width), F32)])
    back_ffn = norm_back(grads * gf, normed_ffn, inverse_ffn)
    d_output = back_ffn.astype(BF)
    g_out = jnp.einsum("rf,rd->fd", act_low * once_low, d_output, preferred_element_type=F32).astype(BF)
    d_act = jnp.einsum("rd,fd->rf", d_output, w_out, preferred_element_type=F32)
    d_pre = (d_act * (half_erf + pre_act * jnp.exp(-0.5 * pre_act * pre_act) * GELU_DENSITY)).astype(BF)
    after_once = after_low * once_low
    g_hid = jnp.stack(
        [jnp.einsum("rd,rf->df", after_once, d_pre[:, q * width : (q + 1) * width], preferred_element_type=F32).astype(BF)
         for q in range(4)]
    )
    back_first = back_ffn + sum(
        jnp.einsum("rf,df->rd", d_pre[:, q * width : (q + 1) * width], w_hid[q], preferred_element_type=F32)
        for q in range(4)
    )
    back_attn = norm_back(back_first * ga, normed_attn, inverse_attn)
    d_branch = back_attn.astype(BF)
    d_context = jnp.einsum("re,de->rd", d_branch, qkvo[3], preferred_element_type=F32).astype(BF)
    dq, dkt, dvt = attention_back(query, keys, values, qseg, kseg, once, context, lse, d_context, scaling)
    g_qkvo = jnp.stack([
        jnp.einsum("rd,re->de", low_rows * once_low, dq, preferred_element_type=F32).astype(BF),
        jnp.einsum("rd,er->de", x_all, dkt, preferred_element_type=F32).astype(BF),
        jnp.einsum("rd,er->de", x_all, dvt, preferred_element_type=F32).astype(BF),
        jnp.einsum("rd,re->de", context_low * once_low, d_branch, preferred_element_type=F32).astype(BF),
    ])
    dx = jnp.einsum("er,de->rd", dkt, qkvo[1], preferred_element_type=F32) + jnp.einsum(
        "er,de->rd", dvt, qkvo[2], preferred_element_type=F32
    )
    base = back_attn + jnp.einsum("re,de->rd", dq, qkvo[0], preferred_element_type=F32)

    def over_rows(terms):
        return jnp.sum(once * terms, axis=0)

    gb_hidden = over_rows(d_pre.astype(F32)).reshape(shards, 4, srows).transpose(1, 0, 2).reshape(4, width)
    squares = jnp.stack([jnp.sum(v[:tok] * v[:tok]) for v in (result, branch, second)])
    vec_grads = jnp.concatenate([
        jnp.stack([
            over_rows(dq.astype(F32)),
            jnp.sum(dvt.astype(F32), axis=1),
            over_rows(d_branch.astype(F32)),
            over_rows(d_output.astype(F32)),
            over_rows(back_first * normed_attn),
            over_rows(back_first),
            over_rows(grads * normed_ffn),
            over_rows(grads),
        ]),
        gb_hidden,
        jnp.pad(squares[None], ((0, 3), (0, width - 3))),
    ])
    g_qkvo, g_hid, g_out, dx_own, dx_mem, vec_sum = reduce_plain(
        g_qkvo, g_hid, g_out, dx[:seq].astype(BF), dx[seq : seq + MEM_PAD], vec_grads
    )
    own = lax.dynamic_slice(vec_sum, (0, s * srows), (12, srows))
    rms = jnp.sqrt(vec_sum[12, :3] / float(seq * width * lax.axis_size("replica")))
    g_qkvo = g_qkvo.astype(F32)
    grad_hidden = jnp.concatenate([g_hid[q] for q in range(4)], axis=1).astype(F32)
    return (
        result[:tok],
        result[tok : tok + mem][None],
        base[:tok] + dx_own,
        (base[tok : tok + mem] + dx_mem[:mem])[None],
        g_qkvo[0],
        g_qkvo[1],
        g_qkvo[2],
        g_qkvo[3],
        grad_hidden,
        g_out.astype(F32),
        own[0],
        own[1],
        own[2],
        own[8:12].reshape(-1),
        own[3],
        own[4],
        own[5],
        own[6],
        own[7],
        rms[0],
        rms[1],
        rms[2],
    )


def direct_body(tokens, memory_rows, doc_lengths, w_query, w_key, w_value, w_attn_out, w_hidden, w_output,
                b_query, b_value, b_attn_out, b_hidden, b_output, gain_attn, shift_attn, gain_ffn, shift_ffn,
                out_grad, memory_grad):
    tok, width = tokens.shape
    mem = memory_rows.shape[1]
    shards = lax.axis_size("shard")
    s = lax.axis_index("shard")
    srows = w_query.shape[0]
    vec = jnp.concatenate(
        [b_query, b_value, b_attn_out, b_output, gain_attn, shift_attn, gain_ffn, shift_ffn]
        + [jnp.zeros((8 * srows,), BF)]
    ).reshape(16, srows)
    b_hid = jnp.broadcast_to(b_hidden.astype(F32)[None], (8, width))
    *saved, result, vec_full, squares = forward_all(
        w_query, w_key, w_value, w_attn_out, w_hidden, w_output, tokens, memory_rows[0], vec, b_hid, doc_lengths
    )
    g_qkvo, g_hid, g_out, grad_rows, vec_sum = backward_all(
        tuple(saved) + (vec_full, squares), out_grad, memory_grad[0], doc_lengths
    )
    own = lax.dynamic_slice(vec_sum, (0, s * srows), (8, srows))
    own_hid = lax.dynamic_slice(vec_sum, (8 + s, 0), (1, width))[0]
    count = float(tok * shards * width * lax.axis_size("replica"))
    rms = jnp.sqrt(jnp.sum(vec_sum[12:15], axis=1) / count)
    g_qkvo = g_qkvo.reshape(4, srows, width).astype(F32)
    g_hid = g_hid.reshape(4, srows, width)
    return (
        result[:tok],
        result[tok : tok + mem][None],
        grad_rows[:tok],
        grad_rows[tok : tok + mem][None],
        g_qkvo[0],
        g_qkvo[1],
        g_qkvo[2],
        g_qkvo[3],
        jnp.concatenate([g_hid[q] for q in range(4)], axis=1).astype(F32),
        g_out.reshape(4 * srows, width).astype(F32),
        own[0],
        own[1],
        own[2],
        own_hid,
        own[3],
        own[4],
        own[5],
        own[6],
        own[7],
        rms[0],
        rms[1],
        rms[2],
    )


def solution(mesh):
    direct = mesh.shape["replica"] == 8 and mesh.shape["shard"] == 4
    shard1, shard2 = P("shard"), P("shard", None)
    both, rep3 = P(("replica", "shard"), None), P("replica", None, None)
    return jax.shard_map(
        direct_body if direct else plain_body,
        mesh=mesh,
        in_specs=(both, rep3, P("replica", None)) + (shard2,) * 6 + (shard1,) * 9 + (both, rep3),
        out_specs=(both, rep3, both, rep3) + (shard2,) * 6 + (shard1,) * 9 + (P(), P(), P()),
        check_vma=False,
    )
```

```python
import functools
import math

import jax
import jax.numpy as jnp
from jax import lax
from jax.experimental import pallas as pl
from jax.experimental.pallas import tpu as pltpu
from jax.sharding import PartitionSpec as P

H = 12
HD = 64
EPSILON = 1e-12
GELU_ROOT = 0.7071067811865476
GELU_DENSITY = 0.3989422804014327
MESH = pl.DeviceIdType.MESH
BF = jnp.bfloat16
F32 = jnp.float32
MEM_PAD = 32
MEM_KEYS = 128
VMEM_LIMIT = 60 << 20
NEG = -1e30


def region(ref, group, sh, q0, nq, h0, nh, cols=None):
    hs = h0 if nh == 1 else pl.ds(h0, nh)
    qs = q0 if nq == 1 else pl.ds(q0, nq)
    tail = () if cols is None else (slice(None), cols)
    return ref.at[((sh, qs, hs) if group == 2 else (qs, sh, hs)) + tail]


def neighbours():
    r = lax.axis_index("replica")
    s = lax.axis_index("shard")
    core, xbit, ybit = r % 2, (r // 2) % 2, (r // 4) % 2
    return r, s, core, xbit, ybit, r + 1 - 2 * core, r + 2 - 4 * xbit, r + 4 - 8 * ybit


def enter(peers, r, s, shards):
    sem = pltpu.get_barrier_semaphore()
    for p in peers:
        pl.semaphore_signal(sem, 1, device_id=(p, s), device_id_type=MESH)
    for t in range(1, shards):
        pl.semaphore_signal(sem, 1, device_id=(r, lax.rem(s + t, shards)), device_id_type=MESH)
    return lambda: pl.semaphore_wait(sem, len(peers) + shards - 1)


def remote(src, dst, ssem, rsem, dev):
    return pltpu.make_async_remote_copy(
        src_ref=src, dst_ref=dst, send_sem=ssem, recv_sem=rsem, device_id=dev, device_id_type=MESH
    )


def gather_plain(qkvo, hid, outw, xtok, vec):
    width = qkvo.shape[2]
    full = functools.partial(lax.all_gather, axis_name="shard", tiled=True)
    hid = full(hid, axis=0)
    return (
        full(qkvo, axis=1),
        jnp.stack([hid[:, q * width : (q + 1) * width] for q in range(4)]),
        full(outw, axis=0),
        full(xtok, axis=0),
        lax.all_gather(vec, "shard", axis=0),
    )


def reduce_plain(g_qkvo, g_hid, g_out, dx, mem, vec):
    scatter = functools.partial(lax.psum_scatter, axis_name="shard", tiled=True)
    return (
        lax.psum(scatter(g_qkvo, scatter_dimension=1), "replica"),
        lax.psum(scatter(g_hid, scatter_dimension=1), "replica"),
        lax.psum(scatter(g_out, scatter_dimension=0), "replica"),
        scatter(dx, scatter_dimension=0).astype(F32),
        lax.psum(mem, "shard"),
        lax.psum(vec, ("replica", "shard")),
    )


NT = (((1,), (1,)), ((), ()))
NN = (((1,), (0,)), ((), ()))
TN = (((0,), (0,)), ((), ()))


def dot(a, b, dims=NN):
    return lax.dot_general(a, b, dims, preferred_element_type=F32)


def head_lanes(shape, head):
    lane = lax.broadcasted_iota(jnp.int32, shape, 1)
    return (lane < HD) if head == 0 else (lane >= HD)


def mask_bias(qseg, kseg):
    allowed = (qseg == kseg) | (kseg == -1) | ((qseg == -2) & (kseg != -4))
    return jnp.where(allowed, 0.0, NEG)


def attend_kernel(scaling, q_ref, k_ref, v_ref, qseg_ref, kseg_ref, ctx_ref, lse_ref, bias_ref):
    @pl.when(pl.program_id(0) == 0)
    def _():
        bias_ref[...] = mask_bias(qseg_ref[...], kseg_ref[...])

    q, k, v = q_ref[...], k_ref[...], v_ref[...]
    zero_q = jnp.zeros_like(q)
    contexts, totals = [], []
    for head in range(2):
        qh = jnp.where(head_lanes(q.shape, head), q, zero_q)
        scores = dot(qh, k, NT) * scaling + bias_ref[...]
        top = jnp.max(scores, axis=1, keepdims=True)
        powers = jnp.exp(scores - top)
        lse = top + jnp.log(jnp.sum(powers, axis=1, keepdims=True))
        probs = powers * jnp.exp(top - lse)
        contexts.append(dot(probs.astype(BF), v))
        totals.append(lse)
    first = head_lanes(q.shape, 0)
    ctx_ref[...] = jnp.where(first, contexts[0], contexts[1])
    lse_ref[...] = jnp.where(first, totals[0], totals[1])


def attend_back_kernel(scaling, q_ref, k_ref, v_ref, qseg_ref, kseg_ref, weight_ref, ctx_ref, lse_ref, do_ref,
                       dq_ref, dk_ref, dv_ref, bias_ref):
    @pl.when(pl.program_id(0) == 0)
    def _():
        bias_ref[...] = mask_bias(qseg_ref[...], kseg_ref[...])

    q, k, v, do = q_ref[...], k_ref[...], v_ref[...], do_ref[...]
    weight = weight_ref[...] > 0
    dq, dk, dv = None, None, None
    for head in range(2):
        lanes = head_lanes(q.shape, head)
        qh = jnp.where(lanes, q, jnp.zeros_like(q))
        doh = jnp.where(lanes, do, jnp.zeros_like(do))
        lse = lse_ref[:, head * HD : head * HD + 1]
        scores = dot(qh, k, NT) * scaling + bias_ref[...]
        probs = jnp.exp(scores - lse)
        delta = jnp.sum(doh.astype(F32) * ctx_ref[...], axis=1, keepdims=True)
        d_scores = (probs * (dot(doh, v, NT) - delta)).astype(BF)
        kh = jnp.where(head_lanes(k.shape, head), k, jnp.zeros_like(k))
        part_q = dot(d_scores, kh)
        part_k = dot(jnp.where(weight, qh, jnp.zeros_like(qh)), d_scores, TN)
        part_v = dot(jnp.where(weight, doh, jnp.zeros_like(doh)), probs.astype(BF), TN)
        dq = part_q if dq is None else dq + part_q
        dk = part_k if dk is None else dk + part_k
        dv = part_v if dv is None else dv + part_v
    dq_ref[...] = (dq * scaling).astype(BF)
    dk_ref[...] = (dk * scaling).astype(BF)
    dv_ref[...] = dv.astype(BF)


def attention(query, keys, values, qseg, kseg, scaling):
    m, width = query.shape
    n = keys.shape[0]
    rows = pl.BlockSpec((m, 2 * HD), lambda i: (0, i))
    cols = pl.BlockSpec((n, 2 * HD), lambda i: (0, i))
    return pl.pallas_call(
        functools.partial(attend_kernel, scaling),
        grid=(width // (2 * HD),),
        out_shape=(jax.ShapeDtypeStruct((m, width), F32), jax.ShapeDtypeStruct((m, width), F32)),
        in_specs=[rows, cols, cols, pl.BlockSpec((m, 1), lambda i: (0, 0)), pl.BlockSpec((1, n), lambda i: (0, 0))],
        out_specs=[rows, rows],
        scratch_shapes=[pltpu.VMEM((m, n), F32)],
        compiler_params=pltpu.CompilerParams(vmem_limit_bytes=VMEM_LIMIT),
        name="attend",
    )(query, keys, values, qseg, kseg)


def attention_back(query, keys, values, qseg, kseg, weight, context, lse, d_context, scaling):
    m, width = query.shape
    n = keys.shape[0]
    rows = pl.BlockSpec((m, 2 * HD), lambda i: (0, i))
    cols = pl.BlockSpec((n, 2 * HD), lambda i: (0, i))
    turned = pl.BlockSpec((2 * HD, n), lambda i: (i, 0))
    column = pl.BlockSpec((m, 1), lambda i: (0, 0))
    return pl.pallas_call(
        functools.partial(attend_back_kernel, scaling),
        grid=(width // (2 * HD),),
        out_shape=(
            jax.ShapeDtypeStruct((m, width), BF),
            jax.ShapeDtypeStruct((width, n), BF),
            jax.ShapeDtypeStruct((width, n), BF),
        ),
        in_specs=[rows, cols, cols, column, pl.BlockSpec((1, n), lambda i: (0, 0)), column, rows, rows, rows],
        out_specs=[rows, turned, turned],
        scratch_shapes=[pltpu.VMEM((m, n), F32)],
        compiler_params=pltpu.CompilerParams(vmem_limit_bytes=VMEM_LIMIT),
        name="attend_back",
    )(query, keys, values, qseg, kseg, weight, context, lse, d_context)


def layer_stats(totals):
    center = totals - jnp.mean(totals, axis=-1, keepdims=True)
    spread = jnp.mean(center * center, axis=-1, keepdims=True)
    inverse = lax.rsqrt(spread + EPSILON)
    return (center * inverse, inverse)


def norm_back(grad_normed, normed, inverse):
    return inverse * (
        grad_normed
        - jnp.mean(grad_normed, axis=-1, keepdims=True)
        - normed * jnp.mean(grad_normed * normed, axis=-1, keepdims=True)
    )


LOG_ROWS = 32


def row_blocks(m, step=LOG_ROWS):
    return [pl.ds(i, step) for i in range(0, m, step)]


def matrix(ref, *lead, cols=None):
    value = ref[lead + (slice(None),) * 3 + ((slice(None),) if cols is None else (cols,))]
    return value.reshape(-1, value.shape[-1])


def full_vectors(vec_all, shards, srows, width):
    total = None
    for i in range(shards):
        row = lax.broadcasted_iota(jnp.int32, (srows, width), 0)
        col = lax.broadcasted_iota(jnp.int32, (srows, width), 1)
        place = jnp.where(col == row + i * srows, 1.0, 0.0).astype(BF)
        part = dot(vec_all[i].astype(BF), place)
        total = part if total is None else total + part
    return total


def segments(docs, ndoc, pos):
    end = docs[0, 0]
    seg = jnp.where(pos >= end, 1, 0)
    for i in range(1, ndoc):
        end = end + docs[0, i]
        seg = seg + jnp.where(pos >= end, 1, 0)
    return seg


def write_bias(bias, docs, ndoc, s, tok, seq, mem):
    m, n = bias.shape
    kpos = lax.broadcasted_iota(jnp.int32, (1, n), 1)
    place = kpos - seq
    kseg = jnp.where(kpos < seq, segments(docs, ndoc, kpos), jnp.where((place >= 0) & (place < mem // 2), -1, -3))
    for rows in row_blocks(tok):
        index = lax.broadcasted_iota(jnp.int32, (LOG_ROWS, 1), 0) + rows.start
        allowed = (segments(docs, ndoc, index + s * tok) == kseg) | (kseg == -1)
        bias[rows, :] = jnp.where(allowed, 0.0, NEG)
    if m > tok:
        own = (kpos >= s * tok) & (kpos < (s + 1) * tok)
        allowed = own | ((s == 0) & (place >= 0) & (place < mem))
        bias[pl.ds(tok, m - tok), :] = jnp.broadcast_to(jnp.where(allowed, 0.0, NEG), (m - tok, n))


def forward_kernel(shards, half, width, mem, ndoc,
                   wq, wk, wv, wo, hid, outw, tokens, memr, bq, bv, bo, bout, ga, sa, gf, sf, bhid, docs,
                   o_qkvo, o_hid, o_out, o_x, o_q, o_k, o_v, o_ctx, o_lse, o_na, o_ia, o_al, o_act, o_slope, o_nf, o_if,
                   o_res, o_vec, o_sq, o_mem,
                   w_qkvo, w_hid, w_out, x_all, vec_all, bh_all, rows, q_s, k_s, v_s, s_s, p_s, bias, inv_s, ctx, ctx_low, lse,
                   branch, na, ia, after, al, act, slope, second, nf, if_, res, vfull, sq, mctx, mlse,
                   zs, zr, hsem, hrem, xs, xr, vs, vr, hs, hr, ms, mr, es, er, ls, os_, wsem):
    r, s, core, xbit, ybit, fc, fx, fy = neighbours()
    q_own, q_lo = 2 * core + ybit, 2 * core
    bufs = (w_qkvo, w_hid, w_out)
    tok = tokens.shape[0]
    m, n = rows.shape[0], x_all.shape[0]
    seq = tok * shards
    reach = shards // 2

    local = [pltpu.make_async_copy(w, w_qkvo.at[i, s], ls.at[i]) for i, w in enumerate((wq, wk, wv, wo))]
    local.append(pltpu.make_async_copy(tokens, rows.at[pl.ds(0, tok), :], ls.at[4]))
    late = [pltpu.make_async_copy(hid.at[:, :, pl.ds(q * width, width)], w_hid.at[q, s], ls.at[5 + q]) for q in range(4)]
    late.append(pltpu.make_async_copy(outw, w_out.at[s], ls.at[9]))
    for c in local + late:
        c.start()
    everyone_in = enter((fc, fx, fy), r, s, shards)

    def reg(g, sh, q0, nq, h0, nh):
        return region(bufs[g], g, sh, q0, nq, h0, nh)

    def block(i):
        return x_all.at[pl.ds(pl.multiple_of(i * tok, tok), tok), :]

    def rows_copy(sh, k):
        return remote(block(sh), block(sh), xs.at[k, sh], xr.at[sh], (r, s + 1 if k == 0 else s - 1))

    def on_line(k, fn):
        pl.when(s + 1 < shards if k == 0 else s > 0)(fn)

    sends = []
    side = width // 2
    left_cols, right_cols = pl.ds(0, side), pl.ds(side, side)

    def piece_copy(g, sh, k):
        a = reg(g, sh, q_own, 1, xbit, 1)
        return remote(a, a, zs.at[g, k, sh], zr.at[g, sh], (r, s + 1 if k == 0 else s - 1))

    def push(g):
        for k in range(2):
            on_line(k, lambda k=k: piece_copy(g, s, k).start())

    def hop(g, sh, k):
        if k == 0:
            moves = ((q_own, 1, xbit, 1, left_cols, fx), (q_own, 1, xbit, 1, right_cols, fy))
        elif k == 1:
            moves = ((q_own, 1, 0, 2, left_cols, fy), (q_lo, 2, xbit, 1, right_cols, fx))
        else:
            moves = ((q_lo, 2, 0, 2, None, fc),)
        out = []
        for i, (q0, nq, h0, nh, cols, dev) in enumerate(moves):
            a = region(bufs[g], g, sh, q0, nq, h0, nh, cols)
            out.append(remote(a, a, hsem.at[g, k, i, sh], hrem.at[g, k, i, sh], (dev, s)))
        return out

    def each_foreign(fn, g, t):
        for left in (True, False):
            sh = s - t if left else s + t
            pl.when(s >= t if left else s + t < shards)(functools.partial(fn, g, left, sh))

    def relay_rows(last, g, left, sh):
        rows_copy(sh, 0).wait_recv()
        if not last:
            k = 0 if left else 1
            on_line(k, lambda: rows_copy(sh, k).start())

    def far_block(g, left, sh):
        at = pl.ds(pl.multiple_of(sh * tok, tok), tok)
        x_all[at, :] = jnp.zeros((tok, width), BF)
        k_s[:, at, :] = jnp.zeros((width // 128, tok, 128), BF)
        v_s[:, at, :] = jnp.zeros((width // 128, tok, 128), BF)

    def rows_in(t):
        if t <= reach:
            each_foreign(functools.partial(relay_rows, t == reach), 0, t)

    def stage0(g, left, sh):
        piece_copy(g, sh, 0).wait_recv()
        k = 0 if left else 1
        on_line(k, lambda: piece_copy(g, sh, k).start())
        for c in hop(g, sh, 0):
            c.start()

    def advance(k, g, left, sh):
        for c in hop(g, sh, k - 1):
            c.wait_recv()
        for c in hop(g, sh, k):
            c.start()

    stage1, stage2 = functools.partial(advance, 1), functools.partial(advance, 2)

    def save_shard(g, sh):
        bank = (o_qkvo, o_hid, o_out)[g]
        a, b = (bufs[g].at[sh], bank.at[sh]) if g == 2 else (bufs[g].at[:, sh], bank.at[:, sh])
        return pltpu.make_async_copy(a, b, wsem.at[g, sh])

    def stage3(g, left, sh):
        hop(g, sh, 2)[0].wait_recv()
        save_shard(g, sh).start()

    def finish(g, left, sh):
        for k in range(3):
            for c in hop(g, sh, k):
                c.wait_send()
        k = 0 if left else 1

        on_line(k, lambda: piece_copy(g, sh, k).wait_send())

    def finish_rows(g, left, sh):
        k = 0 if left else 1
        on_line(k, lambda: rows_copy(sh, k).wait_send())

    def run(stage, g):
        for t in range(1, shards):
            each_foreign(stage, g, t)

    saves = []

    def save(src, dst):
        saves.append(pltpu.make_async_copy(src, dst, os_.at[len(saves)]))
        saves[-1].start()

    for c in local[:4]:
        c.wait()
    everyone_in()
    push(0)
    local[4].wait()
    rows[pl.ds(tok, mem), :] = memr[:, 0, :]
    rows[pl.ds(tok + mem, MEM_PAD - mem), :] = jnp.zeros((MEM_PAD - mem, width), F32)
    block(s)[...] = rows[pl.ds(0, tok), :].astype(BF)
    x_all[pl.ds(seq, MEM_PAD), :] = rows[pl.ds(tok, MEM_PAD), :].astype(BF)
    x_all[pl.ds(seq + MEM_PAD, MEM_KEYS - MEM_PAD), :] = jnp.zeros((MEM_KEYS - MEM_PAD, width), BF)
    for t in range(reach + 1, shards):
        each_foreign(far_block, 0, t)
    for c in late:
        c.wait()
    push(1)
    for i, v in enumerate((bq, bv, bo, bout, ga, sa, gf, sf)):
        vec_all[s, pl.ds(i, 1), :] = v[...].astype(F32).reshape(1, 2 * half)
    bh_all[s, pl.ds(0, 1), :] = bhid[...].astype(F32).reshape(1, width)
    for t in range(1, shards):
        dev = (r, lax.rem(s + t, shards))
        sends.append(remote(vec_all.at[s], vec_all.at[s], vs.at[t], vr.at[s], dev))
        sends[-1].start()
        sends.append(remote(bh_all.at[s], bh_all.at[s], hs.at[t], hr.at[s], dev))
        sends[-1].start()
    write_bias(bias, docs, ndoc, s, tok, seq, mem)
    for g in range(3):
        save_shard(g, s).start()
    def push_rows():
        for k in range(2):
            on_line(k, lambda k=k: rows_copy(s, k).start())

    order = [(g, t) for g in range(3) for t in range(1, shards)]
    extras = {1: push_rows, 3: lambda: push(2), 5: lambda: rows_in(1), 8: lambda: rows_in(2)}

    def tick(i):
        for k, stage in enumerate((stage0, stage1, stage2)):
            if 0 <= i - 2 * k < len(order):
                each_foreign(stage, *order[i - 2 * k])
        if i in extras:
            extras[i]()

    for i in range(7):
        tick(i)
    for t in range(1, shards):
        other = lax.rem(s + t, shards)
        remote(vec_all.at[other], vec_all.at[other], vs.at[t], vr.at[other], (r, other)).wait_recv()
        remote(bh_all.at[other], bh_all.at[other], hs.at[t], hr.at[other], (r, other)).wait_recv()
    vfull[...] = full_vectors(vec_all, shards, 2 * half, width)
    run(stage3, 0)
    save(vfull, o_vec)

    def vrow(i):
        return vfull[pl.ds(i, 1), :]

    def bias_cols(i, c):
        return vfull[pl.ds(i, 1), c]

    def keys_values(start, size):
        at = pl.ds(start, size)

        @pl.loop(0, width // 256)
        def _(ct):
            c = pl.ds(pl.multiple_of(ct * 256, 256), 256)
            xb = x_all[at, :]
            y = dot(xb, matrix(w_qkvo, 1, cols=c)).astype(BF)
            k_s[2 * ct, at] = y[:, :128]
            k_s[2 * ct + 1, at] = y[:, 128:]
            y = (dot(xb, matrix(w_qkvo, 2, cols=c)) + bias_cols(1, c)).astype(BF)
            v_s[2 * ct, at] = y[:, :128]
            v_s[2 * ct + 1, at] = y[:, 128:]

    @pl.loop(0, width // 256)
    def _(ct):
        c = pl.ds(pl.multiple_of(ct * 256, 256), 256)
        wt = matrix(w_qkvo, 0, cols=c)
        b = bias_cols(0, c)
        for part, at, size in ((block(s)[...], 0, tok), (x_all[pl.ds(seq, MEM_PAD), :], tok, MEM_PAD)):
            y = (dot(part, wt) + b).astype(BF) * jnp.asarray(0.125, BF)
            q_s[2 * ct, pl.ds(at, size)] = y[:, :128]
            q_s[2 * ct + 1, pl.ds(at, size)] = y[:, 128:]

    own_at = pl.multiple_of(s * tok, tok)
    keys_values(own_at, tok)
    keys_values(seq, MEM_KEYS)
    save(q_s, o_q)
    lane = lax.broadcasted_iota(jnp.int32, (tok, 128), 1)
    lane_m = lane[:MEM_PAD]
    mrows = pl.ds(tok, MEM_PAD)

    def memory_pair(p):
        seen = jnp.concatenate([bias[mrows, pl.ds(own_at, tok)], bias[mrows, pl.ds(seq, MEM_KEYS)]], axis=1)
        kk = jnp.concatenate([k_s[p, pl.ds(own_at, tok)], k_s[p, pl.ds(seq, MEM_KEYS)]])
        vv = jnp.concatenate([v_s[p, pl.ds(own_at, tok)], v_s[p, pl.ds(seq, MEM_KEYS)]])
        q = q_s[p, mrows]
        outs = []
        for head in range(2):
            sc = dot(jnp.where((lane_m < HD) == (head == 0), q, jnp.zeros_like(q)), kk, NT) + seen
            top = jnp.max(sc, axis=1, keepdims=True)
            e = jnp.exp(sc - top)
            tot = jnp.sum(e, axis=1, keepdims=True)
            outs.append(dot(e.astype(BF), vv) / tot)
            mlse[s] = jnp.where(lane_m == 2 * p + head, top + jnp.log(tot), mlse[s])
        mctx[s, :, pl.ds(pl.multiple_of(p * 128, 128), 128)] = jnp.where(lane_m < HD, outs[0], outs[1]).astype(BF)

    mlse[s] = jnp.zeros((MEM_PAD, 128), F32)
    def served(i, services):
        for at, service in services.items():
            pl.when(i == at)(service)

    tick(7)

    @pl.loop(0, width // 128)
    def _(p):
        memory_pair(p)
        served(p, {3: lambda: tick(8)})

    for t in range(1, shards):
        dev = (r, lax.rem(s + t, shards))
        for buf, ssem, rsem in ((mctx, ms, mr), (mlse, es, er)):
            sends.append(remote(buf.at[s], buf.at[s], ssem.at[t], rsem.at[s], dev))
            sends[-1].start()

    @pl.loop(0, 2 * reach)
    def _(i):
        b = s + (1 + i // 2) * (1 - 2 * lax.rem(i, 2))
        pl.when((b >= 0) & (b < shards))(lambda: keys_values(pl.multiple_of(b * tok, tok), tok))
        served(i, {3: lambda: tick(9)})

    save(x_all, o_x)
    save(k_s, o_k)
    save(v_s, o_v)

    def pair(p):
        outs = []
        for head in range(2):
            q = q_s[p, pl.ds(0, tok)]
            s_s[pl.ds(0, tok), :] = dot(jnp.where((lane < HD) == (head == 0), q, jnp.zeros_like(q)), k_s[p], NT)
            for rb in row_blocks(tok):
                sc = s_s[rb, :] + bias[rb, :]
                top = jnp.max(sc, axis=1, keepdims=True)
                e = jnp.exp(sc - top)
                tot = jnp.sum(e, axis=1, keepdims=True)
                p_s[rb, :] = e.astype(BF)
                wide = jnp.broadcast_to(top + jnp.log(tot), (LOG_ROWS, 128))
                inv = jnp.broadcast_to(1.0 / tot, (LOG_ROWS, 128))
                if head == 0:
                    lse[p, rb] = wide
                    inv_s[rb, :] = inv
                else:
                    right = lane[:LOG_ROWS] >= HD
                    lse[p, rb] = jnp.where(right, wide, lse[p, rb])
                    inv_s[rb, :] = jnp.where(right, inv, inv_s[rb, :])
            outs.append(dot(p_s[...], v_s[p]))
        value = jnp.where(lane < HD, outs[0], outs[1]) * inv_s[...]
        c = pl.ds(pl.multiple_of(p * 128, 128), 128)
        ctx[pl.ds(0, tok), c] = value
        ctx_low[pl.ds(0, tok), c] = value.astype(BF)

    @pl.loop(0, width // 128)
    def _(p):
        pair(p)
        served(p, {2: lambda: tick(10), 4: lambda: tick(11), 5: lambda: tick(12)})

    for t in range(1, shards):
        other = lax.rem(s + t, shards)
        remote(mctx.at[other], mctx.at[other], ms.at[t], mr.at[other], (r, other)).wait_recv()
        remote(mlse.at[other], mlse.at[other], es.at[t], er.at[other], (r, other)).wait_recv()
    top = mlse[0]
    for i in range(1, shards):
        top = jnp.maximum(top, mlse[i])
    tot = sum(jnp.exp(mlse[i] - top) for i in range(shards))
    whole = top + jnp.log(tot)
    shares = [jnp.exp(mlse[i] - whole) for i in range(shards)]

    def spread(v, p):
        return jnp.where(lane_m < HD, v[:, 2 * p : 2 * p + 1], v[:, 2 * p + 1 : 2 * p + 2])

    for p in range(width // 128):
        c = pl.ds(p * 128, 128)
        value = sum(spread(shares[i], p) * mctx[i, :, c].astype(F32) for i in range(shards))
        ctx[mrows, c] = value
        ctx_low[mrows, c] = value.astype(BF)
        lse[p, mrows] = spread(whole, p)
    save(ctx, o_ctx)
    save(lse, o_lse)

    def stats(totals):
        center = totals - jnp.mean(totals, axis=1, keepdims=True)
        spread = jnp.mean(center * center, axis=1, keepdims=True)
        inverse = lax.rsqrt(spread + EPSILON)
        return center * inverse, inverse

    @pl.loop(0, width // 256)
    def _(ct):
        c = pl.ds(pl.multiple_of(ct * 256, 256), 256)
        branch[:, c] = dot(ctx_low[...], matrix(w_qkvo, 3, cols=c)) + bias_cols(2, c)
        second[:, c] = jnp.broadcast_to(bias_cols(3, c), (m, 256))

    sq[...] = jnp.zeros_like(sq)

    def add_square(i, rb, value):
        if rb.start < tok:
            total = jnp.sum(value * value, axis=0, keepdims=True)
            sq[pl.ds(i, 1), :] = sq[pl.ds(i, 1), :] + total

    for rb in row_blocks(m):
        b = branch[rb, :]
        add_square(1, rb, b)
        normed, inverse = stats(rows[rb, :] + b)
        na[rb, :] = normed
        ia[rb, :] = jnp.broadcast_to(inverse, (LOG_ROWS, 128))
        y = normed * vrow(4) + vrow(5)
        after[rb, :] = y
        al[rb, :] = y.astype(BF)
    save(na, o_na)
    save(ia, o_ia)
    save(al, o_al)
    run(stage3, 1)

    @pl.loop(0, 4)
    def _(q):
        @pl.loop(0, width // 256)
        def _(ct):
            c = pl.ds(pl.multiple_of(ct * 256, 256), 256)
            s_s[:, :256] = dot(al[...], matrix(w_hid, q, cols=c))
            b = bh_all[q, pl.ds(0, 1), c]
            for rb in row_blocks(m):
                z = s_s[rb, :256] + b
                he = 0.5 * (1.0 + lax.erf(z * GELU_ROOT))
                act[q, rb, c] = (z * he).astype(BF)
                slope[q, rb, c] = he + z * jnp.exp(-0.5 * z * z) * GELU_DENSITY


    save(act, o_act)
    save(slope, o_slope)

    def add_second(sh):
        @pl.loop(0, width // 256)
        def _(ct):
            c = pl.ds(pl.multiple_of(ct * 256, 256), 256)
            second[:, c] = second[:, c] + dot(act[sh], matrix(w_out, sh, cols=c))

    @pl.loop(0, 2 * shards - 1)
    def _(i):
        t = (i + 1) // 2
        sh = s + t * (1 - 2 * lax.rem(i, 2))

        @pl.when((sh >= 0) & (sh < shards))
        def _():
            pl.when(t > 0)(lambda: stage3(2, True, sh))
            add_second(sh)

    for rb in row_blocks(m):
        b = second[rb, :]
        add_square(2, rb, b)
        normed, inverse = stats(after[rb, :] + b)
        nf[rb, :] = normed
        if_[rb, :] = jnp.broadcast_to(inverse, (LOG_ROWS, 128))
        y = normed * vrow(6) + vrow(7)
        add_square(0, rb, y)
        res[rb, :] = y
    save(nf, o_nf)
    save(if_, o_if)
    save(res.at[pl.ds(0, tok), :], o_res)
    o_mem[:, 0, :] = res[pl.ds(tok, mem), :]
    save(sq, o_sq)
    for g in range(3):
        run(finish, g)
    for t in range(1, reach):
        each_foreign(finish_rows, 0, t)
    for c in sends:
        c.wait_send()
    for k in range(2):
        on_line(k, lambda k=k: rows_copy(s, k).wait_send())
        for g in range(3):
            on_line(k, lambda g=g, k=k: piece_copy(g, s, k).wait_send())
    for c in saves:
        c.wait()
    for g in range(3):
        for i in range(shards):
            save_shard(g, i).wait()


def forward_all(wq, wk, wv, wo, hid, outw, tokens, memr, vectors, docs):
    shards = lax.axis_size("shard")
    half, width = wq.shape[0] // 2, wq.shape[1]
    tok, mem = tokens.shape[0], memr.shape[0]
    m, n = tok + MEM_PAD, tok * shards + MEM_KEYS
    pairs = width // 128
    stack = (4, shards, 2, half, width)
    any_space = pl.BlockSpec(memory_space=pl.ANY)
    vm = pl.BlockSpec(memory_space=pltpu.VMEM)
    dma = pltpu.SemaphoreType.DMA

    def sd(shape, dtype):
        return jax.ShapeDtypeStruct(shape, dtype)

    outs = (
        sd(stack, BF), sd(stack, BF), sd((shards, 4, 2, half, width), BF), sd((n, width), BF),
        sd((pairs, m, 128), BF), sd((pairs, n, 128), BF), sd((pairs, n, 128), BF),
        sd((m, width), F32), sd((pairs, m, 128), F32), sd((m, width), F32), sd((m, 128), F32), sd((m, width), BF),
        sd((4, m, width), BF), sd((4, m, width), F32), sd((m, width), F32), sd((m, 128), F32), sd((tok, width), F32),
        sd((8, width), F32), sd((8, width), F32), sd((mem, 1, width), F32),
    )
    V = pltpu.VMEM
    scratch = [
        V(stack, BF), V(stack, BF), V((shards, 4, 2, half, width), BF), V((n, width), BF), V((shards, 8, 2 * half), F32), V((shards, 8, width), F32),
        V((m, width), F32), V((pairs, m, 128), BF), V((pairs, n, 128), BF), V((pairs, n, 128), BF), V((m, n), F32),
        V((tok, n), BF), V((m, n), F32), V((tok, 128), F32), V((m, width), F32), V((m, width), BF), V((pairs, m, 128), F32),
        V((m, width), F32), V((m, width), F32), V((m, 128), F32), V((m, width), F32), V((m, width), BF),
        V((4, m, width), BF), V((4, m, width), F32), V((m, width), F32), V((m, width), F32), V((m, 128), F32),
        V((m, width), F32), V((8, width), F32), V((8, width), F32),
        V((shards, MEM_PAD, width), BF), V((shards, MEM_PAD, 128), F32),
    ]
    return pl.pallas_call(
        functools.partial(forward_kernel, shards, half, width, mem, docs.shape[1]),
        out_shape=outs,
        in_specs=[any_space] * 7 + [vm] * 10 + [pl.BlockSpec(memory_space=pltpu.SMEM)],
        out_specs=[any_space] * (len(outs) - 1) + [vm],
        scratch_shapes=scratch
        + [dma((3, 2, shards)), dma((3, shards)), dma((3, 3, 2, shards)), dma((3, 3, 2, shards)), dma((2, shards))] + [dma((shards,))] * 9 + [dma((10,)), dma((len(outs),)), dma((3, shards))],
        compiler_params=pltpu.CompilerParams(collective_id=3, has_side_effects=True, vmem_limit_bytes=VMEM_LIMIT),
        name="forward_layer",
    )(
        wq.reshape(2, half, width), wk.reshape(2, half, width), wv.reshape(2, half, width), wo.reshape(2, half, width),
        hid.reshape(2, half, 4 * width), outw.reshape(4, 2, half, width), tokens, memr, *vectors, docs,
    )


def backward_kernel(shards, half, width, mem,
                    h_qkvo, h_hid, h_out, h_x, h_q, h_k, h_v, h_ctx, h_lse, h_na, h_ia, h_al, h_act, h_slope, h_nf, h_if,
                    vfull, sq, out_grad, mem_grad, docs,
                    o_qkvo, o_hid, o_out, o_x, o_mem, o_vec,
                    grad, ra, rb, rc, rd, rx, relay, rm, rv, vz, vacc,
                    wbuf, x_all, pq, pk, pv, pctx, plse, bias, s_s, dp_s, p_s, ds_s, al, abuf, sbuf, d_pre, nf, if_,
                    gr, d_out, back, d_branch, dctx, dq, dkt, dvt,
                    asem, arem, bsem, brem, csem, crem, zsem, zrem, dsem, drem, xsem, xrem, msem, mrem, vsem, vrem,
                    vzs, vzr, fsem, wsem, psem, asem_, lsem, osem):
    r, s, core, xbit, ybit, fc, fx, fy = neighbours()
    q_own, q_lo = 2 * core + ybit, 2 * core
    tok = out_grad.shape[0]
    m, n = gr.shape[0], x_all.shape[0]
    seq = tok * shards
    pairs = width // 128
    outs = (o_qkvo, o_hid, o_out)
    groups = (2, 1, 0)
    units = 3 * shards

    def turn(i):
        return lax.rem((shards - 1) * i, shards)

    def load(src, dst, i):
        c = pltpu.make_async_copy(src, dst, lsem.at[i])
        c.start()
        return c

    def w_copy(j, src):
        return pltpu.make_async_copy(src, wbuf.at[j % 4], wsem.at[j])

    def a_copy(i):
        return (
            pltpu.make_async_copy(h_act.at[turn(i)], abuf.at[lax.rem(i, 2)], asem_.at[0, i]),
            pltpu.make_async_copy(h_slope.at[turn(i)], sbuf.at[lax.rem(i, 2)], asem_.at[1, i]),
        )

    def p_copy(p, slot):
        return [
            pltpu.make_async_copy(a.at[p], b.at[slot], psem.at[i, slot])
            for i, (a, b) in enumerate(((h_q, pq), (h_k, pk), (h_v, pv), (h_lse, plse)))
        ]

    first = [load(h_nf, nf, 0), load(out_grad, gr.at[pl.ds(0, tok), :], 1), load(h_if, if_, 2)]
    for j, src in enumerate((h_out.at[0], h_hid.at[0], h_out.at[turn(1)])):
        w_copy(j, src).start()
    for c in a_copy(jnp.int32(0)):
        c.start()
    second = [load(h_al, al, 3), load(h_x, x_all, 6), load(h_ctx, pctx, 7)]
    everyone_in = enter((fc, fx, fy), r, s, shards)

    def unit_shard(u):
        return turn(lax.rem(u, shards))

    def copy_a(u):
        return remote(grad.at[u, 1 - core], ra.at[u], asem.at[u], arem.at[u], (fc, s))

    side = width // 2
    left_cols, right_cols = pl.ds(0, side), pl.ds(side, side)

    def copy_b(u):
        return (
            remote(grad.at[u, core, :, 1 - xbit, :, left_cols], rb.at[u, 0], bsem.at[u, 0], brem.at[u, 0], (fx, s)),
            remote(grad.at[u, core, 1 - ybit, :, :, right_cols], rb.at[u, 1], bsem.at[u, 1], brem.at[u, 1], (fy, s)),
        )

    def copy_c(u):
        return (
            remote(grad.at[u, core, 1 - ybit, xbit, :, left_cols], rc.at[u, 0], csem.at[u, 0], crem.at[u, 0], (fy, s)),
            remote(grad.at[u, core, ybit, 1 - xbit, :, right_cols], rc.at[u, 1], csem.at[u, 1], crem.at[u, 1], (fx, s)),
        )

    def copy_z(u):
        return remote(
            grad.at[u, core, ybit, xbit], rd.at[u // shards, s], zsem.at[u], zrem.at[u // shards, s], (r, unit_shard(u))
        )

    def start_b(u):
        copy_a(u).wait_recv()
        grad[u, core] = grad[u, core] + ra[u]
        for c in copy_b(u):
            c.start()

    def start_c(u):
        for c in copy_b(u):
            c.wait_recv()
        grad[u, core, :, xbit, :, left_cols] = grad[u, core, :, xbit, :, left_cols] + rb[u, 0]
        grad[u, core, ybit, :, :, right_cols] = grad[u, core, ybit, :, :, right_cols] + rb[u, 1]
        for c in copy_c(u):
            c.start()

    def start_z(u):
        for c in copy_c(u):
            c.wait_recv()
        grad[u, core, ybit, xbit, :, left_cols] = grad[u, core, ybit, xbit, :, left_cols] + rc[u, 0]
        grad[u, core, ybit, xbit, :, right_cols] = grad[u, core, ybit, xbit, :, right_cols] + rc[u, 1]
        pl.when(s != unit_shard(u))(lambda: copy_z(u).start())

    def hop(k, j):
        o = outs[groups[k]]
        if j == 0:
            moves = ((o.at[q_own, xbit, :, left_cols], fx), (o.at[q_own, xbit, :, right_cols], fy))
        elif j == 1:
            moves = ((o.at[q_own, :, :, left_cols], fy), (o.at[pl.ds(q_lo, 2), xbit, :, right_cols], fx))
        else:
            moves = ((o.at[pl.ds(q_lo, 2)], fc),)
        return [remote(a, a, dsem.at[k, j, i], drem.at[k, j, i], (dev, s)) for i, (a, dev) in enumerate(moves)]

    def hop_start(k, j):
        for c in hop(k, j):
            c.start()

    def hop_wait(k, j):
        for c in hop(k, j):
            c.wait_recv()

    def finish_group(k):
        total = grad[k * shards + turn(s), core, ybit, xbit].astype(F32)
        for t in range(1, shards):
            other = lax.rem(s + t, shards)
            slot = rd.at[k, other]
            remote(slot, slot, zsem.at[0], zrem.at[k, other], (r, s)).wait_recv()
            total = total + rd[k, other].astype(F32)
        fin = ra.at[k * shards, 0, 0]
        fin[...] = total.astype(BF)
        c = pltpu.make_async_copy(fin, outs[groups[k]].at[q_own, xbit], fsem.at[k])
        c.start()
        c.wait()
        hop_start(k, 0)

    def hop_step(k, j):
        hop_wait(k, j - 1)
        hop_start(k, j)

    lag = 2
    steps = []
    for when, j, k in ((10, 0, 0), (11, 1, 0), (12, 2, 0), (14, 0, 1), (15, 1, 1), (16, 0, 2), (16, 2, 1), (17, 1, 2), (18, 2, 2)):
        steps.append((when, functools.partial(hop_step, k, j) if j else functools.partial(finish_group, k)))
    ticks = max(when for when, fn in steps) + 1

    def tick(i):
        def guarded(lo, fn):
            pl.when((i >= lo) & (i < lo + units))(lambda: fn(i - lo))

        guarded(0, start_b)
        guarded(lag, start_c)
        guarded(2 * lag, start_z)

    def late_tick(i):
        tick(jnp.int32(i))
        for when, fn in steps:
            if when == i:
                fn()

    def vrow(i):
        return vfull[pl.ds(i, 1), :]

    index = lax.broadcasted_iota(jnp.int32, (m, 1), 0)
    once = jnp.where((index < tok) | ((index < tok + mem) & (s == 0)), 1.0, 0.0)

    def add_sum(i, rw, value):
        total = jnp.sum(value * once[rw.start : rw.start + LOG_ROWS], axis=0, keepdims=True)
        vacc[0, pl.ds(i, 1), :] = vacc[0, pl.ds(i, 1), :] + total

    def mean(v):
        return jnp.mean(v, axis=1, keepdims=True)

    def norm_back_rows(e, normed, inverse):
        return inverse * (e - mean(e) - normed * mean(e * normed))

    vacc[0] = jnp.zeros(vacc.shape[1:], F32)
    for c in first:
        c.wait()
    gr[pl.ds(tok, mem), :] = mem_grad[:, 0, :]
    gr[pl.ds(tok + mem, MEM_PAD - mem), :] = jnp.zeros((MEM_PAD - mem, width), F32)
    for rw in row_blocks(m):
        g, normed = gr[rw, :], nf[rw, :]
        add_sum(6, rw, g * normed)
        add_sum(7, rw, g)
        v = norm_back_rows(g * vrow(6), normed, if_[rw, :1])
        back[rw, :] = v
        low = v.astype(BF)
        add_sum(3, rw, low.astype(F32))
        d_out[rw, :] = low
    na, ia = nf, if_
    second += [load(h_na, na, 4), load(h_ia, ia, 5)]
    second[0].wait()
    once_low = once.astype(BF)

    def turned(a, b):
        return dot(a, b, TN)

    def put(k, q, j, value):
        value = value.astype(BF).reshape(2, 2, half, width)
        for i in range(2):
            unit = k * shards + (shards - 1) * (2 * j + i) % shards
            grad[unit, q // 2, q % 2] = value[i]

    wide = 2 * 2 * half
    def feed_forward(i):
        q = turn(i)
        even = 2 * lax.rem(i, 2)
        for c in a_copy(i):
            c.wait()

        @pl.when(i + 1 < 4)
        def _():
            for c in a_copy(i + 1):
                c.start()

        w_copy(2 * i, h_out.at[q]).wait()
        pl.when(i < 3)(lambda: w_copy(2 * i + 3, h_hid.at[turn(i + 1)]).start())
        pl.when(i == 3)(lambda: w_copy(9, h_qkvo.at[1]).start())
        slot = lax.rem(i, 2)
        do = d_out[...] * once_low
        for j in range(2):
            value = turned(abuf[slot, :, j * wide : (j + 1) * wide], do)
            grad[i, j] = value.astype(BF).reshape(2, 2, half, width)
        pl.when(i == 0)(everyone_in)
        copy_a(i).start()
        for j in range(2):
            wt = wbuf[even, 2 * j : 2 * j + 2].reshape(wide, width)
            s_s[:, j * wide : (j + 1) * wide] = dot(d_out[...], wt, NT)
        for rw in row_blocks(m):
            v = s_s[rw, :width] * sbuf[slot, rw, :]
            low = v.astype(BF)
            d_pre[rw, :] = low
            add_sum(8 + q, rw, low.astype(F32))
        w_copy(2 * i + 1, h_hid.at[q]).wait()
        pl.when(i < 2)(lambda: w_copy(2 * i + 4, h_out.at[turn(i + 2)]).start())
        pl.when(i == 2)(lambda: w_copy(8, h_qkvo.at[3]).start())
        pl.when(i == 3)(lambda: w_copy(10, h_qkvo.at[2]).start())
        dp = d_pre[...] * once_low
        for j in range(2):
            value = turned(al[:, j * wide : (j + 1) * wide], dp).astype(BF).reshape(2, 2, half, width)
            for k in range(2):
                unit = shards + (shards - 1) * (2 * j + k) % shards
                grad[unit, q // 2, lax.rem(q, 2)] = value[k]
        for j in range(2):
            wt = wbuf[even + 1, 2 * j : 2 * j + 2].reshape(wide, width)
            s_s[:, j * wide : (j + 1) * wide] = dot(d_pre[...], wt, NT)
        for rw in row_blocks(m):
            back[rw, :] = back[rw, :] + s_s[rw, :width]
        tick(i)

    pl.loop(0, 4)(feed_forward)
    for j in range(shards):
        copy_a(shards + j).start()
    for c in p_copy(0, 0):
        c.start()

    for c in second[1:]:
        c.wait()

    for rw in row_blocks(m):
        f, normed = back[rw, :], na[rw, :]
        add_sum(4, rw, f * normed)
        add_sum(5, rw, f)
        v = norm_back_rows(f * vrow(4), normed, ia[rw, :1])
        back[rw, :] = v
        low = v.astype(BF)
        d_branch[rw, :] = low
        add_sum(2, rw, low.astype(F32))
        d_out[rw, :] = pctx[rw, :].astype(BF)
    write_bias(bias, docs, docs.shape[1], s, tok, seq, mem)
    w_copy(8, h_qkvo.at[3]).wait()
    w_copy(11, h_qkvo.at[0]).start()
    db = d_branch[...] * once_low
    for j in range(2):
        put(2, 3, j, turned(d_out[:, j * wide : (j + 1) * wide], db))
    for j in range(2):
        wt = wbuf[0, 2 * j : 2 * j + 2].reshape(wide, width)
        value = dot(d_branch[...], wt, NT).astype(BF)
        for i in range(wide // 128):
            dctx[j * (wide // 128) + i] = value[:, i * 128 : (i + 1) * 128]
    lane = lax.broadcasted_iota(jnp.int32, (m, 128), 1)
    lane_k = lax.broadcasted_iota(jnp.int32, (n, 128), 1)
    tick(jnp.int32(4))

    def pair(p):
        slot = lax.rem(p, 2)
        for c in p_copy(p, slot):
            c.wait()

        @pl.when(p + 1 < pairs)
        def _():
            for c in p_copy(p + 1, 1 - slot):
                c.start()

        c = pl.ds(pl.multiple_of(p * 128, 128), 128)
        part_q, part_k, part_v = None, None, None
        zero = jnp.zeros((m, 128), BF)
        for head in range(2):
            mine = (lane < HD) == (head == 0)
            qh = jnp.where(mine, pq[slot], zero)
            doh = jnp.where(mine, dctx[p], zero)
            s_s[...] = dot(qh, pk[slot], NT)
            dp_s[...] = dot(doh, pv[slot], NT)
            for rw in row_blocks(m):
                sub = slice(rw.start, rw.start + LOG_ROWS)
                delta = jnp.sum(doh[sub].astype(F32) * pctx[rw, c], axis=1, keepdims=True)
                top = plse[slot, rw, head * HD : head * HD + 1]
                probs = jnp.exp(s_s[rw, :] + bias[rw, :] - top)
                p_s[rw, :] = probs.astype(BF)
                ds_s[rw, :] = (probs * (dp_s[rw, :] - delta)).astype(BF)
            kh = jnp.where((lane_k < HD) == (head == 0), pk[slot], jnp.zeros((n, 128), BF))
            a = dot(ds_s[...], kh)
            b = turned(qh, ds_s[...])
            d = turned(doh, p_s[...])
            part_q = a if head == 0 else part_q + a
            part_k = b if head == 0 else part_k + b
            part_v = d if head == 0 else part_v + d
        dq[:, c] = (part_q * 0.125).astype(BF)
        dkt[c, :] = part_k.astype(BF)
        dvt[c, :] = part_v.astype(BF)
        pl.when(lax.rem(p, 2) == 1)(lambda: tick(5 + p // 2))

    pl.loop(0, pairs)(pair)

    ones = jnp.ones((8, n), BF)
    vacc[0, pl.ds(1, 1), :] = dot(ones, dvt[...], NT)[:1]
    vacc[0, pl.ds(0, 1), :] = jnp.sum(dq[...].astype(F32), axis=0, keepdims=True)
    vacc[0, pl.ds(12, 3), :] = sq[pl.ds(0, 3), :]
    rv_first = remote(vacc.at[0], rv.at[0], vsem.at[0], vrem.at[0], (fc, s))
    rv_first.start()
    def vec_hop(k):
        return remote(vacc.at[k], rv.at[k], vsem.at[k], vrem.at[k], ((fc, fx, fy)[k], s))

    def vec_step(k):
        vec_hop(k - 1).wait_recv()
        vacc[k] = vacc[k - 1] + rv[k - 1]
        vec_hop(k).start()

    w_copy(9, h_qkvo.at[1]).wait()
    w_copy(10, h_qkvo.at[2]).wait()
    wkm = wbuf[1].reshape(width, width)
    wvm = wbuf[2].reshape(width, width)
    spare = (abuf.at[0, pl.ds(0, tok)], abuf.at[1, pl.ds(0, tok)], d_pre.at[pl.ds(0, tok)])
    small = []

    def to_shard(src, dst, ssem, rsem, t):
        return remote(src, dst.at[s], ssem.at[t], rsem.at[s], (r, lax.rem(s + t, shards)))

    def row_grads(blk):
        c = pl.ds(pl.multiple_of(blk * tok, tok), tok)
        return jnp.transpose(dot(wkm, dkt[:, c]) + dot(wvm, dvt[:, c]))

    def along(src, dst, i, up):
        return remote(src, dst, xsem.at[i], xrem.at[i], (r, s + 1 if up else s - 1))

    far = (along(spare[0], relay.at[0], 0, True), along(spare[0], relay.at[1], 1, False))
    near = (along(spare[1], rx.at[0], 2, True), along(spare[2], rx.at[1], 3, False))
    has_far = (s < 2, s >= 2)
    has_near = (s < shards - 1, s > 0)
    has_relay = (s > 0, s < shards - 1)
    spare[0][...] = row_grads(lax.rem(s + 2, shards)).astype(BF)
    for i in range(2):
        pl.when(has_far[i])(far[i].start)
    for j in range(2):
        xs_ = x_all[:, j * wide : (j + 1) * wide]
        x_own = jnp.concatenate([
            x_all[pl.ds(pl.multiple_of(s * tok, tok), tok), j * wide : (j + 1) * wide],
            x_all[pl.ds(seq, MEM_PAD), j * wide : (j + 1) * wide],
        ])
        put(2, 0, j, turned(x_own, dq[...]))
        xt = jnp.transpose(xs_)
        put(2, 1, j, dot(xt, dkt[...], NT))
        put(2, 2, j, dot(xt, dvt[...], NT))
        pass
    for j in range(shards):
        copy_a(2 * shards + j).start()
    tick(jnp.int32(8))

    vec_step(1)
    tick(jnp.int32(9))
    for i in range(2):
        @pl.when(has_near[i])
        def _():
            spare[1 + i][...] = row_grads(s + 1 - 2 * i).astype(BF)

            @pl.when(has_relay[i])
            def _():
                along(spare[0], relay.at[i], i, i == 0).wait_recv()
                spare[1 + i][...] = (spare[1 + i][...].astype(F32) + relay[i].astype(F32)).astype(BF)

            near[i].start()

        if i == 0:
            late_tick(10)
    own_rows = pl.ds(0, tok)
    back[own_rows, :] = back[own_rows, :] + row_grads(s)
    value = dot(wkm, dkt[:, pl.ds(seq, MEM_KEYS)]) + dot(wvm, dvt[:, pl.ds(seq, MEM_KEYS)])
    w_copy(11, h_qkvo.at[0]).wait()
    mrows = pl.ds(tok, MEM_PAD)
    value = jnp.transpose(value)[:MEM_PAD] + dot(dq[mrows, :], wbuf[3].reshape(width, width), NT)
    rm[s] = value.astype(BF)
    for t in range(1, shards):
        small.append(remote(rm.at[s], rm.at[s], msem.at[t], mrem.at[s], (r, lax.rem(s + t, shards))))
        small[-1].start()
    vec_step(2)
    for j in range(2):
        wt = wbuf[3, 2 * j : 2 * j + 2].reshape(wide, width)
        c = pl.ds(j * wide, wide)
        back[own_rows, c] = back[own_rows, c] + dot(dq[own_rows, :], wt, NT)
    vec_hop(2).wait_recv()
    vz[s] = vacc[2] + rv[2]
    for t in range(1, shards):
        small.append(to_shard(vz.at[s], vz, vzs, vzr, t))
        small[-1].start()
    for i in range(11, ticks):
        late_tick(i)

    for t in range(1, shards):
        other = lax.rem(s + t, shards)
        for buf, rsem in ((rm, mrem), (vz, vzr)):
            remote(buf.at[other], buf.at[other], msem.at[0], rsem.at[other], (r, s)).wait_recv()
    for i in range(2):
        @pl.when(has_relay[i])
        def _():
            along(spare[0], rx.at[i], 2 + i, i == 0).wait_recv()
            back[own_rows, :] = back[own_rows, :] + rx[i].astype(F32)

    sx, sm, sv = back[own_rows, :], back[mrows, :], vz[0]
    for t in range(shards):
        sm = sm + rm[t].astype(F32)
        if t:
            sv = sv + vz[t]
    gr[pl.ds(0, tok), :] = sx
    o_mem[:, 0, :] = sm[:mem]
    final = [
        pltpu.make_async_copy(gr.at[pl.ds(0, tok), :], o_x, osem.at[0]),
    ]
    for c in final:
        c.start()
    o_vec[...] = sv
    for k in range(3):
        hop_wait(k, 2)
    for c in final:
        c.wait()

    @pl.loop(0, units)
    def _(u):
        copy_a(u).wait_send()
        for c in copy_b(u) + copy_c(u):
            c.wait_send()
        pl.when(s != unit_shard(u))(lambda: copy_z(u).wait_send())

    for k in range(3):
        for j in range(3):
            for c in hop(k, j):
                c.wait_send()
    for c in small:
        c.wait_send()
    for i in range(2):
        pl.when(has_far[i])(far[i].wait_send)
        pl.when(has_near[i])(near[i].wait_send)
    for k in range(3):
        vec_hop(k).wait_send()


def backward_all(saved, out_grad, mem_grad, docs):
    shards = lax.axis_size("shard")
    tok, width = out_grad.shape
    mem = mem_grad.shape[0]
    half = saved[0].shape[3]
    m, n = tok + MEM_PAD, tok * shards + MEM_KEYS
    pairs = width // 128
    any_space = pl.BlockSpec(memory_space=pl.ANY)
    vm = pl.BlockSpec(memory_space=pltpu.VMEM)
    dma = pltpu.SemaphoreType.DMA
    V = pltpu.VMEM
    units = 3 * shards
    piece4 = (4, 2, half, width)
    outs = tuple(jax.ShapeDtypeStruct(piece4, BF) for _ in range(3)) + (
        jax.ShapeDtypeStruct((tok, width), F32),
        jax.ShapeDtypeStruct((mem, 1, width), F32),
        jax.ShapeDtypeStruct((16, width), F32),
    )
    big = (4, 2, half, width)
    scratch = [
        V((units, 2, 2, 2, half, width), BF), V((units, 2, 2, half, width), BF), V((units, 2, 2, half, width // 2), BF),
        V((units, 2, half, width // 2), BF), V((3, shards, half, width), BF), V((2, tok, width), BF), V((2, tok, width), BF),
        V((shards, MEM_PAD, width), BF), V((3, 16, width), F32), V((shards, 16, width), F32), V((3, 16, width), F32),
        V((4,) + big, BF), V((n, width), BF), V((2, m, 128), BF), V((2, n, 128), BF), V((2, n, 128), BF),
        V((m, width), F32), V((2, m, 128), F32), V((m, n), F32), V((m, n), F32), V((m, n), F32), V((m, n), BF),
        V((m, n), BF), V((m, width), BF), V((2, m, width), BF),
        V((2, m, width), F32), V((m, width), BF), V((m, width), F32), V((m, 128), F32), V((m, width), F32),
        V((m, width), BF), V((m, width), F32), V((m, width), BF), V((pairs, m, 128), BF), V((m, width), BF),
        V((width, n), BF), V((width, n), BF),
    ]
    sems = (
        [dma((units,))] * 2 + [dma((units, 2))] * 4 + [dma((units,)), dma((3, shards))]
        + [dma((3, 3, 2)), dma((3, 3, 2)), dma((shards,)), dma((shards,)), dma((shards,)), dma((shards,))]
        + [dma((3,)), dma((3,)), dma((shards,)), dma((shards,)), dma((3,)), dma((12,)), dma((4, 2)), dma((2, 4))]
        + [dma((8,)), dma((1,))]
    )
    return pl.pallas_call(
        functools.partial(backward_kernel, shards, half, width, mem),
        out_shape=outs,
        in_specs=[any_space] * 16 + [vm, vm, any_space, vm, pl.BlockSpec(memory_space=pltpu.SMEM)],
        out_specs=[any_space] * 4 + [vm, vm],
        scratch_shapes=scratch + sems,
        compiler_params=pltpu.CompilerParams(collective_id=4, has_side_effects=True, vmem_limit_bytes=VMEM_LIMIT),
        name="backward_layer",
    )(*saved, out_grad, mem_grad, docs)


def plain_body(tokens, memory_rows, doc_lengths, w_query, w_key, w_value, w_attn_out, w_hidden, w_output,
         b_query, b_value, b_attn_out, b_hidden, b_output, gain_attn, shift_attn, gain_ffn, shift_ffn,
         out_grad, memory_grad):
    tok, width = tokens.shape
    mem = memory_rows.shape[1]
    shards = lax.axis_size("shard")
    s = lax.axis_index("shard")
    seq = tok * shards
    srows = w_query.shape[0]
    m = tok + MEM_PAD
    n = seq + MEM_KEYS
    scaling = 1.0 / math.sqrt(HD)

    vec = jnp.concatenate(
        [v.reshape(-1, srows) for v in (
            b_query, b_value, b_attn_out, b_output, gain_attn, shift_attn, gain_ffn, shift_ffn, b_hidden
        )]
        + [jnp.zeros((4, srows), BF)]
    )
    vec = lax.dynamic_update_slice(jnp.zeros((16, width), BF), vec, (0, s * srows))
    rows = jnp.concatenate([tokens, memory_rows[0], jnp.zeros((MEM_PAD - mem, width), F32)])
    low_rows = rows.astype(BF)
    qkvo = jnp.stack([w_query, w_key, w_value, w_attn_out])
    qkvo, w_hid, w_out, x_tok, vec_all = gather_plain(qkvo, w_hidden, w_output, low_rows[:tok], vec)
    vec = jnp.sum(vec_all.astype(F32), axis=0)
    bq, bv, bo, bout, ga, sa, gf, sf = (vec[i] for i in range(8))
    bh = jnp.transpose(vec[8:12].reshape(4, shards, srows), (1, 0, 2)).reshape(4 * width)

    doc_ends = jnp.cumsum(doc_lengths[0])
    seg = jnp.sum((jnp.arange(seq, dtype=jnp.int32)[:, None] >= doc_ends[None, :]).astype(jnp.int32), axis=1)
    place = jnp.arange(MEM_KEYS, dtype=jnp.int32)
    mem_seg = jnp.where(place < mem // 2, -1, jnp.where(place < mem, -3, -4)).astype(jnp.int32)
    kseg = jnp.concatenate([seg, mem_seg])[None, :]
    qseg = jnp.concatenate(
        [lax.dynamic_slice_in_dim(seg, s * tok, tok), jnp.full((MEM_PAD,), -2, jnp.int32)]
    )[:, None]
    index = jnp.arange(m, dtype=jnp.int32)[:, None]
    once = jnp.where(index < tok, 1.0, jnp.where((index < tok + mem) & (s == 0), 1.0, 0.0)).astype(F32)
    once_low = once.astype(BF)

    x_all = jnp.concatenate([x_tok, low_rows[tok:], jnp.zeros((MEM_KEYS - MEM_PAD, width), BF)])
    query = (jnp.dot(low_rows, qkvo[0], preferred_element_type=F32) + bq).astype(BF)
    keys = jnp.dot(x_all, qkvo[1], preferred_element_type=F32).astype(BF)
    values = (jnp.dot(x_all, qkvo[2], preferred_element_type=F32) + bv).astype(BF)
    context, lse = attention(query, keys, values, qseg, kseg, scaling)
    context_low = context.astype(BF)
    branch = jnp.dot(context_low, qkvo[3], preferred_element_type=F32) + bo
    normed_attn, inverse_attn = layer_stats(rows + branch)
    after_attn = normed_attn * ga + sa
    after_low = after_attn.astype(BF)
    pre_act = jnp.concatenate([jnp.dot(after_low, w_hid[q], preferred_element_type=F32) for q in range(4)], axis=1) + bh
    half_erf = 0.5 * (1.0 + lax.erf(pre_act * GELU_ROOT))
    act_low = (pre_act * half_erf).astype(BF)
    second = jnp.dot(act_low, w_out, preferred_element_type=F32) + bout
    normed_ffn, inverse_ffn = layer_stats(after_attn + second)
    result = normed_ffn * gf + sf

    grads = jnp.concatenate([out_grad, memory_grad[0], jnp.zeros((MEM_PAD - mem, width), F32)])
    back_ffn = norm_back(grads * gf, normed_ffn, inverse_ffn)
    d_output = back_ffn.astype(BF)
    g_out = jnp.einsum("rf,rd->fd", act_low * once_low, d_output, preferred_element_type=F32).astype(BF)
    d_act = jnp.einsum("rd,fd->rf", d_output, w_out, preferred_element_type=F32)
    d_pre = (d_act * (half_erf + pre_act * jnp.exp(-0.5 * pre_act * pre_act) * GELU_DENSITY)).astype(BF)
    after_once = after_low * once_low
    g_hid = jnp.stack(
        [jnp.einsum("rd,rf->df", after_once, d_pre[:, q * width : (q + 1) * width], preferred_element_type=F32).astype(BF)
         for q in range(4)]
    )
    back_first = back_ffn + sum(
        jnp.einsum("rf,df->rd", d_pre[:, q * width : (q + 1) * width], w_hid[q], preferred_element_type=F32)
        for q in range(4)
    )
    back_attn = norm_back(back_first * ga, normed_attn, inverse_attn)
    d_branch = back_attn.astype(BF)
    d_context = jnp.einsum("re,de->rd", d_branch, qkvo[3], preferred_element_type=F32).astype(BF)
    dq, dkt, dvt = attention_back(query, keys, values, qseg, kseg, once, context, lse, d_context, scaling)
    g_qkvo = jnp.stack([
        jnp.einsum("rd,re->de", low_rows * once_low, dq, preferred_element_type=F32).astype(BF),
        jnp.einsum("rd,er->de", x_all, dkt, preferred_element_type=F32).astype(BF),
        jnp.einsum("rd,er->de", x_all, dvt, preferred_element_type=F32).astype(BF),
        jnp.einsum("rd,re->de", context_low * once_low, d_branch, preferred_element_type=F32).astype(BF),
    ])
    dx = jnp.einsum("er,de->rd", dkt, qkvo[1], preferred_element_type=F32) + jnp.einsum(
        "er,de->rd", dvt, qkvo[2], preferred_element_type=F32
    )
    base = back_attn + jnp.einsum("re,de->rd", dq, qkvo[0], preferred_element_type=F32)

    def over_rows(terms):
        return jnp.sum(once * terms, axis=0)

    gb_hidden = over_rows(d_pre.astype(F32)).reshape(shards, 4, srows).transpose(1, 0, 2).reshape(4, width)
    squares = jnp.stack([jnp.sum(v[:tok] * v[:tok]) for v in (result, branch, second)])
    vec_grads = jnp.concatenate([
        jnp.stack([
            over_rows(dq.astype(F32)),
            jnp.sum(dvt.astype(F32), axis=1),
            over_rows(d_branch.astype(F32)),
            over_rows(d_output.astype(F32)),
            over_rows(back_first * normed_attn),
            over_rows(back_first),
            over_rows(grads * normed_ffn),
            over_rows(grads),
        ]),
        gb_hidden,
        jnp.pad(squares[None], ((0, 3), (0, width - 3))),
    ])
    g_qkvo, g_hid, g_out, dx_own, dx_mem, vec_sum = reduce_plain(
        g_qkvo, g_hid, g_out, dx[:seq].astype(BF), dx[seq : seq + MEM_PAD], vec_grads
    )
    own = lax.dynamic_slice(vec_sum, (0, s * srows), (12, srows))
    rms = jnp.sqrt(vec_sum[12, :3] / float(seq * width * lax.axis_size("replica")))
    g_qkvo = g_qkvo.astype(F32)
    grad_hidden = jnp.concatenate([g_hid[q] for q in range(4)], axis=1).astype(F32)
    return (
        result[:tok],
        result[tok : tok + mem][None],
        base[:tok] + dx_own,
        (base[tok : tok + mem] + dx_mem[:mem])[None],
        g_qkvo[0],
        g_qkvo[1],
        g_qkvo[2],
        g_qkvo[3],
        grad_hidden,
        g_out.astype(F32),
        own[0],
        own[1],
        own[2],
        own[8:12].reshape(-1),
        own[3],
        own[4],
        own[5],
        own[6],
        own[7],
        rms[0],
        rms[1],
        rms[2],
    )


def direct_body(tokens, memory_rows, doc_lengths, w_query, w_key, w_value, w_attn_out, w_hidden, w_output,
                b_query, b_value, b_attn_out, b_hidden, b_output, gain_attn, shift_attn, gain_ffn, shift_ffn,
                out_grad, memory_grad):
    tok, width = tokens.shape
    shards = lax.axis_size("shard")
    s = lax.axis_index("shard")
    srows = w_query.shape[0]
    vectors = (b_query, b_value, b_attn_out, b_output, gain_attn, shift_attn, gain_ffn, shift_ffn, b_hidden)
    *saved, result, vec_full, squares, result_mem = forward_all(
        w_query, w_key, w_value, w_attn_out, w_hidden, w_output, tokens, jnp.transpose(memory_rows, (1, 0, 2)), vectors, doc_lengths
    )
    g_qkvo, g_hid, g_out, grad_rows, grad_mem, vec_sum = backward_all(
        tuple(saved) + (vec_full, squares), out_grad, jnp.transpose(memory_grad, (1, 0, 2)), doc_lengths
    )
    own = lax.dynamic_slice(vec_sum, (0, s * srows), (8, srows))
    own_hid = lax.dynamic_slice(vec_sum, (8 + s, 0), (1, width))[0]
    count = float(tok * shards * width * lax.axis_size("replica"))
    rms = jnp.sqrt(jnp.sum(vec_sum[12:15], axis=1) / count)
    g_qkvo = g_qkvo.reshape(4, srows, width).astype(F32)
    g_hid = g_hid.reshape(4, srows, width)
    return (
        result,
        jnp.transpose(result_mem, (1, 0, 2)),
        grad_rows,
        jnp.transpose(grad_mem, (1, 0, 2)),
        g_qkvo[0],
        g_qkvo[1],
        g_qkvo[2],
        g_qkvo[3],
        jnp.concatenate([g_hid[q] for q in range(4)], axis=1).astype(F32),
        g_out.reshape(4 * srows, width).astype(F32),
        own[0],
        own[1],
        own[2],
        own_hid,
        own[3],
        own[4],
        own[5],
        own[6],
        own[7],
        rms[0],
        rms[1],
        rms[2],
    )


def solution(mesh):
    direct = mesh.shape["replica"] == 8 and mesh.shape["shard"] == 4
    shard1, shard2 = P("shard"), P("shard", None)
    both, rep3 = P(("replica", "shard"), None), P("replica", None, None)
    return jax.shard_map(
        direct_body if direct else plain_body,
        mesh=mesh,
        in_specs=(both, rep3, P("replica", None)) + (shard2,) * 6 + (shard1,) * 9 + (both, rep3),
        out_specs=(both, rep3, both, rep3) + (shard2,) * 6 + (shard1,) * 9 + (P(), P(), P()),
        check_vma=False,
    )
```

```python
import functools
import math

import jax
import jax.numpy as jnp
from jax import lax
from jax.experimental import pallas as pl
from jax.experimental.pallas import tpu as pltpu
from jax.sharding import PartitionSpec as P

H = 12
HD = 64
EPSILON = 1e-12
GELU_ROOT = 0.7071067811865476
GELU_DENSITY = 0.3989422804014327
MESH = pl.DeviceIdType.MESH
BF = jnp.bfloat16
F32 = jnp.float32
MEM_PAD = 32
MEM_KEYS = 128
VMEM_LIMIT = 60 << 20
NEG = -1e30


def region(ref, group, sh, q0, nq, h0, nh, cols=None):
    hs = h0 if nh == 1 else pl.ds(h0, nh)
    qs = q0 if nq == 1 else pl.ds(q0, nq)
    tail = () if cols is None else (slice(None), cols)
    return ref.at[((sh, qs, hs) if group == 2 else (qs, sh, hs)) + tail]


def neighbours():
    r = lax.axis_index("replica")
    s = lax.axis_index("shard")
    core, xbit, ybit = r % 2, (r // 2) % 2, (r // 4) % 2
    return r, s, core, xbit, ybit, r + 1 - 2 * core, r + 2 - 4 * xbit, r + 4 - 8 * ybit


def enter(peers, r, s, shards):
    sem = pltpu.get_barrier_semaphore()
    for p in peers:
        pl.semaphore_signal(sem, 1, device_id=(p, s), device_id_type=MESH)
    for t in range(1, shards):
        pl.semaphore_signal(sem, 1, device_id=(r, lax.rem(s + t, shards)), device_id_type=MESH)
    return lambda: pl.semaphore_wait(sem, len(peers) + shards - 1)


def remote(src, dst, ssem, rsem, dev):
    return pltpu.make_async_remote_copy(
        src_ref=src, dst_ref=dst, send_sem=ssem, recv_sem=rsem, device_id=dev, device_id_type=MESH
    )


def gather_plain(qkvo, hid, outw, xtok, vec):
    width = qkvo.shape[2]
    full = functools.partial(lax.all_gather, axis_name="shard", tiled=True)
    hid = full(hid, axis=0)
    return (
        full(qkvo, axis=1),
        jnp.stack([hid[:, q * width : (q + 1) * width] for q in range(4)]),
        full(outw, axis=0),
        full(xtok, axis=0),
        lax.all_gather(vec, "shard", axis=0),
    )


def reduce_plain(g_qkvo, g_hid, g_out, dx, mem, vec):
    scatter = functools.partial(lax.psum_scatter, axis_name="shard", tiled=True)
    return (
        lax.psum(scatter(g_qkvo, scatter_dimension=1), "replica"),
        lax.psum(scatter(g_hid, scatter_dimension=1), "replica"),
        lax.psum(scatter(g_out, scatter_dimension=0), "replica"),
        scatter(dx, scatter_dimension=0).astype(F32),
        lax.psum(mem, "shard"),
        lax.psum(vec, ("replica", "shard")),
    )


NT = (((1,), (1,)), ((), ()))
NN = (((1,), (0,)), ((), ()))
TN = (((0,), (0,)), ((), ()))


def dot(a, b, dims=NN):
    return lax.dot_general(a, b, dims, preferred_element_type=F32)


def head_lanes(shape, head):
    lane = lax.broadcasted_iota(jnp.int32, shape, 1)
    return (lane < HD) if head == 0 else (lane >= HD)


def mask_bias(qseg, kseg):
    allowed = (qseg == kseg) | (kseg == -1) | ((qseg == -2) & (kseg != -4))
    return jnp.where(allowed, 0.0, NEG)


def attend_kernel(scaling, q_ref, k_ref, v_ref, qseg_ref, kseg_ref, ctx_ref, lse_ref, bias_ref):
    @pl.when(pl.program_id(0) == 0)
    def _():
        bias_ref[...] = mask_bias(qseg_ref[...], kseg_ref[...])

    q, k, v = q_ref[...], k_ref[...], v_ref[...]
    zero_q = jnp.zeros_like(q)
    contexts, totals = [], []
    for head in range(2):
        qh = jnp.where(head_lanes(q.shape, head), q, zero_q)
        scores = dot(qh, k, NT) * scaling + bias_ref[...]
        top = jnp.max(scores, axis=1, keepdims=True)
        powers = jnp.exp(scores - top)
        lse = top + jnp.log(jnp.sum(powers, axis=1, keepdims=True))
        probs = powers * jnp.exp(top - lse)
        contexts.append(dot(probs.astype(BF), v))
        totals.append(lse)
    first = head_lanes(q.shape, 0)
    ctx_ref[...] = jnp.where(first, contexts[0], contexts[1])
    lse_ref[...] = jnp.where(first, totals[0], totals[1])


def attend_back_kernel(scaling, q_ref, k_ref, v_ref, qseg_ref, kseg_ref, weight_ref, ctx_ref, lse_ref, do_ref,
                       dq_ref, dk_ref, dv_ref, bias_ref):
    @pl.when(pl.program_id(0) == 0)
    def _():
        bias_ref[...] = mask_bias(qseg_ref[...], kseg_ref[...])

    q, k, v, do = q_ref[...], k_ref[...], v_ref[...], do_ref[...]
    weight = weight_ref[...] > 0
    dq, dk, dv = None, None, None
    for head in range(2):
        lanes = head_lanes(q.shape, head)
        qh = jnp.where(lanes, q, jnp.zeros_like(q))
        doh = jnp.where(lanes, do, jnp.zeros_like(do))
        lse = lse_ref[:, head * HD : head * HD + 1]
        scores = dot(qh, k, NT) * scaling + bias_ref[...]
        probs = jnp.exp(scores - lse)
        delta = jnp.sum(doh.astype(F32) * ctx_ref[...], axis=1, keepdims=True)
        d_scores = (probs * (dot(doh, v, NT) - delta)).astype(BF)
        kh = jnp.where(head_lanes(k.shape, head), k, jnp.zeros_like(k))
        part_q = dot(d_scores, kh)
        part_k = dot(jnp.where(weight, qh, jnp.zeros_like(qh)), d_scores, TN)
        part_v = dot(jnp.where(weight, doh, jnp.zeros_like(doh)), probs.astype(BF), TN)
        dq = part_q if dq is None else dq + part_q
        dk = part_k if dk is None else dk + part_k
        dv = part_v if dv is None else dv + part_v
    dq_ref[...] = (dq * scaling).astype(BF)
    dk_ref[...] = (dk * scaling).astype(BF)
    dv_ref[...] = dv.astype(BF)


def attention(query, keys, values, qseg, kseg, scaling):
    m, width = query.shape
    n = keys.shape[0]
    rows = pl.BlockSpec((m, 2 * HD), lambda i: (0, i))
    cols = pl.BlockSpec((n, 2 * HD), lambda i: (0, i))
    return pl.pallas_call(
        functools.partial(attend_kernel, scaling),
        grid=(width // (2 * HD),),
        out_shape=(jax.ShapeDtypeStruct((m, width), F32), jax.ShapeDtypeStruct((m, width), F32)),
        in_specs=[rows, cols, cols, pl.BlockSpec((m, 1), lambda i: (0, 0)), pl.BlockSpec((1, n), lambda i: (0, 0))],
        out_specs=[rows, rows],
        scratch_shapes=[pltpu.VMEM((m, n), F32)],
        compiler_params=pltpu.CompilerParams(vmem_limit_bytes=VMEM_LIMIT),
        name="attend",
    )(query, keys, values, qseg, kseg)


def attention_back(query, keys, values, qseg, kseg, weight, context, lse, d_context, scaling):
    m, width = query.shape
    n = keys.shape[0]
    rows = pl.BlockSpec((m, 2 * HD), lambda i: (0, i))
    cols = pl.BlockSpec((n, 2 * HD), lambda i: (0, i))
    turned = pl.BlockSpec((2 * HD, n), lambda i: (i, 0))
    column = pl.BlockSpec((m, 1), lambda i: (0, 0))
    return pl.pallas_call(
        functools.partial(attend_back_kernel, scaling),
        grid=(width // (2 * HD),),
        out_shape=(
            jax.ShapeDtypeStruct((m, width), BF),
            jax.ShapeDtypeStruct((width, n), BF),
            jax.ShapeDtypeStruct((width, n), BF),
        ),
        in_specs=[rows, cols, cols, column, pl.BlockSpec((1, n), lambda i: (0, 0)), column, rows, rows, rows],
        out_specs=[rows, turned, turned],
        scratch_shapes=[pltpu.VMEM((m, n), F32)],
        compiler_params=pltpu.CompilerParams(vmem_limit_bytes=VMEM_LIMIT),
        name="attend_back",
    )(query, keys, values, qseg, kseg, weight, context, lse, d_context)


def layer_stats(totals):
    center = totals - jnp.mean(totals, axis=-1, keepdims=True)
    spread = jnp.mean(center * center, axis=-1, keepdims=True)
    inverse = lax.rsqrt(spread + EPSILON)
    return (center * inverse, inverse)


def norm_back(grad_normed, normed, inverse):
    return inverse * (
        grad_normed
        - jnp.mean(grad_normed, axis=-1, keepdims=True)
        - normed * jnp.mean(grad_normed * normed, axis=-1, keepdims=True)
    )


LOG_ROWS = 32


def row_blocks(m, step=LOG_ROWS):
    return [pl.ds(i, step) for i in range(0, m, step)]


def matrix(ref, *lead, cols=None):
    value = ref[lead + (slice(None),) * 3 + ((slice(None),) if cols is None else (cols,))]
    return value.reshape(-1, value.shape[-1])


def full_vectors(vec_all, shards, srows, width):
    total = None
    for i in range(shards):
        row = lax.broadcasted_iota(jnp.int32, (srows, width), 0)
        col = lax.broadcasted_iota(jnp.int32, (srows, width), 1)
        place = jnp.where(col == row + i * srows, 1.0, 0.0).astype(BF)
        part = dot(vec_all[i].astype(BF), place)
        total = part if total is None else total + part
    return total


def segments(docs, ndoc, pos):
    end = docs[0, 0]
    seg = jnp.where(pos >= end, 1, 0)
    for i in range(1, ndoc):
        end = end + docs[0, i]
        seg = seg + jnp.where(pos >= end, 1, 0)
    return seg


def write_bias(bias, docs, ndoc, s, tok, seq, mem):
    m, n = bias.shape
    kpos = lax.broadcasted_iota(jnp.int32, (1, n), 1)
    place = kpos - seq
    kseg = jnp.where(kpos < seq, segments(docs, ndoc, kpos), jnp.where((place >= 0) & (place < mem // 2), -1, -3))
    for rows in row_blocks(tok):
        index = lax.broadcasted_iota(jnp.int32, (LOG_ROWS, 1), 0) + rows.start
        allowed = (segments(docs, ndoc, index + s * tok) == kseg) | (kseg == -1)
        bias[rows, :] = jnp.where(allowed, 0.0, NEG)
    if m > tok:
        own = (kpos >= s * tok) & (kpos < (s + 1) * tok)
        allowed = own | ((s == 0) & (place >= 0) & (place < mem))
        bias[pl.ds(tok, m - tok), :] = jnp.broadcast_to(jnp.where(allowed, 0.0, NEG), (m - tok, n))


def forward_kernel(shards, half, width, mem, ndoc,
                   wq, wk, wv, wo, hid, outw, tokens, memr, bq, bv, bo, bout, ga, sa, gf, sf, bhid, docs,
                   o_qkvo, o_hid, o_out, o_x, o_q, o_k, o_v, o_ctx, o_lse, o_na, o_ia, o_al, o_act, o_slope, o_nf, o_if,
                   o_res, o_vec, o_sq, o_mem,
                   w_qkvo, w_hid, w_out, x_all, vec_all, bh_all, rows, q_s, k_s, v_s, s_s, p_s, bias, inv_s, ctx, ctx_low, lse,
                   branch, na, ia, after, al, act, slope, second, nf, if_, res, vfull, sq, mctx, mlse,
                   zs, zr, hsem, hrem, xs, xr, vs, vr, hs, hr, ms, mr, es, er, ls, os_, wsem):
    r, s, core, xbit, ybit, fc, fx, fy = neighbours()
    q_own, q_lo = 2 * core + ybit, 2 * core
    bufs = (w_qkvo, w_hid, w_out)
    tok = tokens.shape[0]
    m, n = rows.shape[0], x_all.shape[0]
    seq = tok * shards
    reach = shards // 2

    local = [pltpu.make_async_copy(w, w_qkvo.at[i, s], ls.at[i]) for i, w in enumerate((wq, wk, wv, wo))]
    local.append(pltpu.make_async_copy(tokens, rows.at[pl.ds(0, tok), :], ls.at[4]))
    late = [pltpu.make_async_copy(hid.at[:, :, pl.ds(q * width, width)], w_hid.at[q, s], ls.at[5 + q]) for q in range(4)]
    late.append(pltpu.make_async_copy(outw, w_out.at[s], ls.at[9]))
    for c in local + late:
        c.start()
    everyone_in = enter((fc, fx, fy), r, s, shards)

    def reg(g, sh, q0, nq, h0, nh):
        return region(bufs[g], g, sh, q0, nq, h0, nh)

    def block(i):
        return x_all.at[pl.ds(pl.multiple_of(i * tok, tok), tok), :]

    def rows_copy(sh, k):
        return remote(block(sh), block(sh), xs.at[k, sh], xr.at[sh], (r, s + 1 if k == 0 else s - 1))

    def on_line(k, fn):
        pl.when(s + 1 < shards if k == 0 else s > 0)(fn)

    sends = []
    side = width // 2
    left_cols, right_cols = pl.ds(0, side), pl.ds(side, side)

    def piece_copy(g, sh, k):
        a = reg(g, sh, q_own, 1, xbit, 1)
        return remote(a, a, zs.at[g, k, sh], zr.at[g, sh], (r, s + 1 if k == 0 else s - 1))

    def push(g):
        for k in range(2):
            on_line(k, lambda k=k: piece_copy(g, s, k).start())

    def hop(g, sh, k):
        if k == 0:
            moves = ((q_own, 1, xbit, 1, left_cols, fx), (q_own, 1, xbit, 1, right_cols, fy))
        elif k == 1:
            moves = ((q_own, 1, 0, 2, left_cols, fy), (q_lo, 2, xbit, 1, right_cols, fx))
        else:
            moves = ((q_lo, 2, 0, 2, None, fc),)
        out = []
        for i, (q0, nq, h0, nh, cols, dev) in enumerate(moves):
            a = region(bufs[g], g, sh, q0, nq, h0, nh, cols)
            out.append(remote(a, a, hsem.at[g, k, i, sh], hrem.at[g, k, i, sh], (dev, s)))
        return out

    def each_foreign(fn, g, t):
        for left in (True, False):
            sh = s - t if left else s + t
            pl.when(s >= t if left else s + t < shards)(functools.partial(fn, g, left, sh))

    def relay_rows(last, g, left, sh):
        rows_copy(sh, 0).wait_recv()
        if not last:
            k = 0 if left else 1
            on_line(k, lambda: rows_copy(sh, k).start())

    def far_block(g, left, sh):
        at = pl.ds(pl.multiple_of(sh * tok, tok), tok)
        x_all[at, :] = jnp.zeros((tok, width), BF)
        k_s[:, at, :] = jnp.zeros((width // 128, tok, 128), BF)
        v_s[:, at, :] = jnp.zeros((width // 128, tok, 128), BF)

    def rows_in(t):
        if t <= reach:
            each_foreign(functools.partial(relay_rows, t == reach), 0, t)

    def stage0(g, left, sh):
        piece_copy(g, sh, 0).wait_recv()
        k = 0 if left else 1
        on_line(k, lambda: piece_copy(g, sh, k).start())
        for c in hop(g, sh, 0):
            c.start()

    def advance(k, g, left, sh):
        for c in hop(g, sh, k - 1):
            c.wait_recv()
        for c in hop(g, sh, k):
            c.start()

    stage1, stage2 = functools.partial(advance, 1), functools.partial(advance, 2)

    def save_shard(g, sh):
        bank = (o_qkvo, o_hid, o_out)[g]
        a, b = (bufs[g].at[sh], bank.at[sh]) if g == 2 else (bufs[g].at[:, sh], bank.at[:, sh])
        return pltpu.make_async_copy(a, b, wsem.at[g, sh])

    def stage3(g, left, sh):
        hop(g, sh, 2)[0].wait_recv()
        save_shard(g, sh).start()

    def finish(g, left, sh):
        for k in range(3):
            for c in hop(g, sh, k):
                c.wait_send()
        k = 0 if left else 1

        on_line(k, lambda: piece_copy(g, sh, k).wait_send())

    def finish_rows(g, left, sh):
        k = 0 if left else 1
        on_line(k, lambda: rows_copy(sh, k).wait_send())

    def run(stage, g):
        for t in range(1, shards):
            each_foreign(stage, g, t)

    saves = []

    def save(src, dst):
        saves.append(pltpu.make_async_copy(src, dst, os_.at[len(saves)]))
        saves[-1].start()

    for c in local[:4]:
        c.wait()
    everyone_in()
    push(0)
    local[4].wait()
    rows[pl.ds(tok, mem), :] = memr[:, 0, :]
    rows[pl.ds(tok + mem, MEM_PAD - mem), :] = jnp.zeros((MEM_PAD - mem, width), F32)
    block(s)[...] = rows[pl.ds(0, tok), :].astype(BF)
    x_all[pl.ds(seq, MEM_PAD), :] = rows[pl.ds(tok, MEM_PAD), :].astype(BF)
    x_all[pl.ds(seq + MEM_PAD, MEM_KEYS - MEM_PAD), :] = jnp.zeros((MEM_KEYS - MEM_PAD, width), BF)
    for t in range(reach + 1, shards):
        each_foreign(far_block, 0, t)
    for c in late:
        c.wait()
    push(1)
    for i, v in enumerate((bq, bv, bo, bout, ga, sa, gf, sf)):
        vec_all[s, pl.ds(i, 1), :] = v[...].astype(F32).reshape(1, 2 * half)
    bh_all[s, pl.ds(0, 1), :] = bhid[...].astype(F32).reshape(1, width)
    for t in range(1, shards):
        dev = (r, lax.rem(s + t, shards))
        sends.append(remote(vec_all.at[s], vec_all.at[s], vs.at[t], vr.at[s], dev))
        sends[-1].start()
        sends.append(remote(bh_all.at[s], bh_all.at[s], hs.at[t], hr.at[s], dev))
        sends[-1].start()
    write_bias(bias, docs, ndoc, s, tok, seq, mem)
    for g in range(3):
        save_shard(g, s).start()
    def push_rows():
        for k in range(2):
            on_line(k, lambda k=k: rows_copy(s, k).start())

    order = [(g, t) for g in range(3) for t in range(1, shards)]
    extras = {2: push_rows, 3: lambda: push(2), 6: lambda: rows_in(1), 8: lambda: rows_in(2)}

    def tick(i):
        for k, stage in enumerate((stage0, stage1, stage2)):
            if 0 <= i - 2 * k < len(order) - (k == 0):
                each_foreign(stage, *order[i - 2 * k])
        if i in extras:
            extras[i]()

    for i in range(7):
        tick(i)
    for t in range(1, shards):
        other = lax.rem(s + t, shards)
        remote(vec_all.at[other], vec_all.at[other], vs.at[t], vr.at[other], (r, other)).wait_recv()
        remote(bh_all.at[other], bh_all.at[other], hs.at[t], hr.at[other], (r, other)).wait_recv()
    vfull[...] = full_vectors(vec_all, shards, 2 * half, width)
    run(stage3, 0)
    save(vfull, o_vec)

    def vrow(i):
        return vfull[pl.ds(i, 1), :]

    def bias_cols(i, c):
        return vfull[pl.ds(i, 1), c]

    def keys_values(start, size):
        at = pl.ds(start, size)

        @pl.loop(0, width // 256)
        def _(ct):
            c = pl.ds(pl.multiple_of(ct * 256, 256), 256)
            xb = x_all[at, :]
            y = dot(xb, matrix(w_qkvo, 1, cols=c)).astype(BF)
            k_s[2 * ct, at] = y[:, :128]
            k_s[2 * ct + 1, at] = y[:, 128:]
            y = (dot(xb, matrix(w_qkvo, 2, cols=c)) + bias_cols(1, c)).astype(BF)
            v_s[2 * ct, at] = y[:, :128]
            v_s[2 * ct + 1, at] = y[:, 128:]

    @pl.loop(0, width // 256)
    def _(ct):
        c = pl.ds(pl.multiple_of(ct * 256, 256), 256)
        wt = matrix(w_qkvo, 0, cols=c)
        b = bias_cols(0, c)
        for part, at, size in ((block(s)[...], 0, tok), (x_all[pl.ds(seq, MEM_PAD), :], tok, MEM_PAD)):
            y = (dot(part, wt) + b).astype(BF) * jnp.asarray(0.125, BF)
            q_s[2 * ct, pl.ds(at, size)] = y[:, :128]
            q_s[2 * ct + 1, pl.ds(at, size)] = y[:, 128:]

    own_at = pl.multiple_of(s * tok, tok)
    keys_values(own_at, tok)
    keys_values(seq, MEM_KEYS)
    save(q_s, o_q)
    lane = lax.broadcasted_iota(jnp.int32, (tok, 128), 1)
    lane_m = lane[:MEM_PAD]
    mrows = pl.ds(tok, MEM_PAD)

    def memory_pair(p):
        seen = jnp.concatenate([bias[mrows, pl.ds(own_at, tok)], bias[mrows, pl.ds(seq, MEM_KEYS)]], axis=1)
        kk = jnp.concatenate([k_s[p, pl.ds(own_at, tok)], k_s[p, pl.ds(seq, MEM_KEYS)]])
        vv = jnp.concatenate([v_s[p, pl.ds(own_at, tok)], v_s[p, pl.ds(seq, MEM_KEYS)]])
        q = q_s[p, mrows]
        outs = []
        for head in range(2):
            sc = dot(jnp.where((lane_m < HD) == (head == 0), q, jnp.zeros_like(q)), kk, NT) + seen
            top = jnp.max(sc, axis=1, keepdims=True)
            e = jnp.exp(sc - top)
            tot = jnp.sum(e, axis=1, keepdims=True)
            outs.append(dot(e.astype(BF), vv) / tot)
            mlse[s] = jnp.where(lane_m == 2 * p + head, top + jnp.log(tot), mlse[s])
        mctx[s, :, pl.ds(pl.multiple_of(p * 128, 128), 128)] = jnp.where(lane_m < HD, outs[0], outs[1]).astype(BF)

    mlse[s] = jnp.zeros((MEM_PAD, 128), F32)
    def served(i, services):
        for at, service in services.items():
            pl.when(i == at)(service)

    tick(7)

    @pl.loop(0, width // 128)
    def _(p):
        memory_pair(p)
        served(p, {3: lambda: tick(8)})

    for t in range(1, shards):
        dev = (r, lax.rem(s + t, shards))
        for buf, ssem, rsem in ((mctx, ms, mr), (mlse, es, er)):
            sends.append(remote(buf.at[s], buf.at[s], ssem.at[t], rsem.at[s], dev))
            sends[-1].start()

    @pl.loop(0, 2 * reach)
    def _(i):
        b = s + (1 + i // 2) * (1 - 2 * lax.rem(i, 2))
        pl.when((b >= 0) & (b < shards))(lambda: keys_values(pl.multiple_of(b * tok, tok), tok))
        served(i, {3: lambda: tick(9)})

    save(x_all, o_x)
    save(k_s, o_k)
    save(v_s, o_v)

    def pair(p):
        outs = []
        for head in range(2):
            q = q_s[p, pl.ds(0, tok)]
            s_s[pl.ds(0, tok), :] = dot(jnp.where((lane < HD) == (head == 0), q, jnp.zeros_like(q)), k_s[p], NT)
            for rb in row_blocks(tok):
                sc = s_s[rb, :] + bias[rb, :]
                top = jnp.max(sc, axis=1, keepdims=True)
                e = jnp.exp(sc - top)
                tot = jnp.sum(e, axis=1, keepdims=True)
                p_s[rb, :] = e.astype(BF)
                wide = jnp.broadcast_to(top + jnp.log(tot), (LOG_ROWS, 128))
                inv = jnp.broadcast_to(1.0 / tot, (LOG_ROWS, 128))
                if head == 0:
                    lse[p, rb] = wide
                    inv_s[rb, :] = inv
                else:
                    right = lane[:LOG_ROWS] >= HD
                    lse[p, rb] = jnp.where(right, wide, lse[p, rb])
                    inv_s[rb, :] = jnp.where(right, inv, inv_s[rb, :])
            outs.append(dot(p_s[...], v_s[p]))
        value = jnp.where(lane < HD, outs[0], outs[1]) * inv_s[...]
        c = pl.ds(pl.multiple_of(p * 128, 128), 128)
        ctx[pl.ds(0, tok), c] = value
        ctx_low[pl.ds(0, tok), c] = value.astype(BF)

    @pl.loop(0, width // 128)
    def _(p):
        pair(p)
        served(p, {1: lambda: each_foreign(stage0, *order[-1]), 4: lambda: tick(10), 5: lambda: tick(11)})

    for t in range(1, shards):
        other = lax.rem(s + t, shards)
        remote(mctx.at[other], mctx.at[other], ms.at[t], mr.at[other], (r, other)).wait_recv()
        remote(mlse.at[other], mlse.at[other], es.at[t], er.at[other], (r, other)).wait_recv()
    top = mlse[0]
    for i in range(1, shards):
        top = jnp.maximum(top, mlse[i])
    tot = sum(jnp.exp(mlse[i] - top) for i in range(shards))
    whole = top + jnp.log(tot)
    shares = [jnp.exp(mlse[i] - whole) for i in range(shards)]

    def spread(v, p):
        return jnp.where(lane_m < HD, v[:, 2 * p : 2 * p + 1], v[:, 2 * p + 1 : 2 * p + 2])

    for p in range(width // 128):
        c = pl.ds(p * 128, 128)
        value = sum(spread(shares[i], p) * mctx[i, :, c].astype(F32) for i in range(shards))
        ctx[mrows, c] = value
        ctx_low[mrows, c] = value.astype(BF)
        lse[p, mrows] = spread(whole, p)
    save(ctx, o_ctx)
    save(lse, o_lse)

    def stats(totals):
        center = totals - jnp.mean(totals, axis=1, keepdims=True)
        spread = jnp.mean(center * center, axis=1, keepdims=True)
        inverse = lax.rsqrt(spread + EPSILON)
        return center * inverse, inverse

    @pl.loop(0, width // 256)
    def _(ct):
        c = pl.ds(pl.multiple_of(ct * 256, 256), 256)
        branch[:, c] = dot(ctx_low[...], matrix(w_qkvo, 3, cols=c)) + bias_cols(2, c)
        second[:, c] = jnp.broadcast_to(bias_cols(3, c), (m, 256))

    sq[...] = jnp.zeros_like(sq)

    def add_square(i, rb, value):
        if rb.start < tok:
            total = jnp.sum(value * value, axis=0, keepdims=True)
            sq[pl.ds(i, 1), :] = sq[pl.ds(i, 1), :] + total

    for rb in row_blocks(m):
        b = branch[rb, :]
        add_square(1, rb, b)
        normed, inverse = stats(rows[rb, :] + b)
        na[rb, :] = normed
        ia[rb, :] = jnp.broadcast_to(inverse, (LOG_ROWS, 128))
        y = normed * vrow(4) + vrow(5)
        after[rb, :] = y
        al[rb, :] = y.astype(BF)
    save(na, o_na)
    save(ia, o_ia)
    save(al, o_al)
    run(stage3, 1)

    @pl.loop(0, 4)
    def _(q):
        @pl.loop(0, width // 256)
        def _(ct):
            c = pl.ds(pl.multiple_of(ct * 256, 256), 256)
            s_s[:, :256] = dot(al[...], matrix(w_hid, q, cols=c))
            b = bh_all[q, pl.ds(0, 1), c]
            for rb in row_blocks(m):
                z = s_s[rb, :256] + b
                he = 0.5 * (1.0 + lax.erf(z * GELU_ROOT))
                act[q, rb, c] = (z * he).astype(BF)
                slope[q, rb, c] = he + z * jnp.exp(-0.5 * z * z) * GELU_DENSITY

        served(q, {0: lambda: tick(12)})


    save(act, o_act)
    save(slope, o_slope)

    def add_second(sh):
        @pl.loop(0, width // 256)
        def _(ct):
            c = pl.ds(pl.multiple_of(ct * 256, 256), 256)
            second[:, c] = second[:, c] + dot(act[sh], matrix(w_out, sh, cols=c))

    @pl.loop(0, 2 * shards - 1)
    def _(i):
        t = (i + 1) // 2
        sh = s + t * (1 - 2 * lax.rem(i, 2))

        @pl.when((sh >= 0) & (sh < shards))
        def _():
            pl.when(t > 0)(lambda: stage3(2, True, sh))
            add_second(sh)

    for rb in row_blocks(m):
        b = second[rb, :]
        add_square(2, rb, b)
        normed, inverse = stats(after[rb, :] + b)
        nf[rb, :] = normed
        if_[rb, :] = jnp.broadcast_to(inverse, (LOG_ROWS, 128))
        y = normed * vrow(6) + vrow(7)
        add_square(0, rb, y)
        res[rb, :] = y
    save(nf, o_nf)
    save(if_, o_if)
    save(res.at[pl.ds(0, tok), :], o_res)
    o_mem[:, 0, :] = res[pl.ds(tok, mem), :]
    save(sq, o_sq)
    for g in range(3):
        run(finish, g)
    for t in range(1, reach):
        each_foreign(finish_rows, 0, t)
    for c in sends:
        c.wait_send()
    for k in range(2):
        on_line(k, lambda k=k: rows_copy(s, k).wait_send())
        for g in range(3):
            on_line(k, lambda g=g, k=k: piece_copy(g, s, k).wait_send())
    for c in saves:
        c.wait()
    for g in range(3):
        for i in range(shards):
            save_shard(g, i).wait()


def forward_all(wq, wk, wv, wo, hid, outw, tokens, memr, vectors, docs):
    shards = lax.axis_size("shard")
    half, width = wq.shape[0] // 2, wq.shape[1]
    tok, mem = tokens.shape[0], memr.shape[0]
    m, n = tok + MEM_PAD, tok * shards + MEM_KEYS
    pairs = width // 128
    stack = (4, shards, 2, half, width)
    any_space = pl.BlockSpec(memory_space=pl.ANY)
    vm = pl.BlockSpec(memory_space=pltpu.VMEM)
    dma = pltpu.SemaphoreType.DMA

    def sd(shape, dtype):
        return jax.ShapeDtypeStruct(shape, dtype)

    outs = (
        sd(stack, BF), sd(stack, BF), sd((shards, 4, 2, half, width), BF), sd((n, width), BF),
        sd((pairs, m, 128), BF), sd((pairs, n, 128), BF), sd((pairs, n, 128), BF),
        sd((m, width), F32), sd((pairs, m, 128), F32), sd((m, width), F32), sd((m, 128), F32), sd((m, width), BF),
        sd((4, m, width), BF), sd((4, m, width), F32), sd((m, width), F32), sd((m, 128), F32), sd((tok, width), F32),
        sd((8, width), F32), sd((8, width), F32), sd((mem, 1, width), F32),
    )
    V = pltpu.VMEM
    scratch = [
        V(stack, BF), V(stack, BF), V((shards, 4, 2, half, width), BF), V((n, width), BF), V((shards, 8, 2 * half), F32), V((shards, 8, width), F32),
        V((m, width), F32), V((pairs, m, 128), BF), V((pairs, n, 128), BF), V((pairs, n, 128), BF), V((m, n), F32),
        V((tok, n), BF), V((m, n), F32), V((tok, 128), F32), V((m, width), F32), V((m, width), BF), V((pairs, m, 128), F32),
        V((m, width), F32), V((m, width), F32), V((m, 128), F32), V((m, width), F32), V((m, width), BF),
        V((4, m, width), BF), V((4, m, width), F32), V((m, width), F32), V((m, width), F32), V((m, 128), F32),
        V((m, width), F32), V((8, width), F32), V((8, width), F32),
        V((shards, MEM_PAD, width), BF), V((shards, MEM_PAD, 128), F32),
    ]
    return pl.pallas_call(
        functools.partial(forward_kernel, shards, half, width, mem, docs.shape[1]),
        out_shape=outs,
        in_specs=[any_space] * 7 + [vm] * 10 + [pl.BlockSpec(memory_space=pltpu.SMEM)],
        out_specs=[any_space] * (len(outs) - 1) + [vm],
        scratch_shapes=scratch
        + [dma((3, 2, shards)), dma((3, shards)), dma((3, 3, 2, shards)), dma((3, 3, 2, shards)), dma((2, shards))] + [dma((shards,))] * 9 + [dma((10,)), dma((len(outs),)), dma((3, shards))],
        compiler_params=pltpu.CompilerParams(collective_id=3, has_side_effects=True, vmem_limit_bytes=VMEM_LIMIT),
        name="forward_layer",
    )(
        wq.reshape(2, half, width), wk.reshape(2, half, width), wv.reshape(2, half, width), wo.reshape(2, half, width),
        hid.reshape(2, half, 4 * width), outw.reshape(4, 2, half, width), tokens, memr, *vectors, docs,
    )


def backward_kernel(shards, half, width, mem, count,
                    h_qkvo, h_hid, h_out, h_x, h_q, h_k, h_v, h_ctx, h_lse, h_na, h_ia, h_al, h_act, h_slope, h_nf, h_if,
                    vfull, sq, out_grad, mem_grad, docs,
                    o_qkvo, o_hid, o_out, o_x, o_mem, o_own, o_bhid, o_rms,
                    grad, ra, rb, rc, rd, rx, relay, rm, rv, vz, vacc,
                    wbuf, x_all, pq, pk, pv, pctx, plse, bias, s_s, dp_s, p_s, ds_s, al, abuf, sbuf, d_pre, nf, if_,
                    gr, d_out, back, d_branch, dctx, dq, dkt, dvt,
                    asem, arem, bsem, brem, csem, crem, zsem, zrem, dsem, drem, xsem, xrem, msem, mrem, vsem, vrem,
                    vzs, vzr, fsem, wsem, psem, asem_, lsem, osem):
    r, s, core, xbit, ybit, fc, fx, fy = neighbours()
    q_own, q_lo = 2 * core + ybit, 2 * core
    tok = out_grad.shape[0]
    m, n = gr.shape[0], x_all.shape[0]
    seq = tok * shards
    pairs = width // 128
    outs = (o_qkvo, o_hid, o_out)
    groups = (2, 1, 0)
    units = 3 * shards

    def turn(i):
        return lax.rem((shards - 1) * i, shards)

    def load(src, dst, i):
        c = pltpu.make_async_copy(src, dst, lsem.at[i])
        c.start()
        return c

    def w_copy(j, src):
        return pltpu.make_async_copy(src, wbuf.at[j % 4], wsem.at[j])

    def a_copy(i):
        return (
            pltpu.make_async_copy(h_act.at[turn(i)], abuf.at[lax.rem(i, 2)], asem_.at[0, i]),
            pltpu.make_async_copy(h_slope.at[turn(i)], sbuf.at[lax.rem(i, 2)], asem_.at[1, i]),
        )

    def p_copy(p, slot):
        return [
            pltpu.make_async_copy(a.at[p], b.at[slot], psem.at[i, slot])
            for i, (a, b) in enumerate(((h_q, pq), (h_k, pk), (h_v, pv), (h_lse, plse)))
        ]

    first = [load(h_nf, nf, 0), load(out_grad, gr.at[pl.ds(0, tok), :], 1), load(h_if, if_, 2)]
    for j, src in enumerate((h_out.at[0], h_hid.at[0], h_out.at[turn(1)])):
        w_copy(j, src).start()
    for c in a_copy(jnp.int32(0)):
        c.start()
    second = [load(h_al, al, 3), load(h_x, x_all, 6), load(h_ctx, pctx, 7)]
    everyone_in = enter((fc, fx, fy), r, s, shards)

    def unit_shard(u):
        return turn(lax.rem(u, shards))

    def copy_a(u):
        return remote(grad.at[u, 1 - core], ra.at[u], asem.at[u], arem.at[u], (fc, s))

    side = width // 2
    left_cols, right_cols = pl.ds(0, side), pl.ds(side, side)

    def copy_b(u):
        return (
            remote(grad.at[u, core, :, 1 - xbit, :, left_cols], rb.at[u, 0], bsem.at[u, 0], brem.at[u, 0], (fx, s)),
            remote(grad.at[u, core, 1 - ybit, :, :, right_cols], rb.at[u, 1], bsem.at[u, 1], brem.at[u, 1], (fy, s)),
        )

    def copy_c(u):
        return (
            remote(grad.at[u, core, 1 - ybit, xbit, :, left_cols], rc.at[u, 0], csem.at[u, 0], crem.at[u, 0], (fy, s)),
            remote(grad.at[u, core, ybit, 1 - xbit, :, right_cols], rc.at[u, 1], csem.at[u, 1], crem.at[u, 1], (fx, s)),
        )

    def copy_z(u):
        return remote(
            grad.at[u, core, ybit, xbit], rd.at[u // shards, s], zsem.at[u], zrem.at[u // shards, s], (r, unit_shard(u))
        )

    def start_b(u):
        copy_a(u).wait_recv()
        grad[u, core] = grad[u, core] + ra[u]
        for c in copy_b(u):
            c.start()

    def start_c(u):
        for c in copy_b(u):
            c.wait_recv()
        grad[u, core, :, xbit, :, left_cols] = grad[u, core, :, xbit, :, left_cols] + rb[u, 0]
        grad[u, core, ybit, :, :, right_cols] = grad[u, core, ybit, :, :, right_cols] + rb[u, 1]
        for c in copy_c(u):
            c.start()

    def start_z(u):
        for c in copy_c(u):
            c.wait_recv()
        grad[u, core, ybit, xbit, :, left_cols] = grad[u, core, ybit, xbit, :, left_cols] + rc[u, 0]
        grad[u, core, ybit, xbit, :, right_cols] = grad[u, core, ybit, xbit, :, right_cols] + rc[u, 1]
        pl.when(s != unit_shard(u))(lambda: copy_z(u).start())

    def hop(k, j):
        o = outs[groups[k]]
        if j == 0:
            moves = ((o.at[q_own, xbit, :, left_cols], fx), (o.at[q_own, xbit, :, right_cols], fy))
        elif j == 1:
            moves = ((o.at[q_own, :, :, left_cols], fy), (o.at[pl.ds(q_lo, 2), xbit, :, right_cols], fx))
        else:
            moves = ((o.at[pl.ds(q_lo, 2)], fc),)
        return [remote(a, a, dsem.at[k, j, i], drem.at[k, j, i], (dev, s)) for i, (a, dev) in enumerate(moves)]

    def hop_start(k, j):
        for c in hop(k, j):
            c.start()

    def hop_wait(k, j):
        for c in hop(k, j):
            c.wait_recv()

    def finish_group(k):
        total = grad[k * shards + turn(s), core, ybit, xbit].astype(F32)
        for t in range(1, shards):
            other = lax.rem(s + t, shards)
            slot = rd.at[k, other]
            remote(slot, slot, zsem.at[0], zrem.at[k, other], (r, s)).wait_recv()
            total = total + rd[k, other].astype(F32)
        fin = ra.at[k * shards, 0, 0]
        fin[...] = total.astype(BF)
        c = pltpu.make_async_copy(fin, outs[groups[k]].at[q_own, xbit], fsem.at[k])
        c.start()
        c.wait()
        hop_start(k, 0)

    def hop_step(k, j):
        hop_wait(k, j - 1)
        hop_start(k, j)

    lag = 2
    steps = []
    for when, j, k in ((10, 0, 0), (11, 1, 0), (12, 2, 0), (14, 0, 1), (15, 1, 1), (16, 0, 2), (16, 2, 1), (17, 1, 2), (18, 2, 2)):
        steps.append((when, functools.partial(hop_step, k, j) if j else functools.partial(finish_group, k)))
    ticks = max(when for when, fn in steps) + 1

    def tick(i):
        def guarded(lo, fn):
            pl.when((i >= lo) & (i < lo + units))(lambda: fn(i - lo))

        guarded(0, start_b)
        guarded(lag, start_c)
        guarded(2 * lag, start_z)

    def late_tick(i):
        tick(jnp.int32(i))
        for when, fn in steps:
            if when == i:
                fn()

    def vrow(i):
        return vfull[pl.ds(i, 1), :]

    index = lax.broadcasted_iota(jnp.int32, (m, 1), 0)
    once = jnp.where((index < tok) | ((index < tok + mem) & (s == 0)), 1.0, 0.0)

    def add_sum(i, rw, value):
        total = jnp.sum(value * once[rw.start : rw.start + LOG_ROWS], axis=0, keepdims=True)
        vacc[0, pl.ds(i, 1), :] = vacc[0, pl.ds(i, 1), :] + total

    def mean(v):
        return jnp.mean(v, axis=1, keepdims=True)

    def norm_back_rows(e, normed, inverse):
        return inverse * (e - mean(e) - normed * mean(e * normed))

    vacc[0] = jnp.zeros(vacc.shape[1:], F32)
    for c in first:
        c.wait()
    gr[pl.ds(tok, mem), :] = mem_grad[:, 0, :]
    gr[pl.ds(tok + mem, MEM_PAD - mem), :] = jnp.zeros((MEM_PAD - mem, width), F32)
    for rw in row_blocks(m):
        g, normed = gr[rw, :], nf[rw, :]
        add_sum(6, rw, g * normed)
        add_sum(7, rw, g)
        v = norm_back_rows(g * vrow(6), normed, if_[rw, :1])
        back[rw, :] = v
        low = v.astype(BF)
        add_sum(3, rw, low.astype(F32))
        d_out[rw, :] = low
    na, ia = nf, if_
    second += [load(h_na, na, 4), load(h_ia, ia, 5)]
    second[0].wait()
    once_low = once.astype(BF)

    def turned(a, b):
        return dot(a, b, TN)

    def put(k, q, j, value):
        value = value.astype(BF).reshape(2, 2, half, width)
        for i in range(2):
            unit = k * shards + (shards - 1) * (2 * j + i) % shards
            grad[unit, q // 2, q % 2] = value[i]

    wide = 2 * 2 * half
    def feed_forward(i):
        q = turn(i)
        even = 2 * lax.rem(i, 2)
        for c in a_copy(i):
            c.wait()

        @pl.when(i + 1 < 4)
        def _():
            for c in a_copy(i + 1):
                c.start()

        w_copy(2 * i, h_out.at[q]).wait()
        pl.when(i < 3)(lambda: w_copy(2 * i + 3, h_hid.at[turn(i + 1)]).start())
        pl.when(i == 3)(lambda: w_copy(9, h_qkvo.at[1]).start())
        slot = lax.rem(i, 2)
        do = d_out[...] * once_low
        for j in range(2):
            value = turned(abuf[slot, :, j * wide : (j + 1) * wide], do)
            grad[i, j] = value.astype(BF).reshape(2, 2, half, width)
        pl.when(i == 0)(everyone_in)
        copy_a(i).start()
        for j in range(2):
            wt = wbuf[even, 2 * j : 2 * j + 2].reshape(wide, width)
            s_s[:, j * wide : (j + 1) * wide] = dot(d_out[...], wt, NT)
        for rw in row_blocks(m):
            v = s_s[rw, :width] * sbuf[slot, rw, :]
            low = v.astype(BF)
            d_pre[rw, :] = low
            add_sum(8 + q, rw, low.astype(F32))
        w_copy(2 * i + 1, h_hid.at[q]).wait()
        pl.when(i < 2)(lambda: w_copy(2 * i + 4, h_out.at[turn(i + 2)]).start())
        pl.when(i == 2)(lambda: w_copy(8, h_qkvo.at[3]).start())
        pl.when(i == 3)(lambda: w_copy(10, h_qkvo.at[2]).start())
        dp = d_pre[...] * once_low
        for j in range(2):
            value = turned(al[:, j * wide : (j + 1) * wide], dp).astype(BF).reshape(2, 2, half, width)
            for k in range(2):
                unit = shards + (shards - 1) * (2 * j + k) % shards
                grad[unit, q // 2, lax.rem(q, 2)] = value[k]
        for j in range(2):
            wt = wbuf[even + 1, 2 * j : 2 * j + 2].reshape(wide, width)
            s_s[:, j * wide : (j + 1) * wide] = dot(d_pre[...], wt, NT)
        for rw in row_blocks(m):
            back[rw, :] = back[rw, :] + s_s[rw, :width]
        tick(i)

    pl.loop(0, 4)(feed_forward)
    for j in range(shards):
        copy_a(shards + j).start()
    for c in p_copy(0, 0):
        c.start()

    for c in second[1:]:
        c.wait()

    for rw in row_blocks(m):
        f, normed = back[rw, :], na[rw, :]
        add_sum(4, rw, f * normed)
        add_sum(5, rw, f)
        v = norm_back_rows(f * vrow(4), normed, ia[rw, :1])
        back[rw, :] = v
        low = v.astype(BF)
        d_branch[rw, :] = low
        add_sum(2, rw, low.astype(F32))
        d_out[rw, :] = pctx[rw, :].astype(BF)
    write_bias(bias, docs, docs.shape[1], s, tok, seq, mem)
    w_copy(8, h_qkvo.at[3]).wait()
    w_copy(11, h_qkvo.at[0]).start()
    db = d_branch[...] * once_low
    for j in range(2):
        put(2, 3, j, turned(d_out[:, j * wide : (j + 1) * wide], db))
    for j in range(2):
        wt = wbuf[0, 2 * j : 2 * j + 2].reshape(wide, width)
        value = dot(d_branch[...], wt, NT).astype(BF)
        for i in range(wide // 128):
            dctx[j * (wide // 128) + i] = value[:, i * 128 : (i + 1) * 128]
    lane = lax.broadcasted_iota(jnp.int32, (m, 128), 1)
    lane_k = lax.broadcasted_iota(jnp.int32, (n, 128), 1)
    tick(jnp.int32(4))

    def pair(p):
        slot = lax.rem(p, 2)
        for c in p_copy(p, slot):
            c.wait()

        @pl.when(p + 1 < pairs)
        def _():
            for c in p_copy(p + 1, 1 - slot):
                c.start()

        c = pl.ds(pl.multiple_of(p * 128, 128), 128)
        part_q, part_k, part_v = None, None, None
        zero = jnp.zeros((m, 128), BF)
        for head in range(2):
            mine = (lane < HD) == (head == 0)
            qh = jnp.where(mine, pq[slot], zero)
            doh = jnp.where(mine, dctx[p], zero)
            s_s[...] = dot(qh, pk[slot], NT)
            dp_s[...] = dot(doh, pv[slot], NT)
            for rw in row_blocks(m):
                sub = slice(rw.start, rw.start + LOG_ROWS)
                delta = jnp.sum(doh[sub].astype(F32) * pctx[rw, c], axis=1, keepdims=True)
                top = plse[slot, rw, head * HD : head * HD + 1]
                probs = jnp.exp(s_s[rw, :] + bias[rw, :] - top)
                p_s[rw, :] = probs.astype(BF)
                ds_s[rw, :] = (probs * (dp_s[rw, :] - delta)).astype(BF)
            kh = jnp.where((lane_k < HD) == (head == 0), pk[slot], jnp.zeros((n, 128), BF))
            a = dot(ds_s[...], kh)
            b = turned(qh, ds_s[...])
            d = turned(doh, p_s[...])
            part_q = a if head == 0 else part_q + a
            part_k = b if head == 0 else part_k + b
            part_v = d if head == 0 else part_v + d
        dq[:, c] = (part_q * 0.125).astype(BF)
        dkt[c, :] = part_k.astype(BF)
        dvt[c, :] = part_v.astype(BF)
        pl.when(lax.rem(p, 2) == 1)(lambda: tick(5 + p // 2))

    pl.loop(0, pairs)(pair)

    ones = jnp.ones((8, n), BF)
    vacc[0, pl.ds(1, 1), :] = dot(ones, dvt[...], NT)[:1]
    vacc[0, pl.ds(0, 1), :] = jnp.sum(dq[...].astype(F32), axis=0, keepdims=True)
    vacc[0, pl.ds(12, 3), :] = sq[pl.ds(0, 3), :]
    rv_first = remote(vacc.at[0], rv.at[0], vsem.at[0], vrem.at[0], (fc, s))
    rv_first.start()
    def vec_hop(k):
        return remote(vacc.at[k], rv.at[k], vsem.at[k], vrem.at[k], ((fc, fx, fy)[k], s))

    def vec_step(k):
        vec_hop(k - 1).wait_recv()
        vacc[k] = vacc[k - 1] + rv[k - 1]
        vec_hop(k).start()

    w_copy(9, h_qkvo.at[1]).wait()
    w_copy(10, h_qkvo.at[2]).wait()
    wkm = wbuf[1].reshape(width, width)
    wvm = wbuf[2].reshape(width, width)
    spare = (abuf.at[0, pl.ds(0, tok)], abuf.at[1, pl.ds(0, tok)], d_pre.at[pl.ds(0, tok)])
    small = []

    def to_shard(src, dst, ssem, rsem, t):
        return remote(src, dst.at[s], ssem.at[t], rsem.at[s], (r, lax.rem(s + t, shards)))

    def row_grads(blk):
        c = pl.ds(pl.multiple_of(blk * tok, tok), tok)
        return jnp.transpose(dot(wkm, dkt[:, c]) + dot(wvm, dvt[:, c]))

    def along(src, dst, i, up):
        return remote(src, dst, xsem.at[i], xrem.at[i], (r, s + 1 if up else s - 1))

    far = (along(spare[0], relay.at[0], 0, True), along(spare[0], relay.at[1], 1, False))
    near = (along(spare[1], rx.at[0], 2, True), along(spare[2], rx.at[1], 3, False))
    has_far = (s < 2, s >= 2)
    has_near = (s < shards - 1, s > 0)
    has_relay = (s > 0, s < shards - 1)
    spare[0][...] = row_grads(lax.rem(s + 2, shards)).astype(BF)
    for i in range(2):
        pl.when(has_far[i])(far[i].start)
    for j in range(2):
        xs_ = x_all[:, j * wide : (j + 1) * wide]
        x_own = jnp.concatenate([
            x_all[pl.ds(pl.multiple_of(s * tok, tok), tok), j * wide : (j + 1) * wide],
            x_all[pl.ds(seq, MEM_PAD), j * wide : (j + 1) * wide],
        ])
        put(2, 0, j, turned(x_own, dq[...]))
        xt = jnp.transpose(xs_)
        put(2, 1, j, dot(xt, dkt[...], NT))
        put(2, 2, j, dot(xt, dvt[...], NT))
    for j in range(shards):
        copy_a(2 * shards + j).start()
    tick(jnp.int32(8))

    vec_step(1)
    tick(jnp.int32(9))
    for i in range(2):
        @pl.when(has_near[i])
        def _():
            spare[1 + i][...] = row_grads(s + 1 - 2 * i).astype(BF)

            @pl.when(has_relay[i])
            def _():
                along(spare[0], relay.at[i], i, i == 0).wait_recv()
                spare[1 + i][...] = (spare[1 + i][...].astype(F32) + relay[i].astype(F32)).astype(BF)

            near[i].start()

        if i == 0:
            late_tick(10)
    own_rows = pl.ds(0, tok)
    back[own_rows, :] = back[own_rows, :] + row_grads(s)
    value = dot(wkm, dkt[:, pl.ds(seq, MEM_KEYS)]) + dot(wvm, dvt[:, pl.ds(seq, MEM_KEYS)])
    w_copy(11, h_qkvo.at[0]).wait()
    mrows = pl.ds(tok, MEM_PAD)
    value = jnp.transpose(value)[:MEM_PAD] + dot(dq[mrows, :], wbuf[3].reshape(width, width), NT)
    rm[s] = value.astype(BF)
    for t in range(1, shards):
        small.append(remote(rm.at[s], rm.at[s], msem.at[t], mrem.at[s], (r, lax.rem(s + t, shards))))
        small[-1].start()
    vec_step(2)
    for j in range(2):
        wt = wbuf[3, 2 * j : 2 * j + 2].reshape(wide, width)
        c = pl.ds(j * wide, wide)
        back[own_rows, c] = back[own_rows, c] + dot(dq[own_rows, :], wt, NT)
    vec_hop(2).wait_recv()
    vz[s] = vacc[2] + rv[2]
    for t in range(1, shards):
        small.append(to_shard(vz.at[s], vz, vzs, vzr, t))
        small[-1].start()
    for i in range(11, ticks):
        late_tick(i)

    for t in range(1, shards):
        other = lax.rem(s + t, shards)
        for buf, rsem in ((rm, mrem), (vz, vzr)):
            remote(buf.at[other], buf.at[other], msem.at[0], rsem.at[other], (r, s)).wait_recv()
    for i in range(2):
        @pl.when(has_relay[i])
        def _():
            along(spare[0], rx.at[i], 2 + i, i == 0).wait_recv()
            back[own_rows, :] = back[own_rows, :] + rx[i].astype(F32)

    sx, sm, sv = back[own_rows, :], back[mrows, :], vz[0]
    for t in range(shards):
        sm = sm + rm[t].astype(F32)
        if t:
            sv = sv + vz[t]
    gr[pl.ds(0, tok), :] = sx
    o_mem[:, 0, :] = sm[:mem]
    final = [
        pltpu.make_async_copy(gr.at[pl.ds(0, tok), :], o_x, osem.at[0]),
    ]
    for c in final:
        c.start()
    srows = 2 * half
    for i in range(shards):
        @pl.when(s == i)
        def _():
            o_own[...] = sv[:8, i * srows : (i + 1) * srows]
            o_bhid[...] = sv[8 + i : 9 + i]

    squares = jnp.sum(sv[8:16], axis=1, keepdims=True) / count
    o_rms[...] = jnp.broadcast_to(jnp.sqrt(squares), o_rms.shape)
    for k in range(3):
        hop_wait(k, 2)
    for c in final:
        c.wait()

    @pl.loop(0, units)
    def _(u):
        copy_a(u).wait_send()
        for c in copy_b(u) + copy_c(u):
            c.wait_send()
        pl.when(s != unit_shard(u))(lambda: copy_z(u).wait_send())

    for k in range(3):
        for j in range(3):
            for c in hop(k, j):
                c.wait_send()
    for c in small:
        c.wait_send()
    for i in range(2):
        pl.when(has_far[i])(far[i].wait_send)
        pl.when(has_near[i])(near[i].wait_send)
    for k in range(3):
        vec_hop(k).wait_send()


def backward_all(saved, out_grad, mem_grad, docs):
    shards = lax.axis_size("shard")
    tok, width = out_grad.shape
    mem = mem_grad.shape[0]
    half = saved[0].shape[3]
    m, n = tok + MEM_PAD, tok * shards + MEM_KEYS
    pairs = width // 128
    any_space = pl.BlockSpec(memory_space=pl.ANY)
    vm = pl.BlockSpec(memory_space=pltpu.VMEM)
    dma = pltpu.SemaphoreType.DMA
    V = pltpu.VMEM
    units = 3 * shards
    piece4 = (4, 2, half, width)
    outs = tuple(jax.ShapeDtypeStruct(piece4, BF) for _ in range(3)) + (
        jax.ShapeDtypeStruct((tok, width), F32),
        jax.ShapeDtypeStruct((mem, 1, width), F32),
        jax.ShapeDtypeStruct((8, 2 * half), F32),
        jax.ShapeDtypeStruct((1, width), F32),
        jax.ShapeDtypeStruct((8, 128), F32),
    )
    big = (4, 2, half, width)
    scratch = [
        V((units, 2, 2, 2, half, width), BF), V((units, 2, 2, half, width), BF), V((units, 2, 2, half, width // 2), BF),
        V((units, 2, half, width // 2), BF), V((3, shards, half, width), BF), V((2, tok, width), BF), V((2, tok, width), BF),
        V((shards, MEM_PAD, width), BF), V((3, 16, width), F32), V((shards, 16, width), F32), V((3, 16, width), F32),
        V((4,) + big, BF), V((n, width), BF), V((2, m, 128), BF), V((2, n, 128), BF), V((2, n, 128), BF),
        V((m, width), F32), V((2, m, 128), F32), V((m, n), F32), V((m, n), F32), V((m, n), F32), V((m, n), BF),
        V((m, n), BF), V((m, width), BF), V((2, m, width), BF),
        V((2, m, width), F32), V((m, width), BF), V((m, width), F32), V((m, 128), F32), V((m, width), F32),
        V((m, width), BF), V((m, width), F32), V((m, width), BF), V((pairs, m, 128), BF), V((m, width), BF),
        V((width, n), BF), V((width, n), BF),
    ]
    sems = (
        [dma((units,))] * 2 + [dma((units, 2))] * 4 + [dma((units,)), dma((3, shards))]
        + [dma((3, 3, 2)), dma((3, 3, 2)), dma((shards,)), dma((shards,)), dma((shards,)), dma((shards,))]
        + [dma((3,)), dma((3,)), dma((shards,)), dma((shards,)), dma((3,)), dma((12,)), dma((4, 2)), dma((2, 4))]
        + [dma((8,)), dma((1,))]
    )
    return pl.pallas_call(
        functools.partial(backward_kernel, shards, half, width, mem, float(tok * shards * width * lax.axis_size("replica"))),
        out_shape=outs,
        in_specs=[any_space] * 16 + [vm, vm, any_space, vm, pl.BlockSpec(memory_space=pltpu.SMEM)],
        out_specs=[any_space] * 4 + [vm] * 4,
        scratch_shapes=scratch + sems,
        compiler_params=pltpu.CompilerParams(collective_id=4, has_side_effects=True, vmem_limit_bytes=VMEM_LIMIT),
        name="backward_layer",
    )(*saved, out_grad, mem_grad, docs)


def plain_body(tokens, memory_rows, doc_lengths, w_query, w_key, w_value, w_attn_out, w_hidden, w_output,
         b_query, b_value, b_attn_out, b_hidden, b_output, gain_attn, shift_attn, gain_ffn, shift_ffn,
         out_grad, memory_grad):
    tok, width = tokens.shape
    mem = memory_rows.shape[1]
    shards = lax.axis_size("shard")
    s = lax.axis_index("shard")
    seq = tok * shards
    srows = w_query.shape[0]
    m = tok + MEM_PAD
    n = seq + MEM_KEYS
    scaling = 1.0 / math.sqrt(HD)

    vec = jnp.concatenate(
        [v.reshape(-1, srows) for v in (
            b_query, b_value, b_attn_out, b_output, gain_attn, shift_attn, gain_ffn, shift_ffn, b_hidden
        )]
        + [jnp.zeros((4, srows), BF)]
    )
    vec = lax.dynamic_update_slice(jnp.zeros((16, width), BF), vec, (0, s * srows))
    rows = jnp.concatenate([tokens, memory_rows[0], jnp.zeros((MEM_PAD - mem, width), F32)])
    low_rows = rows.astype(BF)
    qkvo = jnp.stack([w_query, w_key, w_value, w_attn_out])
    qkvo, w_hid, w_out, x_tok, vec_all = gather_plain(qkvo, w_hidden, w_output, low_rows[:tok], vec)
    vec = jnp.sum(vec_all.astype(F32), axis=0)
    bq, bv, bo, bout, ga, sa, gf, sf = (vec[i] for i in range(8))
    bh = jnp.transpose(vec[8:12].reshape(4, shards, srows), (1, 0, 2)).reshape(4 * width)

    doc_ends = jnp.cumsum(doc_lengths[0])
    seg = jnp.sum((jnp.arange(seq, dtype=jnp.int32)[:, None] >= doc_ends[None, :]).astype(jnp.int32), axis=1)
    place = jnp.arange(MEM_KEYS, dtype=jnp.int32)
    mem_seg = jnp.where(place < mem // 2, -1, jnp.where(place < mem, -3, -4)).astype(jnp.int32)
    kseg = jnp.concatenate([seg, mem_seg])[None, :]
    qseg = jnp.concatenate(
        [lax.dynamic_slice_in_dim(seg, s * tok, tok), jnp.full((MEM_PAD,), -2, jnp.int32)]
    )[:, None]
    index = jnp.arange(m, dtype=jnp.int32)[:, None]
    once = jnp.where(index < tok, 1.0, jnp.where((index < tok + mem) & (s == 0), 1.0, 0.0)).astype(F32)
    once_low = once.astype(BF)

    x_all = jnp.concatenate([x_tok, low_rows[tok:], jnp.zeros((MEM_KEYS - MEM_PAD, width), BF)])
    query = (jnp.dot(low_rows, qkvo[0], preferred_element_type=F32) + bq).astype(BF)
    keys = jnp.dot(x_all, qkvo[1], preferred_element_type=F32).astype(BF)
    values = (jnp.dot(x_all, qkvo[2], preferred_element_type=F32) + bv).astype(BF)
    context, lse = attention(query, keys, values, qseg, kseg, scaling)
    context_low = context.astype(BF)
    branch = jnp.dot(context_low, qkvo[3], preferred_element_type=F32) + bo
    normed_attn, inverse_attn = layer_stats(rows + branch)
    after_attn = normed_attn * ga + sa
    after_low = after_attn.astype(BF)
    pre_act = jnp.concatenate([jnp.dot(after_low, w_hid[q], preferred_element_type=F32) for q in range(4)], axis=1) + bh
    half_erf = 0.5 * (1.0 + lax.erf(pre_act * GELU_ROOT))
    act_low = (pre_act * half_erf).astype(BF)
    second = jnp.dot(act_low, w_out, preferred_element_type=F32) + bout
    normed_ffn, inverse_ffn = layer_stats(after_attn + second)
    result = normed_ffn * gf + sf

    grads = jnp.concatenate([out_grad, memory_grad[0], jnp.zeros((MEM_PAD - mem, width), F32)])
    back_ffn = norm_back(grads * gf, normed_ffn, inverse_ffn)
    d_output = back_ffn.astype(BF)
    g_out = jnp.einsum("rf,rd->fd", act_low * once_low, d_output, preferred_element_type=F32).astype(BF)
    d_act = jnp.einsum("rd,fd->rf", d_output, w_out, preferred_element_type=F32)
    d_pre = (d_act * (half_erf + pre_act * jnp.exp(-0.5 * pre_act * pre_act) * GELU_DENSITY)).astype(BF)
    after_once = after_low * once_low
    g_hid = jnp.stack(
        [jnp.einsum("rd,rf->df", after_once, d_pre[:, q * width : (q + 1) * width], preferred_element_type=F32).astype(BF)
         for q in range(4)]
    )
    back_first = back_ffn + sum(
        jnp.einsum("rf,df->rd", d_pre[:, q * width : (q + 1) * width], w_hid[q], preferred_element_type=F32)
        for q in range(4)
    )
    back_attn = norm_back(back_first * ga, normed_attn, inverse_attn)
    d_branch = back_attn.astype(BF)
    d_context = jnp.einsum("re,de->rd", d_branch, qkvo[3], preferred_element_type=F32).astype(BF)
    dq, dkt, dvt = attention_back(query, keys, values, qseg, kseg, once, context, lse, d_context, scaling)
    g_qkvo = jnp.stack([
        jnp.einsum("rd,re->de", low_rows * once_low, dq, preferred_element_type=F32).astype(BF),
        jnp.einsum("rd,er->de", x_all, dkt, preferred_element_type=F32).astype(BF),
        jnp.einsum("rd,er->de", x_all, dvt, preferred_element_type=F32).astype(BF),
        jnp.einsum("rd,re->de", context_low * once_low, d_branch, preferred_element_type=F32).astype(BF),
    ])
    dx = jnp.einsum("er,de->rd", dkt, qkvo[1], preferred_element_type=F32) + jnp.einsum(
        "er,de->rd", dvt, qkvo[2], preferred_element_type=F32
    )
    base = back_attn + jnp.einsum("re,de->rd", dq, qkvo[0], preferred_element_type=F32)

    def over_rows(terms):
        return jnp.sum(once * terms, axis=0)

    gb_hidden = over_rows(d_pre.astype(F32)).reshape(shards, 4, srows).transpose(1, 0, 2).reshape(4, width)
    squares = jnp.stack([jnp.sum(v[:tok] * v[:tok]) for v in (result, branch, second)])
    vec_grads = jnp.concatenate([
        jnp.stack([
            over_rows(dq.astype(F32)),
            jnp.sum(dvt.astype(F32), axis=1),
            over_rows(d_branch.astype(F32)),
            over_rows(d_output.astype(F32)),
            over_rows(back_first * normed_attn),
            over_rows(back_first),
            over_rows(grads * normed_ffn),
            over_rows(grads),
        ]),
        gb_hidden,
        jnp.pad(squares[None], ((0, 3), (0, width - 3))),
    ])
    g_qkvo, g_hid, g_out, dx_own, dx_mem, vec_sum = reduce_plain(
        g_qkvo, g_hid, g_out, dx[:seq].astype(BF), dx[seq : seq + MEM_PAD], vec_grads
    )
    own = lax.dynamic_slice(vec_sum, (0, s * srows), (12, srows))
    rms = jnp.sqrt(vec_sum[12, :3] / float(seq * width * lax.axis_size("replica")))
    g_qkvo = g_qkvo.astype(F32)
    grad_hidden = jnp.concatenate([g_hid[q] for q in range(4)], axis=1).astype(F32)
    return (
        result[:tok],
        result[tok : tok + mem][None],
        base[:tok] + dx_own,
        (base[tok : tok + mem] + dx_mem[:mem])[None],
        g_qkvo[0],
        g_qkvo[1],
        g_qkvo[2],
        g_qkvo[3],
        grad_hidden,
        g_out.astype(F32),
        own[0],
        own[1],
        own[2],
        own[8:12].reshape(-1),
        own[3],
        own[4],
        own[5],
        own[6],
        own[7],
        rms[0],
        rms[1],
        rms[2],
    )


def direct_body(tokens, memory_rows, doc_lengths, w_query, w_key, w_value, w_attn_out, w_hidden, w_output,
                b_query, b_value, b_attn_out, b_hidden, b_output, gain_attn, shift_attn, gain_ffn, shift_ffn,
                out_grad, memory_grad):
    width = tokens.shape[1]
    srows = w_query.shape[0]
    vectors = (b_query, b_value, b_attn_out, b_output, gain_attn, shift_attn, gain_ffn, shift_ffn, b_hidden)
    *saved, result, vec_full, squares, result_mem = forward_all(
        w_query, w_key, w_value, w_attn_out, w_hidden, w_output, tokens, jnp.transpose(memory_rows, (1, 0, 2)), vectors, doc_lengths
    )
    g_qkvo, g_hid, g_out, grad_rows, grad_mem, own, own_hid, rms = backward_all(
        tuple(saved) + (vec_full, squares), out_grad, jnp.transpose(memory_grad, (1, 0, 2)), doc_lengths
    )
    g_qkvo = g_qkvo.reshape(4, srows, width).astype(F32)
    g_hid = g_hid.reshape(4, srows, width)
    return (
        result,
        jnp.transpose(result_mem, (1, 0, 2)),
        grad_rows,
        jnp.transpose(grad_mem, (1, 0, 2)),
        g_qkvo[0],
        g_qkvo[1],
        g_qkvo[2],
        g_qkvo[3],
        jnp.concatenate([g_hid[q] for q in range(4)], axis=1).astype(F32),
        g_out.reshape(4 * srows, width).astype(F32),
        own[0],
        own[1],
        own[2],
        own_hid[0],
        own[3],
        own[4],
        own[5],
        own[6],
        own[7],
        rms[4, 0],
        rms[5, 0],
        rms[6, 0],
    )


def solution(mesh):
    direct = mesh.shape["replica"] == 8 and mesh.shape["shard"] == 4
    shard1, shard2 = P("shard"), P("shard", None)
    both, rep3 = P(("replica", "shard"), None), P("replica", None, None)
    return jax.shard_map(
        direct_body if direct else plain_body,
        mesh=mesh,
        in_specs=(both, rep3, P("replica", None)) + (shard2,) * 6 + (shard1,) * 9 + (both, rep3),
        out_specs=(both, rep3, both, rep3) + (shard2,) * 6 + (shard1,) * 9 + (P(), P(), P()),
        check_vma=False,
    )
```

```python
import functools
import math

import jax
import jax.numpy as jnp
from jax import lax
from jax.experimental import pallas as pl
from jax.experimental.pallas import tpu as pltpu
from jax.sharding import PartitionSpec as P

H = 12
HD = 64
EPSILON = 1e-12
GELU_ROOT = 0.7071067811865476
GELU_DENSITY = 0.3989422804014327
MESH = pl.DeviceIdType.MESH
BF = jnp.bfloat16
F32 = jnp.float32
MEM_PAD = 32
MEM_KEYS = 128
VMEM_LIMIT = 60 << 20
NEG = -1e30


def region(ref, group, sh, q0, nq, h0, nh, cols=None):
    hs = h0 if nh == 1 else pl.ds(h0, nh)
    qs = q0 if nq == 1 else pl.ds(q0, nq)
    tail = () if cols is None else (slice(None), cols)
    return ref.at[((sh, qs, hs) if group == 2 else (qs, sh, hs)) + tail]


def neighbours():
    r = lax.axis_index("replica")
    s = lax.axis_index("shard")
    core, xbit, ybit = r % 2, (r // 2) % 2, (r // 4) % 2
    return r, s, core, xbit, ybit, r + 1 - 2 * core, r + 2 - 4 * xbit, r + 4 - 8 * ybit


def enter(peers, r, s, shards):
    sem = pltpu.get_barrier_semaphore()
    for p in peers:
        pl.semaphore_signal(sem, 1, device_id=(p, s), device_id_type=MESH)
    for t in range(1, shards):
        pl.semaphore_signal(sem, 1, device_id=(r, lax.rem(s + t, shards)), device_id_type=MESH)
    return lambda: pl.semaphore_wait(sem, len(peers) + shards - 1)


def remote(src, dst, ssem, rsem, dev):
    return pltpu.make_async_remote_copy(
        src_ref=src, dst_ref=dst, send_sem=ssem, recv_sem=rsem, device_id=dev, device_id_type=MESH
    )


def gather_plain(qkvo, hid, outw, xtok, vec):
    width = qkvo.shape[2]
    full = functools.partial(lax.all_gather, axis_name="shard", tiled=True)
    hid = full(hid, axis=0)
    return (
        full(qkvo, axis=1),
        jnp.stack([hid[:, q * width : (q + 1) * width] for q in range(4)]),
        full(outw, axis=0),
        full(xtok, axis=0),
        lax.all_gather(vec, "shard", axis=0),
    )


def reduce_plain(g_qkvo, g_hid, g_out, dx, mem, vec):
    scatter = functools.partial(lax.psum_scatter, axis_name="shard", tiled=True)
    return (
        lax.psum(scatter(g_qkvo, scatter_dimension=1), "replica"),
        lax.psum(scatter(g_hid, scatter_dimension=1), "replica"),
        lax.psum(scatter(g_out, scatter_dimension=0), "replica"),
        scatter(dx, scatter_dimension=0).astype(F32),
        lax.psum(mem, "shard"),
        lax.psum(vec, ("replica", "shard")),
    )


NT = (((1,), (1,)), ((), ()))
NN = (((1,), (0,)), ((), ()))
TN = (((0,), (0,)), ((), ()))


def dot(a, b, dims=NN):
    return lax.dot_general(a, b, dims, preferred_element_type=F32)


def head_lanes(shape, head):
    lane = lax.broadcasted_iota(jnp.int32, shape, 1)
    return (lane < HD) if head == 0 else (lane >= HD)


def mask_bias(qseg, kseg):
    allowed = (qseg == kseg) | (kseg == -1) | ((qseg == -2) & (kseg != -4))
    return jnp.where(allowed, 0.0, NEG)


def attend_kernel(scaling, q_ref, k_ref, v_ref, qseg_ref, kseg_ref, ctx_ref, lse_ref, bias_ref):
    @pl.when(pl.program_id(0) == 0)
    def _():
        bias_ref[...] = mask_bias(qseg_ref[...], kseg_ref[...])

    q, k, v = q_ref[...], k_ref[...], v_ref[...]
    zero_q = jnp.zeros_like(q)
    contexts, totals = [], []
    for head in range(2):
        qh = jnp.where(head_lanes(q.shape, head), q, zero_q)
        scores = dot(qh, k, NT) * scaling + bias_ref[...]
        top = jnp.max(scores, axis=1, keepdims=True)
        powers = jnp.exp(scores - top)
        lse = top + jnp.log(jnp.sum(powers, axis=1, keepdims=True))
        probs = powers * jnp.exp(top - lse)
        contexts.append(dot(probs.astype(BF), v))
        totals.append(lse)
    first = head_lanes(q.shape, 0)
    ctx_ref[...] = jnp.where(first, contexts[0], contexts[1])
    lse_ref[...] = jnp.where(first, totals[0], totals[1])


def attend_back_kernel(scaling, q_ref, k_ref, v_ref, qseg_ref, kseg_ref, weight_ref, ctx_ref, lse_ref, do_ref,
                       dq_ref, dk_ref, dv_ref, bias_ref):
    @pl.when(pl.program_id(0) == 0)
    def _():
        bias_ref[...] = mask_bias(qseg_ref[...], kseg_ref[...])

    q, k, v, do = q_ref[...], k_ref[...], v_ref[...], do_ref[...]
    weight = weight_ref[...] > 0
    dq, dk, dv = None, None, None
    for head in range(2):
        lanes = head_lanes(q.shape, head)
        qh = jnp.where(lanes, q, jnp.zeros_like(q))
        doh = jnp.where(lanes, do, jnp.zeros_like(do))
        lse = lse_ref[:, head * HD : head * HD + 1]
        scores = dot(qh, k, NT) * scaling + bias_ref[...]
        probs = jnp.exp(scores - lse)
        delta = jnp.sum(doh.astype(F32) * ctx_ref[...], axis=1, keepdims=True)
        d_scores = (probs * (dot(doh, v, NT) - delta)).astype(BF)
        kh = jnp.where(head_lanes(k.shape, head), k, jnp.zeros_like(k))
        part_q = dot(d_scores, kh)
        part_k = dot(jnp.where(weight, qh, jnp.zeros_like(qh)), d_scores, TN)
        part_v = dot(jnp.where(weight, doh, jnp.zeros_like(doh)), probs.astype(BF), TN)
        dq = part_q if dq is None else dq + part_q
        dk = part_k if dk is None else dk + part_k
        dv = part_v if dv is None else dv + part_v
    dq_ref[...] = (dq * scaling).astype(BF)
    dk_ref[...] = (dk * scaling).astype(BF)
    dv_ref[...] = dv.astype(BF)


def attention(query, keys, values, qseg, kseg, scaling):
    m, width = query.shape
    n = keys.shape[0]
    rows = pl.BlockSpec((m, 2 * HD), lambda i: (0, i))
    cols = pl.BlockSpec((n, 2 * HD), lambda i: (0, i))
    return pl.pallas_call(
        functools.partial(attend_kernel, scaling),
        grid=(width // (2 * HD),),
        out_shape=(jax.ShapeDtypeStruct((m, width), F32), jax.ShapeDtypeStruct((m, width), F32)),
        in_specs=[rows, cols, cols, pl.BlockSpec((m, 1), lambda i: (0, 0)), pl.BlockSpec((1, n), lambda i: (0, 0))],
        out_specs=[rows, rows],
        scratch_shapes=[pltpu.VMEM((m, n), F32)],
        compiler_params=pltpu.CompilerParams(vmem_limit_bytes=VMEM_LIMIT),
        name="attend",
    )(query, keys, values, qseg, kseg)


def attention_back(query, keys, values, qseg, kseg, weight, context, lse, d_context, scaling):
    m, width = query.shape
    n = keys.shape[0]
    rows = pl.BlockSpec((m, 2 * HD), lambda i: (0, i))
    cols = pl.BlockSpec((n, 2 * HD), lambda i: (0, i))
    turned = pl.BlockSpec((2 * HD, n), lambda i: (i, 0))
    column = pl.BlockSpec((m, 1), lambda i: (0, 0))
    return pl.pallas_call(
        functools.partial(attend_back_kernel, scaling),
        grid=(width // (2 * HD),),
        out_shape=(
            jax.ShapeDtypeStruct((m, width), BF),
            jax.ShapeDtypeStruct((width, n), BF),
            jax.ShapeDtypeStruct((width, n), BF),
        ),
        in_specs=[rows, cols, cols, column, pl.BlockSpec((1, n), lambda i: (0, 0)), column, rows, rows, rows],
        out_specs=[rows, turned, turned],
        scratch_shapes=[pltpu.VMEM((m, n), F32)],
        compiler_params=pltpu.CompilerParams(vmem_limit_bytes=VMEM_LIMIT),
        name="attend_back",
    )(query, keys, values, qseg, kseg, weight, context, lse, d_context)


def layer_stats(totals):
    center = totals - jnp.mean(totals, axis=-1, keepdims=True)
    spread = jnp.mean(center * center, axis=-1, keepdims=True)
    inverse = lax.rsqrt(spread + EPSILON)
    return (center * inverse, inverse)


def norm_back(grad_normed, normed, inverse):
    return inverse * (
        grad_normed
        - jnp.mean(grad_normed, axis=-1, keepdims=True)
        - normed * jnp.mean(grad_normed * normed, axis=-1, keepdims=True)
    )


LOG_ROWS = 32


def row_blocks(m, step=LOG_ROWS):
    return [pl.ds(i, step) for i in range(0, m, step)]


def matrix(ref, *lead, cols=None):
    value = ref[lead + (slice(None),) * 3 + ((slice(None),) if cols is None else (cols,))]
    return value.reshape(-1, value.shape[-1])


def full_vectors(vec_all, shards, srows, width):
    total = None
    for i in range(shards):
        row = lax.broadcasted_iota(jnp.int32, (srows, width), 0)
        col = lax.broadcasted_iota(jnp.int32, (srows, width), 1)
        place = jnp.where(col == row + i * srows, 1.0, 0.0).astype(BF)
        part = dot(vec_all[i].astype(BF), place)
        total = part if total is None else total + part
    return total


def segments(docs, ndoc, pos):
    end = docs[0, 0]
    seg = jnp.where(pos >= end, 1, 0)
    for i in range(1, ndoc):
        end = end + docs[0, i]
        seg = seg + jnp.where(pos >= end, 1, 0)
    return seg


def write_bias(bias, docs, ndoc, s, tok, seq, mem):
    m, n = bias.shape
    kpos = lax.broadcasted_iota(jnp.int32, (1, n), 1)
    place = kpos - seq
    kseg = jnp.where(kpos < seq, segments(docs, ndoc, kpos), jnp.where((place >= 0) & (place < mem // 2), -1, -3))
    for rows in row_blocks(tok):
        index = lax.broadcasted_iota(jnp.int32, (LOG_ROWS, 1), 0) + rows.start
        allowed = (segments(docs, ndoc, index + s * tok) == kseg) | (kseg == -1)
        bias[rows, :] = jnp.where(allowed, 0.0, NEG)
    if m > tok:
        own = (kpos >= s * tok) & (kpos < (s + 1) * tok)
        allowed = own | ((s == 0) & (place >= 0) & (place < mem))
        bias[pl.ds(tok, m - tok), :] = jnp.broadcast_to(jnp.where(allowed, 0.0, NEG), (m - tok, n))


def forward_kernel(shards, half, width, mem, ndoc,
                   wq, wk, wv, wo, hid, outw, tokens, memr, bq, bv, bo, bout, ga, sa, gf, sf, bhid, docs,
                   o_qkvo, o_hid, o_out, o_x, o_q, o_k, o_v, o_ctx, o_lse, o_na, o_ia, o_al, o_act, o_slope, o_nf, o_if,
                   o_res, o_vec, o_sq, o_mem,
                   w_qkvo, w_hid, w_out, x_all, vec_all, bh_all, rows, q_s, k_s, v_s, s_s, p_s, bias, inv_s, ctx, ctx_low, lse,
                   branch, na, ia, after, al, act, slope, second, nf, if_, res, vfull, sq, mctx, mlse,
                   zs, zr, hsem, hrem, xs, xr, vs, vr, hs, hr, ms, mr, es, er, ls, os_, wsem):
    r, s, core, xbit, ybit, fc, fx, fy = neighbours()
    q_own, q_lo = 2 * core + ybit, 2 * core
    bufs = (w_qkvo, w_hid, w_out)
    tok = tokens.shape[0]
    m, n = rows.shape[0], x_all.shape[0]
    seq = tok * shards
    reach = shards // 2

    local = [pltpu.make_async_copy(w, w_qkvo.at[i, s], ls.at[i]) for i, w in enumerate((wq, wk, wv, wo))]
    local.append(pltpu.make_async_copy(tokens, rows.at[pl.ds(0, tok), :], ls.at[4]))
    late = [pltpu.make_async_copy(hid.at[:, :, pl.ds(q * width, width)], w_hid.at[q, s], ls.at[5 + q]) for q in range(4)]
    late.append(pltpu.make_async_copy(outw, w_out.at[s], ls.at[9]))
    for c in local + late:
        c.start()
    everyone_in = enter((fc, fx, fy), r, s, shards)

    def reg(g, sh, q0, nq, h0, nh):
        return region(bufs[g], g, sh, q0, nq, h0, nh)

    def block(i):
        return x_all.at[pl.ds(pl.multiple_of(i * tok, tok), tok), :]

    def rows_copy(sh, k):
        return remote(block(sh), block(sh), xs.at[k, sh], xr.at[sh], (r, s + 1 if k == 0 else s - 1))

    def on_line(k, fn):
        pl.when(s + 1 < shards if k == 0 else s > 0)(fn)

    sends = []
    side = width // 2
    left_cols, right_cols = pl.ds(0, side), pl.ds(side, side)

    def piece_copy(g, sh, k):
        a = reg(g, sh, q_own, 1, xbit, 1)
        return remote(a, a, zs.at[g, k, sh], zr.at[g, sh], (r, s + 1 if k == 0 else s - 1))

    def push(g):
        for k in range(2):
            on_line(k, lambda k=k: piece_copy(g, s, k).start())

    def hop(g, sh, k):
        if k == 0:
            moves = ((q_own, 1, xbit, 1, left_cols, fx), (q_own, 1, xbit, 1, right_cols, fy))
        elif k == 1:
            moves = ((q_own, 1, 0, 2, left_cols, fy), (q_lo, 2, xbit, 1, right_cols, fx))
        else:
            moves = ((q_lo, 2, 0, 2, None, fc),)
        out = []
        for i, (q0, nq, h0, nh, cols, dev) in enumerate(moves):
            a = region(bufs[g], g, sh, q0, nq, h0, nh, cols)
            out.append(remote(a, a, hsem.at[g, k, i, sh], hrem.at[g, k, i, sh], (dev, s)))
        return out

    def each_foreign(fn, g, t):
        for left in (True, False):
            sh = s - t if left else s + t
            pl.when(s >= t if left else s + t < shards)(functools.partial(fn, g, left, sh))

    def relay_rows(last, g, left, sh):
        rows_copy(sh, 0).wait_recv()
        if not last:
            k = 0 if left else 1
            on_line(k, lambda: rows_copy(sh, k).start())

    def far_block(g, left, sh):
        at = pl.ds(pl.multiple_of(sh * tok, tok), tok)
        x_all[at, :] = jnp.zeros((tok, width), BF)
        k_s[:, at, :] = jnp.zeros((width // 128, tok, 128), BF)
        v_s[:, at, :] = jnp.zeros((width // 128, tok, 128), BF)

    def rows_in(t):
        if t <= reach:
            each_foreign(functools.partial(relay_rows, t == reach), 0, t)

    def stage0(g, left, sh):
        piece_copy(g, sh, 0).wait_recv()
        k = 0 if left else 1
        on_line(k, lambda: piece_copy(g, sh, k).start())
        for c in hop(g, sh, 0):
            c.start()

    def advance(k, g, left, sh):
        for c in hop(g, sh, k - 1):
            c.wait_recv()
        for c in hop(g, sh, k):
            c.start()

    stage1, stage2 = functools.partial(advance, 1), functools.partial(advance, 2)

    def save_shard(g, sh):
        bank = (o_qkvo, o_hid, o_out)[g]
        a, b = (bufs[g].at[sh], bank.at[sh]) if g == 2 else (bufs[g].at[:, sh], bank.at[:, sh])
        return pltpu.make_async_copy(a, b, wsem.at[g, sh])

    def stage3(g, left, sh):
        hop(g, sh, 2)[0].wait_recv()
        save_shard(g, sh).start()

    def finish(g, left, sh):
        for k in range(3):
            for c in hop(g, sh, k):
                c.wait_send()
        k = 0 if left else 1

        on_line(k, lambda: piece_copy(g, sh, k).wait_send())

    def finish_rows(g, left, sh):
        k = 0 if left else 1
        on_line(k, lambda: rows_copy(sh, k).wait_send())

    def run(stage, g):
        for t in range(1, shards):
            each_foreign(stage, g, t)

    saves = []

    def save(src, dst):
        saves.append(pltpu.make_async_copy(src, dst, os_.at[len(saves)]))
        saves[-1].start()

    for c in local[:4]:
        c.wait()
    everyone_in()
    push(0)
    local[4].wait()
    rows[pl.ds(tok, mem), :] = memr[:, 0, :]
    rows[pl.ds(tok + mem, MEM_PAD - mem), :] = jnp.zeros((MEM_PAD - mem, width), F32)
    block(s)[...] = rows[pl.ds(0, tok), :].astype(BF)
    x_all[pl.ds(seq, MEM_PAD), :] = rows[pl.ds(tok, MEM_PAD), :].astype(BF)
    x_all[pl.ds(seq + MEM_PAD, MEM_KEYS - MEM_PAD), :] = jnp.zeros((MEM_KEYS - MEM_PAD, width), BF)
    for t in range(reach + 1, shards):
        each_foreign(far_block, 0, t)
    for c in late:
        c.wait()
    push(1)
    for i, v in enumerate((bq, bv, bo, bout, ga, sa, gf, sf)):
        vec_all[s, pl.ds(i, 1), :] = v[...].astype(F32).reshape(1, 2 * half)
    bh_all[s, pl.ds(0, 1), :] = bhid[...].astype(F32).reshape(1, width)
    for t in range(1, shards):
        dev = (r, lax.rem(s + t, shards))
        sends.append(remote(vec_all.at[s], vec_all.at[s], vs.at[t], vr.at[s], dev))
        sends[-1].start()
        sends.append(remote(bh_all.at[s], bh_all.at[s], hs.at[t], hr.at[s], dev))
        sends[-1].start()
    write_bias(bias, docs, ndoc, s, tok, seq, mem)
    for g in range(3):
        save_shard(g, s).start()
    def push_rows():
        for k in range(2):
            on_line(k, lambda k=k: rows_copy(s, k).start())

    order = [(g, t) for g in range(3) for t in range(1, shards)]
    extras = {2: push_rows, 3: lambda: push(2), 6: lambda: rows_in(1), 8: lambda: rows_in(2)}

    def tick(i):
        for k, stage in enumerate((stage0, stage1, stage2)):
            if 0 <= i - 2 * k < len(order) - (k == 0):
                each_foreign(stage, *order[i - 2 * k])
        if i in extras:
            extras[i]()

    for i in range(7):
        tick(i)
    for t in range(1, shards):
        other = lax.rem(s + t, shards)
        remote(vec_all.at[other], vec_all.at[other], vs.at[t], vr.at[other], (r, other)).wait_recv()
        remote(bh_all.at[other], bh_all.at[other], hs.at[t], hr.at[other], (r, other)).wait_recv()
    vfull[...] = full_vectors(vec_all, shards, 2 * half, width)
    run(stage3, 0)
    save(vfull, o_vec)

    def vrow(i):
        return vfull[pl.ds(i, 1), :]

    def bias_cols(i, c):
        return vfull[pl.ds(i, 1), c]

    def keys_values(start, size):
        at = pl.ds(start, size)

        @pl.loop(0, width // 256)
        def _(ct):
            c = pl.ds(pl.multiple_of(ct * 256, 256), 256)
            xb = x_all[at, :]
            y = dot(xb, matrix(w_qkvo, 1, cols=c)).astype(BF)
            k_s[2 * ct, at] = y[:, :128]
            k_s[2 * ct + 1, at] = y[:, 128:]
            y = (dot(xb, matrix(w_qkvo, 2, cols=c)) + bias_cols(1, c)).astype(BF)
            v_s[2 * ct, at] = y[:, :128]
            v_s[2 * ct + 1, at] = y[:, 128:]

    @pl.loop(0, width // 256)
    def _(ct):
        c = pl.ds(pl.multiple_of(ct * 256, 256), 256)
        wt = matrix(w_qkvo, 0, cols=c)
        b = bias_cols(0, c)
        for part, at, size in ((block(s)[...], 0, tok), (x_all[pl.ds(seq, MEM_PAD), :], tok, MEM_PAD)):
            y = (dot(part, wt) + b).astype(BF) * jnp.asarray(0.125, BF)
            q_s[2 * ct, pl.ds(at, size)] = y[:, :128]
            q_s[2 * ct + 1, pl.ds(at, size)] = y[:, 128:]

    own_at = pl.multiple_of(s * tok, tok)
    keys_values(own_at, tok)
    keys_values(seq, MEM_KEYS)
    save(q_s, o_q)
    lane = lax.broadcasted_iota(jnp.int32, (tok, 128), 1)
    lane_m = lane[:MEM_PAD]
    mrows = pl.ds(tok, MEM_PAD)

    def memory_pair(p):
        seen = jnp.concatenate([bias[mrows, pl.ds(own_at, tok)], bias[mrows, pl.ds(seq, MEM_KEYS)]], axis=1)
        kk = jnp.concatenate([k_s[p, pl.ds(own_at, tok)], k_s[p, pl.ds(seq, MEM_KEYS)]])
        vv = jnp.concatenate([v_s[p, pl.ds(own_at, tok)], v_s[p, pl.ds(seq, MEM_KEYS)]])
        q = q_s[p, mrows]
        outs = []
        for head in range(2):
            sc = dot(jnp.where((lane_m < HD) == (head == 0), q, jnp.zeros_like(q)), kk, NT) + seen
            top = jnp.max(sc, axis=1, keepdims=True)
            e = jnp.exp(sc - top)
            tot = jnp.sum(e, axis=1, keepdims=True)
            outs.append(dot(e.astype(BF), vv) / tot)
            mlse[s] = jnp.where(lane_m == 2 * p + head, top + jnp.log(tot), mlse[s])
        mctx[s, :, pl.ds(pl.multiple_of(p * 128, 128), 128)] = jnp.where(lane_m < HD, outs[0], outs[1]).astype(BF)

    mlse[s] = jnp.zeros((MEM_PAD, 128), F32)
    def served(i, services):
        for at, service in services.items():
            pl.when(i == at)(service)

    tick(7)

    @pl.loop(0, width // 128)
    def _(p):
        memory_pair(p)
        served(p, {3: lambda: tick(8)})

    for t in range(1, shards):
        dev = (r, lax.rem(s + t, shards))
        for buf, ssem, rsem in ((mctx, ms, mr), (mlse, es, er)):
            sends.append(remote(buf.at[s], buf.at[s], ssem.at[t], rsem.at[s], dev))
            sends[-1].start()

    @pl.loop(0, 2 * reach)
    def _(i):
        b = s + (1 + i // 2) * (1 - 2 * lax.rem(i, 2))
        pl.when((b >= 0) & (b < shards))(lambda: keys_values(pl.multiple_of(b * tok, tok), tok))
        served(i, {3: lambda: tick(9)})

    save(x_all, o_x)
    save(k_s, o_k)
    save(v_s, o_v)

    def pair(p):
        outs = []
        for head in range(2):
            q = q_s[p, pl.ds(0, tok)]
            s_s[pl.ds(0, tok), :] = dot(jnp.where((lane < HD) == (head == 0), q, jnp.zeros_like(q)), k_s[p], NT)
            for rb in row_blocks(tok):
                sc = s_s[rb, :] + bias[rb, :]
                top = jnp.max(sc, axis=1, keepdims=True)
                e = jnp.exp(sc - top)
                tot = jnp.sum(e, axis=1, keepdims=True)
                p_s[rb, :] = e.astype(BF)
                wide = jnp.broadcast_to(top + jnp.log(tot), (LOG_ROWS, 128))
                inv = jnp.broadcast_to(1.0 / tot, (LOG_ROWS, 128))
                if head == 0:
                    lse[p, rb] = wide
                    inv_s[rb, :] = inv
                else:
                    right = lane[:LOG_ROWS] >= HD
                    lse[p, rb] = jnp.where(right, wide, lse[p, rb])
                    inv_s[rb, :] = jnp.where(right, inv, inv_s[rb, :])
            outs.append(dot(p_s[...], v_s[p]))
        value = jnp.where(lane < HD, outs[0], outs[1]) * inv_s[...]
        c = pl.ds(pl.multiple_of(p * 128, 128), 128)
        ctx[pl.ds(0, tok), c] = value
        ctx_low[pl.ds(0, tok), c] = value.astype(BF)

    @pl.loop(0, width // 128)
    def _(p):
        pair(p)
        served(p, {1: lambda: each_foreign(stage0, *order[-1]), 4: lambda: tick(10), 5: lambda: tick(11)})

    for t in range(1, shards):
        other = lax.rem(s + t, shards)
        remote(mctx.at[other], mctx.at[other], ms.at[t], mr.at[other], (r, other)).wait_recv()
        remote(mlse.at[other], mlse.at[other], es.at[t], er.at[other], (r, other)).wait_recv()
    top = mlse[0]
    for i in range(1, shards):
        top = jnp.maximum(top, mlse[i])
    tot = sum(jnp.exp(mlse[i] - top) for i in range(shards))
    whole = top + jnp.log(tot)
    shares = [jnp.exp(mlse[i] - whole) for i in range(shards)]

    def spread(v, p):
        return jnp.where(lane_m < HD, v[:, 2 * p : 2 * p + 1], v[:, 2 * p + 1 : 2 * p + 2])

    for p in range(width // 128):
        c = pl.ds(p * 128, 128)
        value = sum(spread(shares[i], p) * mctx[i, :, c].astype(F32) for i in range(shards))
        ctx[mrows, c] = value
        ctx_low[mrows, c] = value.astype(BF)
        lse[p, mrows] = spread(whole, p)
    save(ctx, o_ctx)
    save(lse, o_lse)

    def stats(totals):
        center = totals - jnp.mean(totals, axis=1, keepdims=True)
        spread = jnp.mean(center * center, axis=1, keepdims=True)
        inverse = lax.rsqrt(spread + EPSILON)
        return center * inverse, inverse

    @pl.loop(0, width // 256)
    def _(ct):
        c = pl.ds(pl.multiple_of(ct * 256, 256), 256)
        branch[:, c] = dot(ctx_low[...], matrix(w_qkvo, 3, cols=c)) + bias_cols(2, c)
        second[:, c] = jnp.broadcast_to(bias_cols(3, c), (m, 256))

    sq[...] = jnp.zeros_like(sq)

    def add_square(i, rb, value):
        if rb.start < tok:
            total = jnp.sum(value * value, axis=0, keepdims=True)
            sq[pl.ds(i, 1), :] = sq[pl.ds(i, 1), :] + total

    for rb in row_blocks(m):
        b = branch[rb, :]
        add_square(1, rb, b)
        normed, inverse = stats(rows[rb, :] + b)
        na[rb, :] = normed
        ia[rb, :] = jnp.broadcast_to(inverse, (LOG_ROWS, 128))
        y = normed * vrow(4) + vrow(5)
        after[rb, :] = y
        al[rb, :] = y.astype(BF)
    save(na, o_na)
    save(ia, o_ia)
    save(al, o_al)
    run(stage3, 1)

    @pl.loop(0, 4)
    def _(q):
        @pl.loop(0, width // 256)
        def _(ct):
            c = pl.ds(pl.multiple_of(ct * 256, 256), 256)
            s_s[:, :256] = dot(al[...], matrix(w_hid, q, cols=c))
            b = bh_all[q, pl.ds(0, 1), c]
            for rb in row_blocks(m):
                z = s_s[rb, :256] + b
                he = 0.5 * (1.0 + lax.erf(z * GELU_ROOT))
                act[q, rb, c] = (z * he).astype(BF)
                slope[q, rb, c] = he + z * jnp.exp(-0.5 * z * z) * GELU_DENSITY

        served(q, {0: lambda: tick(12)})


    save(act, o_act)
    save(slope, o_slope)

    def add_second(sh):
        @pl.loop(0, width // 256)
        def _(ct):
            c = pl.ds(pl.multiple_of(ct * 256, 256), 256)
            second[:, c] = second[:, c] + dot(act[sh], matrix(w_out, sh, cols=c))

    @pl.loop(0, 2 * shards - 1)
    def _(i):
        t = (i + 1) // 2
        sh = s + t * (1 - 2 * lax.rem(i, 2))

        @pl.when((sh >= 0) & (sh < shards))
        def _():
            pl.when(t > 0)(lambda: stage3(2, True, sh))
            add_second(sh)

    for rb in row_blocks(m):
        b = second[rb, :]
        add_square(2, rb, b)
        normed, inverse = stats(after[rb, :] + b)
        nf[rb, :] = normed
        if_[rb, :] = jnp.broadcast_to(inverse, (LOG_ROWS, 128))
        y = normed * vrow(6) + vrow(7)
        add_square(0, rb, y)
        res[rb, :] = y
    save(nf, o_nf)
    save(if_, o_if)
    save(res.at[pl.ds(0, tok), :], o_res)
    o_mem[:, 0, :] = res[pl.ds(tok, mem), :]
    save(sq, o_sq)
    for g in range(3):
        run(finish, g)
    for t in range(1, reach):
        each_foreign(finish_rows, 0, t)
    for c in sends:
        c.wait_send()
    for k in range(2):
        on_line(k, lambda k=k: rows_copy(s, k).wait_send())
        for g in range(3):
            on_line(k, lambda g=g, k=k: piece_copy(g, s, k).wait_send())
    for c in saves:
        c.wait()
    for g in range(3):
        for i in range(shards):
            save_shard(g, i).wait()


def forward_all(wq, wk, wv, wo, hid, outw, tokens, memr, vectors, docs):
    shards = lax.axis_size("shard")
    half, width = wq.shape[0] // 2, wq.shape[1]
    tok, mem = tokens.shape[0], memr.shape[0]
    m, n = tok + MEM_PAD, tok * shards + MEM_KEYS
    pairs = width // 128
    stack = (4, shards, 2, half, width)
    any_space = pl.BlockSpec(memory_space=pl.ANY)
    vm = pl.BlockSpec(memory_space=pltpu.VMEM)
    dma = pltpu.SemaphoreType.DMA

    def sd(shape, dtype):
        return jax.ShapeDtypeStruct(shape, dtype)

    outs = (
        sd(stack, BF), sd(stack, BF), sd((shards, 4, 2, half, width), BF), sd((n, width), BF),
        sd((pairs, m, 128), BF), sd((pairs, n, 128), BF), sd((pairs, n, 128), BF),
        sd((m, width), F32), sd((pairs, m, 128), F32), sd((m, width), F32), sd((m, 128), F32), sd((m, width), BF),
        sd((4, m, width), BF), sd((4, m, width), F32), sd((m, width), F32), sd((m, 128), F32), sd((tok, width), F32),
        sd((8, width), F32), sd((8, width), F32), sd((mem, 1, width), F32),
    )
    V = pltpu.VMEM
    scratch = [
        V(stack, BF), V(stack, BF), V((shards, 4, 2, half, width), BF), V((n, width), BF), V((shards, 8, 2 * half), F32), V((shards, 8, width), F32),
        V((m, width), F32), V((pairs, m, 128), BF), V((pairs, n, 128), BF), V((pairs, n, 128), BF), V((m, n), F32),
        V((tok, n), BF), V((m, n), F32), V((tok, 128), F32), V((m, width), F32), V((m, width), BF), V((pairs, m, 128), F32),
        V((m, width), F32), V((m, width), F32), V((m, 128), F32), V((m, width), F32), V((m, width), BF),
        V((4, m, width), BF), V((4, m, width), F32), V((m, width), F32), V((m, width), F32), V((m, 128), F32),
        V((m, width), F32), V((8, width), F32), V((8, width), F32),
        V((shards, MEM_PAD, width), BF), V((shards, MEM_PAD, 128), F32),
    ]
    return pl.pallas_call(
        functools.partial(forward_kernel, shards, half, width, mem, docs.shape[1]),
        out_shape=outs,
        in_specs=[any_space] * 7 + [vm] * 10 + [pl.BlockSpec(memory_space=pltpu.SMEM)],
        out_specs=[any_space] * (len(outs) - 1) + [vm],
        scratch_shapes=scratch
        + [dma((3, 2, shards)), dma((3, shards)), dma((3, 3, 2, shards)), dma((3, 3, 2, shards)), dma((2, shards))] + [dma((shards,))] * 9 + [dma((10,)), dma((len(outs),)), dma((3, shards))],
        compiler_params=pltpu.CompilerParams(collective_id=3, has_side_effects=True, vmem_limit_bytes=VMEM_LIMIT),
        name="forward_layer",
    )(
        wq.reshape(2, half, width), wk.reshape(2, half, width), wv.reshape(2, half, width), wo.reshape(2, half, width),
        hid.reshape(2, half, 4 * width), outw.reshape(4, 2, half, width), tokens, memr, *vectors, docs,
    )


def backward_kernel(shards, half, width, mem, count,
                    h_qkvo, h_hid, h_out, h_x, h_q, h_k, h_v, h_ctx, h_lse, h_na, h_ia, h_al, h_act, h_slope, h_nf, h_if,
                    vfull, sq, out_grad, mem_grad, docs,
                    o_qkvo, o_hid, o_out, o_x, o_mem, o_own, o_bhid, o_rms,
                    grad, ra, rb, rc, rd, rx, relay, rm, rv, vz, vacc,
                    wbuf, x_all, pq, pk, pv, pctx, plse, bias, s_s, dp_s, p_s, ds_s, al, abuf, sbuf, d_pre, nf, if_,
                    gr, d_out, back, d_branch, dctx, dq, dkt, dvt,
                    asem, arem, bsem, brem, csem, crem, zsem, zrem, dsem, drem, xsem, xrem, msem, mrem, vsem, vrem,
                    vzs, vzr, fsem, wsem, psem, asem_, lsem, osem):
    r, s, core, xbit, ybit, fc, fx, fy = neighbours()
    q_own, q_lo = 2 * core + ybit, 2 * core
    tok = out_grad.shape[0]
    m, n = gr.shape[0], x_all.shape[0]
    seq = tok * shards
    pairs = width // 128
    outs = (o_qkvo, o_hid, o_out)
    groups = (2, 1, 0)
    units = 3 * shards

    def turn(i):
        return lax.rem((shards - 1) * i, shards)

    def load(src, dst, i):
        c = pltpu.make_async_copy(src, dst, lsem.at[i])
        c.start()
        return c

    def w_copy(j, src):
        return pltpu.make_async_copy(src, wbuf.at[j % 4], wsem.at[j])

    def a_copy(i):
        return (
            pltpu.make_async_copy(h_act.at[turn(i)], abuf.at[lax.rem(i, 2)], asem_.at[0, i]),
            pltpu.make_async_copy(h_slope.at[turn(i)], sbuf.at[lax.rem(i, 2)], asem_.at[1, i]),
        )

    def p_copy(p, slot):
        return [
            pltpu.make_async_copy(a.at[p], b.at[slot], psem.at[i, slot])
            for i, (a, b) in enumerate(((h_q, pq), (h_k, pk), (h_v, pv), (h_lse, plse)))
        ]

    first = [load(h_nf, nf, 0), load(out_grad, gr.at[pl.ds(0, tok), :], 1), load(h_if, if_, 2)]
    for j, src in enumerate((h_out.at[0], h_hid.at[0], h_out.at[turn(1)])):
        w_copy(j, src).start()
    for c in a_copy(jnp.int32(0)):
        c.start()
    second = [load(h_al, al, 3), load(h_x, x_all, 6), load(h_ctx, pctx, 7)]
    everyone_in = enter((fc, fx, fy), r, s, shards)

    def unit_shard(u):
        return turn(lax.rem(u, shards))

    def copy_a(u):
        return remote(grad.at[u, 1 - core], ra.at[u], asem.at[u], arem.at[u], (fc, s))

    side = width // 2
    left_cols, right_cols = pl.ds(0, side), pl.ds(side, side)

    def copy_b(u):
        return (
            remote(grad.at[u, core, :, 1 - xbit, :, left_cols], rb.at[u, 0], bsem.at[u, 0], brem.at[u, 0], (fx, s)),
            remote(grad.at[u, core, 1 - ybit, :, :, right_cols], rb.at[u, 1], bsem.at[u, 1], brem.at[u, 1], (fy, s)),
        )

    def copy_c(u):
        return (
            remote(grad.at[u, core, 1 - ybit, xbit, :, left_cols], rc.at[u, 0], csem.at[u, 0], crem.at[u, 0], (fy, s)),
            remote(grad.at[u, core, ybit, 1 - xbit, :, right_cols], rc.at[u, 1], csem.at[u, 1], crem.at[u, 1], (fx, s)),
        )

    def copy_z(u):
        return remote(
            grad.at[u, core, ybit, xbit], rd.at[u // shards, s], zsem.at[u], zrem.at[u // shards, s], (r, unit_shard(u))
        )

    def start_b(u):
        copy_a(u).wait_recv()
        grad[u, core] = grad[u, core] + ra[u]
        for c in copy_b(u):
            c.start()

    def start_c(u):
        for c in copy_b(u):
            c.wait_recv()
        grad[u, core, :, xbit, :, left_cols] = grad[u, core, :, xbit, :, left_cols] + rb[u, 0]
        grad[u, core, ybit, :, :, right_cols] = grad[u, core, ybit, :, :, right_cols] + rb[u, 1]
        for c in copy_c(u):
            c.start()

    def start_z(u):
        for c in copy_c(u):
            c.wait_recv()
        grad[u, core, ybit, xbit, :, left_cols] = grad[u, core, ybit, xbit, :, left_cols] + rc[u, 0]
        grad[u, core, ybit, xbit, :, right_cols] = grad[u, core, ybit, xbit, :, right_cols] + rc[u, 1]
        pl.when(s != unit_shard(u))(lambda: copy_z(u).start())

    def hop(k, j):
        o = outs[groups[k]]
        if j == 0:
            moves = ((o.at[q_own, xbit, :, left_cols], fx), (o.at[q_own, xbit, :, right_cols], fy))
        elif j == 1:
            moves = ((o.at[q_own, :, :, left_cols], fy), (o.at[pl.ds(q_lo, 2), xbit, :, right_cols], fx))
        else:
            moves = ((o.at[pl.ds(q_lo, 2)], fc),)
        return [remote(a, a, dsem.at[k, j, i], drem.at[k, j, i], (dev, s)) for i, (a, dev) in enumerate(moves)]

    def hop_start(k, j):
        for c in hop(k, j):
            c.start()

    def hop_wait(k, j):
        for c in hop(k, j):
            c.wait_recv()

    def finish_group(k):
        total = grad[k * shards + turn(s), core, ybit, xbit].astype(F32)
        for t in range(1, shards):
            other = lax.rem(s + t, shards)
            slot = rd.at[k, other]
            remote(slot, slot, zsem.at[0], zrem.at[k, other], (r, s)).wait_recv()
            total = total + rd[k, other].astype(F32)
        fin = ra.at[k * shards, 0, 0]
        fin[...] = total.astype(BF)
        c = pltpu.make_async_copy(fin, outs[groups[k]].at[q_own, xbit], fsem.at[k])
        c.start()
        c.wait()
        hop_start(k, 0)

    def hop_step(k, j):
        hop_wait(k, j - 1)
        hop_start(k, j)

    lag = 2
    steps = []
    for when, j, k in ((10, 0, 0), (11, 1, 0), (12, 2, 0), (14, 0, 1), (15, 1, 1), (16, 0, 2), (16, 2, 1), (17, 1, 2), (18, 2, 2)):
        steps.append((when, functools.partial(hop_step, k, j) if j else functools.partial(finish_group, k)))
    ticks = max(when for when, fn in steps) + 1

    def tick(i):
        def guarded(lo, fn):
            pl.when((i >= lo) & (i < lo + units))(lambda: fn(i - lo))

        guarded(0, start_b)
        guarded(lag, start_c)
        guarded(2 * lag, start_z)

    def late_tick(i):
        tick(jnp.int32(i))
        for when, fn in steps:
            if when == i:
                fn()

    def vrow(i):
        return vfull[pl.ds(i, 1), :]

    index = lax.broadcasted_iota(jnp.int32, (m, 1), 0)
    once = jnp.where((index < tok) | ((index < tok + mem) & (s == 0)), 1.0, 0.0)

    def add_sum(i, rw, value):
        total = jnp.sum(value * once[rw.start : rw.start + LOG_ROWS], axis=0, keepdims=True)
        vacc[0, pl.ds(i, 1), :] = vacc[0, pl.ds(i, 1), :] + total

    def mean(v):
        return jnp.mean(v, axis=1, keepdims=True)

    def norm_back_rows(e, normed, inverse):
        return inverse * (e - mean(e) - normed * mean(e * normed))

    vacc[0] = jnp.zeros(vacc.shape[1:], F32)
    for c in first:
        c.wait()
    gr[pl.ds(tok, mem), :] = mem_grad[:, 0, :]
    gr[pl.ds(tok + mem, MEM_PAD - mem), :] = jnp.zeros((MEM_PAD - mem, width), F32)
    for rw in row_blocks(m):
        g, normed = gr[rw, :], nf[rw, :]
        add_sum(6, rw, g * normed)
        add_sum(7, rw, g)
        v = norm_back_rows(g * vrow(6), normed, if_[rw, :1])
        back[rw, :] = v
        low = v.astype(BF)
        add_sum(3, rw, low.astype(F32))
        d_out[rw, :] = low
    na, ia = nf, if_
    second += [load(h_na, na, 4), load(h_ia, ia, 5)]
    second[0].wait()
    once_low = once.astype(BF)

    def turned(a, b):
        return dot(a, b, TN)

    def put(k, q, j, value):
        value = value.astype(BF).reshape(2, 2, half, width)
        for i in range(2):
            unit = k * shards + (shards - 1) * (2 * j + i) % shards
            grad[unit, q // 2, q % 2] = value[i]

    wide = 2 * 2 * half
    def feed_forward(i):
        q = turn(i)
        even = 2 * lax.rem(i, 2)
        for c in a_copy(i):
            c.wait()

        @pl.when(i + 1 < 4)
        def _():
            for c in a_copy(i + 1):
                c.start()

        w_copy(2 * i, h_out.at[q]).wait()
        pl.when(i < 3)(lambda: w_copy(2 * i + 3, h_hid.at[turn(i + 1)]).start())
        pl.when(i == 3)(lambda: w_copy(9, h_qkvo.at[1]).start())
        slot = lax.rem(i, 2)
        do = d_out[...] * once_low
        for j in range(2):
            value = turned(abuf[slot, :, j * wide : (j + 1) * wide], do)
            grad[i, j] = value.astype(BF).reshape(2, 2, half, width)
        pl.when(i == 0)(everyone_in)
        copy_a(i).start()
        for j in range(2):
            wt = wbuf[even, 2 * j : 2 * j + 2].reshape(wide, width)
            s_s[:, j * wide : (j + 1) * wide] = dot(d_out[...], wt, NT)
        for rw in row_blocks(m):
            v = s_s[rw, :width] * sbuf[slot, rw, :]
            low = v.astype(BF)
            d_pre[rw, :] = low
            add_sum(8 + q, rw, low.astype(F32))
        w_copy(2 * i + 1, h_hid.at[q]).wait()
        pl.when(i < 2)(lambda: w_copy(2 * i + 4, h_out.at[turn(i + 2)]).start())
        pl.when(i == 2)(lambda: w_copy(8, h_qkvo.at[3]).start())
        pl.when(i == 3)(lambda: w_copy(10, h_qkvo.at[2]).start())
        dp = d_pre[...] * once_low
        for j in range(2):
            value = turned(al[:, j * wide : (j + 1) * wide], dp).astype(BF).reshape(2, 2, half, width)
            for k in range(2):
                unit = shards + (shards - 1) * (2 * j + k) % shards
                grad[unit, q // 2, lax.rem(q, 2)] = value[k]
        for j in range(2):
            wt = wbuf[even + 1, 2 * j : 2 * j + 2].reshape(wide, width)
            s_s[:, j * wide : (j + 1) * wide] = dot(d_pre[...], wt, NT)
        for rw in row_blocks(m):
            back[rw, :] = back[rw, :] + s_s[rw, :width]
        tick(i)

    pl.loop(0, 4)(feed_forward)
    for j in range(shards):
        copy_a(shards + j).start()
    for c in p_copy(0, 0):
        c.start()

    for c in second[1:]:
        c.wait()

    for rw in row_blocks(m):
        f, normed = back[rw, :], na[rw, :]
        add_sum(4, rw, f * normed)
        add_sum(5, rw, f)
        v = norm_back_rows(f * vrow(4), normed, ia[rw, :1])
        back[rw, :] = v
        low = v.astype(BF)
        d_branch[rw, :] = low
        add_sum(2, rw, low.astype(F32))
        d_out[rw, :] = pctx[rw, :].astype(BF)
    write_bias(bias, docs, docs.shape[1], s, tok, seq, mem)
    w_copy(8, h_qkvo.at[3]).wait()
    w_copy(11, h_qkvo.at[0]).start()
    db = d_branch[...] * once_low
    for j in range(2):
        put(2, 3, j, turned(d_out[:, j * wide : (j + 1) * wide], db))
    for j in range(2):
        wt = wbuf[0, 2 * j : 2 * j + 2].reshape(wide, width)
        value = dot(d_branch[...], wt, NT).astype(BF)
        for i in range(wide // 128):
            dctx[j * (wide // 128) + i] = value[:, i * 128 : (i + 1) * 128]
    lane = lax.broadcasted_iota(jnp.int32, (m, 128), 1)
    lane_k = lax.broadcasted_iota(jnp.int32, (n, 128), 1)
    tick(jnp.int32(4))

    def pair(p):
        slot = lax.rem(p, 2)
        for c in p_copy(p, slot):
            c.wait()

        @pl.when(p + 1 < pairs)
        def _():
            for c in p_copy(p + 1, 1 - slot):
                c.start()

        c = pl.ds(pl.multiple_of(p * 128, 128), 128)
        part_q, part_k, part_v = None, None, None
        zero = jnp.zeros((m, 128), BF)
        for head in range(2):
            mine = (lane < HD) == (head == 0)
            qh = jnp.where(mine, pq[slot], zero)
            doh = jnp.where(mine, dctx[p], zero)
            s_s[...] = dot(qh, pk[slot], NT)
            dp_s[...] = dot(doh, pv[slot], NT)
            for rw in row_blocks(m):
                sub = slice(rw.start, rw.start + LOG_ROWS)
                delta = jnp.sum(doh[sub].astype(F32) * pctx[rw, c], axis=1, keepdims=True)
                top = plse[slot, rw, head * HD : head * HD + 1]
                probs = jnp.exp(s_s[rw, :] + bias[rw, :] - top)
                p_s[rw, :] = probs.astype(BF)
                ds_s[rw, :] = (probs * (dp_s[rw, :] - delta)).astype(BF)
            kh = jnp.where((lane_k < HD) == (head == 0), pk[slot], jnp.zeros((n, 128), BF))
            a = dot(ds_s[...], kh)
            b = turned(qh, ds_s[...])
            d = turned(doh, p_s[...])
            part_q = a if head == 0 else part_q + a
            part_k = b if head == 0 else part_k + b
            part_v = d if head == 0 else part_v + d
        dq[:, c] = (part_q * 0.125).astype(BF)
        dkt[c, :] = part_k.astype(BF)
        dvt[c, :] = part_v.astype(BF)
        pl.when(lax.rem(p, 2) == 1)(lambda: tick(5 + p // 2))

    pl.loop(0, pairs)(pair)

    ones = jnp.ones((8, n), BF)
    vacc[0, pl.ds(1, 1), :] = dot(ones, dvt[...], NT)[:1]
    vacc[0, pl.ds(0, 1), :] = jnp.sum(dq[...].astype(F32), axis=0, keepdims=True)
    vacc[0, pl.ds(12, 3), :] = sq[pl.ds(0, 3), :]
    rv_first = remote(vacc.at[0], rv.at[0], vsem.at[0], vrem.at[0], (fc, s))
    rv_first.start()
    def vec_hop(k):
        return remote(vacc.at[k], rv.at[k], vsem.at[k], vrem.at[k], ((fc, fx, fy)[k], s))

    def vec_step(k):
        vec_hop(k - 1).wait_recv()
        vacc[k] = vacc[k - 1] + rv[k - 1]
        vec_hop(k).start()

    w_copy(9, h_qkvo.at[1]).wait()
    w_copy(10, h_qkvo.at[2]).wait()
    wkm = wbuf[1].reshape(width, width)
    wvm = wbuf[2].reshape(width, width)
    spare = (abuf.at[0, pl.ds(0, tok)], abuf.at[1, pl.ds(0, tok)], d_pre.at[pl.ds(0, tok)])
    small = []

    def to_shard(src, dst, ssem, rsem, t):
        return remote(src, dst.at[s], ssem.at[t], rsem.at[s], (r, lax.rem(s + t, shards)))

    def row_grads(blk):
        c = pl.ds(pl.multiple_of(blk * tok, tok), tok)
        return jnp.transpose(dot(wkm, dkt[:, c]) + dot(wvm, dvt[:, c]))

    def along(src, dst, i, up):
        return remote(src, dst, xsem.at[i], xrem.at[i], (r, s + 1 if up else s - 1))

    far = (along(spare[0], relay.at[0], 0, True), along(spare[0], relay.at[1], 1, False))
    near = (along(spare[1], rx.at[0], 2, True), along(spare[2], rx.at[1], 3, False))
    has_far = (s < 2, s >= 2)
    has_near = (s < shards - 1, s > 0)
    has_relay = (s > 0, s < shards - 1)
    spare[0][...] = row_grads(lax.rem(s + 2, shards)).astype(BF)
    for i in range(2):
        pl.when(has_far[i])(far[i].start)
    for j in range(2):
        xs_ = x_all[:, j * wide : (j + 1) * wide]
        x_own = jnp.concatenate([
            x_all[pl.ds(pl.multiple_of(s * tok, tok), tok), j * wide : (j + 1) * wide],
            x_all[pl.ds(seq, MEM_PAD), j * wide : (j + 1) * wide],
        ])
        put(2, 0, j, turned(x_own, dq[...]))
        xt = jnp.transpose(xs_)
        put(2, 1, j, dot(xt, dkt[...], NT))
        put(2, 2, j, dot(xt, dvt[...], NT))
    for j in range(shards):
        copy_a(2 * shards + j).start()
    tick(jnp.int32(8))

    vec_step(1)
    tick(jnp.int32(9))
    for i in range(2):
        @pl.when(has_near[i])
        def _():
            spare[1 + i][...] = row_grads(s + 1 - 2 * i).astype(BF)

            @pl.when(has_relay[i])
            def _():
                along(spare[0], relay.at[i], i, i == 0).wait_recv()
                spare[1 + i][...] = (spare[1 + i][...].astype(F32) + relay[i].astype(F32)).astype(BF)

            near[i].start()

        late_tick(10 + i)
    own_rows = pl.ds(0, tok)
    back[own_rows, :] = back[own_rows, :] + row_grads(s)
    value = dot(wkm, dkt[:, pl.ds(seq, MEM_KEYS)]) + dot(wvm, dvt[:, pl.ds(seq, MEM_KEYS)])
    w_copy(11, h_qkvo.at[0]).wait()
    mrows = pl.ds(tok, MEM_PAD)
    value = jnp.transpose(value)[:MEM_PAD] + dot(dq[mrows, :], wbuf[3].reshape(width, width), NT)
    rm[s] = value.astype(BF)
    for t in range(1, shards):
        small.append(remote(rm.at[s], rm.at[s], msem.at[t], mrem.at[s], (r, lax.rem(s + t, shards))))
        small[-1].start()
    vec_step(2)
    for j in range(2):
        wt = wbuf[3, 2 * j : 2 * j + 2].reshape(wide, width)
        c = pl.ds(j * wide, wide)
        back[own_rows, c] = back[own_rows, c] + dot(dq[own_rows, :], wt, NT)
    late_tick(12)
    vec_hop(2).wait_recv()
    vz[s] = vacc[2] + rv[2]
    for t in range(1, shards):
        small.append(to_shard(vz.at[s], vz, vzs, vzr, t))
        small[-1].start()
    for i in range(13, ticks):
        late_tick(i)

    for t in range(1, shards):
        other = lax.rem(s + t, shards)
        for buf, rsem in ((rm, mrem), (vz, vzr)):
            remote(buf.at[other], buf.at[other], msem.at[0], rsem.at[other], (r, s)).wait_recv()
    for i in range(2):
        @pl.when(has_relay[i])
        def _():
            along(spare[0], rx.at[i], 2 + i, i == 0).wait_recv()
            back[own_rows, :] = back[own_rows, :] + rx[i].astype(F32)

    sx, sm, sv = back[own_rows, :], back[mrows, :], vz[0]
    for t in range(shards):
        sm = sm + rm[t].astype(F32)
        if t:
            sv = sv + vz[t]
    gr[pl.ds(0, tok), :] = sx
    o_mem[:, 0, :] = sm[:mem]
    final = [
        pltpu.make_async_copy(gr.at[pl.ds(0, tok), :], o_x, osem.at[0]),
    ]
    for c in final:
        c.start()
    srows = 2 * half
    for i in range(shards):
        @pl.when(s == i)
        def _():
            o_own[...] = sv[:8, i * srows : (i + 1) * srows]
            o_bhid[...] = sv[8 + i : 9 + i]

    squares = jnp.sum(sv[8:16], axis=1, keepdims=True) / count
    o_rms[...] = jnp.broadcast_to(jnp.sqrt(squares), o_rms.shape)
    for k in range(3):
        hop_wait(k, 2)
    for c in final:
        c.wait()

    @pl.loop(0, units)
    def _(u):
        copy_a(u).wait_send()
        for c in copy_b(u) + copy_c(u):
            c.wait_send()
        pl.when(s != unit_shard(u))(lambda: copy_z(u).wait_send())

    for k in range(3):
        for j in range(3):
            for c in hop(k, j):
                c.wait_send()
    for c in small:
        c.wait_send()
    for i in range(2):
        pl.when(has_far[i])(far[i].wait_send)
        pl.when(has_near[i])(near[i].wait_send)
    for k in range(3):
        vec_hop(k).wait_send()


def backward_all(saved, out_grad, mem_grad, docs):
    shards = lax.axis_size("shard")
    tok, width = out_grad.shape
    mem = mem_grad.shape[0]
    half = saved[0].shape[3]
    m, n = tok + MEM_PAD, tok * shards + MEM_KEYS
    pairs = width // 128
    any_space = pl.BlockSpec(memory_space=pl.ANY)
    vm = pl.BlockSpec(memory_space=pltpu.VMEM)
    dma = pltpu.SemaphoreType.DMA
    V = pltpu.VMEM
    units = 3 * shards
    piece4 = (4, 2, half, width)
    outs = tuple(jax.ShapeDtypeStruct(piece4, BF) for _ in range(3)) + (
        jax.ShapeDtypeStruct((tok, width), F32),
        jax.ShapeDtypeStruct((mem, 1, width), F32),
        jax.ShapeDtypeStruct((8, 2 * half), F32),
        jax.ShapeDtypeStruct((1, width), F32),
        jax.ShapeDtypeStruct((8, 128), F32),
    )
    big = (4, 2, half, width)
    scratch = [
        V((units, 2, 2, 2, half, width), BF), V((units, 2, 2, half, width), BF), V((units, 2, 2, half, width // 2), BF),
        V((units, 2, half, width // 2), BF), V((3, shards, half, width), BF), V((2, tok, width), BF), V((2, tok, width), BF),
        V((shards, MEM_PAD, width), BF), V((3, 16, width), F32), V((shards, 16, width), F32), V((3, 16, width), F32),
        V((4,) + big, BF), V((n, width), BF), V((2, m, 128), BF), V((2, n, 128), BF), V((2, n, 128), BF),
        V((m, width), F32), V((2, m, 128), F32), V((m, n), F32), V((m, n), F32), V((m, n), F32), V((m, n), BF),
        V((m, n), BF), V((m, width), BF), V((2, m, width), BF),
        V((2, m, width), F32), V((m, width), BF), V((m, width), F32), V((m, 128), F32), V((m, width), F32),
        V((m, width), BF), V((m, width), F32), V((m, width), BF), V((pairs, m, 128), BF), V((m, width), BF),
        V((width, n), BF), V((width, n), BF),
    ]
    sems = (
        [dma((units,))] * 2 + [dma((units, 2))] * 4 + [dma((units,)), dma((3, shards))]
        + [dma((3, 3, 2)), dma((3, 3, 2)), dma((shards,)), dma((shards,)), dma((shards,)), dma((shards,))]
        + [dma((3,)), dma((3,)), dma((shards,)), dma((shards,)), dma((3,)), dma((12,)), dma((4, 2)), dma((2, 4))]
        + [dma((8,)), dma((1,))]
    )
    return pl.pallas_call(
        functools.partial(backward_kernel, shards, half, width, mem, float(tok * shards * width * lax.axis_size("replica"))),
        out_shape=outs,
        in_specs=[any_space] * 16 + [vm, vm, any_space, vm, pl.BlockSpec(memory_space=pltpu.SMEM)],
        out_specs=[any_space] * 4 + [vm] * 4,
        scratch_shapes=scratch + sems,
        compiler_params=pltpu.CompilerParams(collective_id=4, has_side_effects=True, vmem_limit_bytes=VMEM_LIMIT),
        name="backward_layer",
    )(*saved, out_grad, mem_grad, docs)


def plain_body(tokens, memory_rows, doc_lengths, w_query, w_key, w_value, w_attn_out, w_hidden, w_output,
         b_query, b_value, b_attn_out, b_hidden, b_output, gain_attn, shift_attn, gain_ffn, shift_ffn,
         out_grad, memory_grad):
    tok, width = tokens.shape
    mem = memory_rows.shape[1]
    shards = lax.axis_size("shard")
    s = lax.axis_index("shard")
    seq = tok * shards
    srows = w_query.shape[0]
    m = tok + MEM_PAD
    n = seq + MEM_KEYS
    scaling = 1.0 / math.sqrt(HD)

    vec = jnp.concatenate(
        [v.reshape(-1, srows) for v in (
            b_query, b_value, b_attn_out, b_output, gain_attn, shift_attn, gain_ffn, shift_ffn, b_hidden
        )]
        + [jnp.zeros((4, srows), BF)]
    )
    vec = lax.dynamic_update_slice(jnp.zeros((16, width), BF), vec, (0, s * srows))
    rows = jnp.concatenate([tokens, memory_rows[0], jnp.zeros((MEM_PAD - mem, width), F32)])
    low_rows = rows.astype(BF)
    qkvo = jnp.stack([w_query, w_key, w_value, w_attn_out])
    qkvo, w_hid, w_out, x_tok, vec_all = gather_plain(qkvo, w_hidden, w_output, low_rows[:tok], vec)
    vec = jnp.sum(vec_all.astype(F32), axis=0)
    bq, bv, bo, bout, ga, sa, gf, sf = (vec[i] for i in range(8))
    bh = jnp.transpose(vec[8:12].reshape(4, shards, srows), (1, 0, 2)).reshape(4 * width)

    doc_ends = jnp.cumsum(doc_lengths[0])
    seg = jnp.sum((jnp.arange(seq, dtype=jnp.int32)[:, None] >= doc_ends[None, :]).astype(jnp.int32), axis=1)
    place = jnp.arange(MEM_KEYS, dtype=jnp.int32)
    mem_seg = jnp.where(place < mem // 2, -1, jnp.where(place < mem, -3, -4)).astype(jnp.int32)
    kseg = jnp.concatenate([seg, mem_seg])[None, :]
    qseg = jnp.concatenate(
        [lax.dynamic_slice_in_dim(seg, s * tok, tok), jnp.full((MEM_PAD,), -2, jnp.int32)]
    )[:, None]
    index = jnp.arange(m, dtype=jnp.int32)[:, None]
    once = jnp.where(index < tok, 1.0, jnp.where((index < tok + mem) & (s == 0), 1.0, 0.0)).astype(F32)
    once_low = once.astype(BF)

    x_all = jnp.concatenate([x_tok, low_rows[tok:], jnp.zeros((MEM_KEYS - MEM_PAD, width), BF)])
    query = (jnp.dot(low_rows, qkvo[0], preferred_element_type=F32) + bq).astype(BF)
    keys = jnp.dot(x_all, qkvo[1], preferred_element_type=F32).astype(BF)
    values = (jnp.dot(x_all, qkvo[2], preferred_element_type=F32) + bv).astype(BF)
    context, lse = attention(query, keys, values, qseg, kseg, scaling)
    context_low = context.astype(BF)
    branch = jnp.dot(context_low, qkvo[3], preferred_element_type=F32) + bo
    normed_attn, inverse_attn = layer_stats(rows + branch)
    after_attn = normed_attn * ga + sa
    after_low = after_attn.astype(BF)
    pre_act = jnp.concatenate([jnp.dot(after_low, w_hid[q], preferred_element_type=F32) for q in range(4)], axis=1) + bh
    half_erf = 0.5 * (1.0 + lax.erf(pre_act * GELU_ROOT))
    act_low = (pre_act * half_erf).astype(BF)
    second = jnp.dot(act_low, w_out, preferred_element_type=F32) + bout
    normed_ffn, inverse_ffn = layer_stats(after_attn + second)
    result = normed_ffn * gf + sf

    grads = jnp.concatenate([out_grad, memory_grad[0], jnp.zeros((MEM_PAD - mem, width), F32)])
    back_ffn = norm_back(grads * gf, normed_ffn, inverse_ffn)
    d_output = back_ffn.astype(BF)
    g_out = jnp.einsum("rf,rd->fd", act_low * once_low, d_output, preferred_element_type=F32).astype(BF)
    d_act = jnp.einsum("rd,fd->rf", d_output, w_out, preferred_element_type=F32)
    d_pre = (d_act * (half_erf + pre_act * jnp.exp(-0.5 * pre_act * pre_act) * GELU_DENSITY)).astype(BF)
    after_once = after_low * once_low
    g_hid = jnp.stack(
        [jnp.einsum("rd,rf->df", after_once, d_pre[:, q * width : (q + 1) * width], preferred_element_type=F32).astype(BF)
         for q in range(4)]
    )
    back_first = back_ffn + sum(
        jnp.einsum("rf,df->rd", d_pre[:, q * width : (q + 1) * width], w_hid[q], preferred_element_type=F32)
        for q in range(4)
    )
    back_attn = norm_back(back_first * ga, normed_attn, inverse_attn)
    d_branch = back_attn.astype(BF)
    d_context = jnp.einsum("re,de->rd", d_branch, qkvo[3], preferred_element_type=F32).astype(BF)
    dq, dkt, dvt = attention_back(query, keys, values, qseg, kseg, once, context, lse, d_context, scaling)
    g_qkvo = jnp.stack([
        jnp.einsum("rd,re->de", low_rows * once_low, dq, preferred_element_type=F32).astype(BF),
        jnp.einsum("rd,er->de", x_all, dkt, preferred_element_type=F32).astype(BF),
        jnp.einsum("rd,er->de", x_all, dvt, preferred_element_type=F32).astype(BF),
        jnp.einsum("rd,re->de", context_low * once_low, d_branch, preferred_element_type=F32).astype(BF),
    ])
    dx = jnp.einsum("er,de->rd", dkt, qkvo[1], preferred_element_type=F32) + jnp.einsum(
        "er,de->rd", dvt, qkvo[2], preferred_element_type=F32
    )
    base = back_attn + jnp.einsum("re,de->rd", dq, qkvo[0], preferred_element_type=F32)

    def over_rows(terms):
        return jnp.sum(once * terms, axis=0)

    gb_hidden = over_rows(d_pre.astype(F32)).reshape(shards, 4, srows).transpose(1, 0, 2).reshape(4, width)
    squares = jnp.stack([jnp.sum(v[:tok] * v[:tok]) for v in (result, branch, second)])
    vec_grads = jnp.concatenate([
        jnp.stack([
            over_rows(dq.astype(F32)),
            jnp.sum(dvt.astype(F32), axis=1),
            over_rows(d_branch.astype(F32)),
            over_rows(d_output.astype(F32)),
            over_rows(back_first * normed_attn),
            over_rows(back_first),
            over_rows(grads * normed_ffn),
            over_rows(grads),
        ]),
        gb_hidden,
        jnp.pad(squares[None], ((0, 3), (0, width - 3))),
    ])
    g_qkvo, g_hid, g_out, dx_own, dx_mem, vec_sum = reduce_plain(
        g_qkvo, g_hid, g_out, dx[:seq].astype(BF), dx[seq : seq + MEM_PAD], vec_grads
    )
    own = lax.dynamic_slice(vec_sum, (0, s * srows), (12, srows))
    rms = jnp.sqrt(vec_sum[12, :3] / float(seq * width * lax.axis_size("replica")))
    g_qkvo = g_qkvo.astype(F32)
    grad_hidden = jnp.concatenate([g_hid[q] for q in range(4)], axis=1).astype(F32)
    return (
        result[:tok],
        result[tok : tok + mem][None],
        base[:tok] + dx_own,
        (base[tok : tok + mem] + dx_mem[:mem])[None],
        g_qkvo[0],
        g_qkvo[1],
        g_qkvo[2],
        g_qkvo[3],
        grad_hidden,
        g_out.astype(F32),
        own[0],
        own[1],
        own[2],
        own[8:12].reshape(-1),
        own[3],
        own[4],
        own[5],
        own[6],
        own[7],
        rms[0],
        rms[1],
        rms[2],
    )


def direct_body(tokens, memory_rows, doc_lengths, w_query, w_key, w_value, w_attn_out, w_hidden, w_output,
                b_query, b_value, b_attn_out, b_hidden, b_output, gain_attn, shift_attn, gain_ffn, shift_ffn,
                out_grad, memory_grad):
    width = tokens.shape[1]
    srows = w_query.shape[0]
    vectors = (b_query, b_value, b_attn_out, b_output, gain_attn, shift_attn, gain_ffn, shift_ffn, b_hidden)
    *saved, result, vec_full, squares, result_mem = forward_all(
        w_query, w_key, w_value, w_attn_out, w_hidden, w_output, tokens, jnp.transpose(memory_rows, (1, 0, 2)), vectors, doc_lengths
    )
    g_qkvo, g_hid, g_out, grad_rows, grad_mem, own, own_hid, rms = backward_all(
        tuple(saved) + (vec_full, squares), out_grad, jnp.transpose(memory_grad, (1, 0, 2)), doc_lengths
    )
    g_qkvo = g_qkvo.reshape(4, srows, width).astype(F32)
    g_hid = g_hid.reshape(4, srows, width)
    return (
        result,
        jnp.transpose(result_mem, (1, 0, 2)),
        grad_rows,
        jnp.transpose(grad_mem, (1, 0, 2)),
        g_qkvo[0],
        g_qkvo[1],
        g_qkvo[2],
        g_qkvo[3],
        jnp.concatenate([g_hid[q] for q in range(4)], axis=1).astype(F32),
        g_out.reshape(4 * srows, width).astype(F32),
        own[0],
        own[1],
        own[2],
        own_hid[0],
        own[3],
        own[4],
        own[5],
        own[6],
        own[7],
        rms[4, 0],
        rms[5, 0],
        rms[6, 0],
    )


def solution(mesh):
    direct = mesh.shape["replica"] == 8 and mesh.shape["shard"] == 4
    shard1, shard2 = P("shard"), P("shard", None)
    both, rep3 = P(("replica", "shard"), None), P("replica", None, None)
    return jax.shard_map(
        direct_body if direct else plain_body,
        mesh=mesh,
        in_specs=(both, rep3, P("replica", None)) + (shard2,) * 6 + (shard1,) * 9 + (both, rep3),
        out_specs=(both, rep3, both, rep3) + (shard2,) * 6 + (shard1,) * 9 + (P(), P(), P()),
        check_vma=False,
    )
```
